1024 devices in a mesh: vel: 16 (over y_lo, x), space: 64 (over y_hi, z, core).
Axes of the slice: x: 8, y: 8 (y_hi: 4, y_lo: 2; y = y_hi * 2 + y_lo), z: 8, core: 2. Of those that a mesh axis runs over, the one named last changes fastest.
Arguments:
- distribution: float32 [2304, 256, 256], P('vel', 'space'), may hold values from -3 to 3
- moments_old: float32 [10, 256, 256], P(None, 'space'), may hold values from -6 to 6
- pore_mask: int32 [256, 256], P('space'), may hold values 0 or 1
- synthetic_rate: float32 [10], replicated, may hold values from 0.2 to 4
Outputs:
- distribution_new: float32 [2304, 256, 256], P('vel', 'space')
- moments_new: float32 [10, 256, 256], P(None, 'space')
The draws below stay inside these ranges and needn't reach their ends.
Inputs may be any that keep to these rules, and one draw needn't show every extreme that they name: `pore_mask`: 1 marks a pore cell, 0 a solid one.
All inputs are finite; a program needn't handle non-finite values. No bound on the sum of `pore_mask` on one device may be relied on, other than what follows from the above.
Results may differ from the reference program's by a relative error of at most 0.000092.
Values sent between devices are 32-bit elements; how exact they have to be, the bound alone decides.
No kernel may reach another device: no remote copies, remote signals or barrier semaphores. Data moves between devices by JAX's collectives and lax.ppermute only.
A program may use at most 32 MiB of HBM per device.

```python
import math
import jax
import jax.numpy as jnp
from jax import lax

VX = 16
VY = 12
VZ = 12
NMOM = 10
NY = 16
NZ = 16
TSWEEPS = 2
SWEEPS = 5
VELS = 2304
NX = 256
PLANE = 256


def touch_ends(drawn, rng, low, top_value):
    dims = drawn.shape
    spot = [jax.random.randint(jax.random.fold_in(rng, axis), (), 0, dims[axis]) for axis in range(len(dims))]
    drawn = drawn.at[tuple(spot)].set(low)
    longest = dims.index(max(dims))
    spot[longest] = (spot[longest] + 1) % dims[longest]
    return drawn.at[tuple(spot)].set(top_value)


def level_of(key, shape, split, least, top_value):
    factor_of = 1.0
    for dim, parts in split:
        steps = jax.random.uniform(jax.random.fold_in(jax.random.fold_in(key, 6), dim), (parts,), jnp.float32, least / len(split), top_value / len(split))
        factor_of = factor_of * jnp.repeat(jnp.exp(steps), shape[dim] // parts).reshape((-1,) + (1,) * (len(shape) - 1 - dim))
    return factor_of


def bell_draw(stream_key, dims, deviation, most, pieces=(), held_as=jnp.bfloat16):
    entries = jax.random.normal(stream_key, dims, jnp.float32) * deviation
    if len(pieces) > 0:
        entries = level_of(stream_key, dims, pieces, -0.22, 0.18) * entries
    return jnp.clip(entries, min=-most, max=most).astype(held_as)


def setup_inputs(seed: int = 0) -> dict:
    seeds = jax.random.split(jax.random.key(seed), 5)
    return {
        "distribution": bell_draw(seeds[0], (VELS, NX, PLANE), 0.5, 3.0, ((0, 16), (1, 64)), jnp.float32),
        "moments_old": bell_draw(seeds[1], (NMOM, NX, PLANE), 1.0, 6.0, ((1, 64),), jnp.float32),
        "pore_mask": touch_ends((jax.random.randint(seeds[2], (NX, PLANE), 0, 4) < 3).astype(jnp.int32), jax.random.fold_in(seeds[2], 1), 0, 1),
        "synthetic_rate": jnp.clip(jnp.exp(jax.random.uniform(seeds[3], (NMOM,), jnp.float32, math.log(0.2), math.log(4.0))), 0.2, 4.0),
    }


extent = 3.0
collide = 1.0
coefficients = (1.0, 2.0, 2.0, 2.0, 0.6667, 0.8, 0.8, 0.8, 2.0, 2.0)


def node_values(indices, count):
    return -extent + (indices.astype(jnp.float32) + 0.5) * (2.0 * extent / count)


def velocity_tables(first_group, groups, along_x, along_y, along_z):
    first_nodes = node_values(first_group + jnp.arange(groups, dtype=jnp.int32), along_x)
    second_nodes = node_values(jnp.arange(along_y, dtype=jnp.int32), along_y)
    third_nodes = node_values(jnp.arange(along_z, dtype=jnp.int32), along_z)
    block_shape = (groups, along_y, along_z)
    speed_one = jnp.broadcast_to(first_nodes[:, None, None], block_shape).reshape(-1)
    speed_two = jnp.broadcast_to(second_nodes[None, :, None], block_shape).reshape(-1)
    speed_three = jnp.broadcast_to(third_nodes[None, None, :], block_shape).reshape(-1)
    energy = speed_one * speed_one + speed_two * speed_two + speed_three * speed_three
    functions = jnp.stack([jnp.ones_like(energy), speed_one, speed_two, speed_three, energy - 1.5,
                           speed_one * (energy - 2.5), speed_two * (energy - 2.5),
                           speed_three * (energy - 2.5), speed_one * speed_two, speed_two * speed_three])
    volume = (2.0 * extent) ** 3 / (along_x * along_y * along_z) / math.pi ** 1.5
    moment_rows = functions * volume
    factors = jnp.array(coefficients, dtype=jnp.float32)
    spread_rows = jnp.transpose(functions * factors[:, None] * jnp.exp(-energy)[None, :])
    return (speed_one, speed_two, speed_three), moment_rows, spread_rows


def upwind_sweep(padded, source, porous, speeds, along_y, along_z):
    speed_one, speed_two, speed_three = speeds
    middle = padded[:, 1:-1]
    groups, thickness, plane_cells = middle.shape
    cube_view = middle.reshape(groups, thickness, along_y, along_z)
    from_first = jnp.where(speed_one[:, None, None] > 0, padded[:, :-2], padded[:, 2:])
    from_second = jnp.where(speed_two[:, None, None, None] > 0, jnp.roll(cube_view, 1, 2), jnp.roll(cube_view, -1, 2))
    from_third = jnp.where(speed_three[:, None, None, None] > 0, jnp.roll(cube_view, 1, 3), jnp.roll(cube_view, -1, 3))
    across = jnp.abs(speed_two)[:, None, None, None] * from_second + jnp.abs(speed_three)[:, None, None, None] * from_third
    inflow = jnp.abs(speed_one)[:, None, None] * from_first + across.reshape(groups, thickness, plane_cells)
    denominator = collide + jnp.abs(speed_one) + jnp.abs(speed_two) + jnp.abs(speed_three)
    return porous[None] * (collide * source + inflow) / denominator[:, None, None]


def relax_step(padded, forcing, porous, rates, along_y, along_z):
    middle = padded[:, 1:-1]
    moment_count, thickness, plane_cells = middle.shape
    cube_view = middle.reshape(moment_count, thickness, along_y, along_z)
    beside = jnp.roll(cube_view, 1, 2) + jnp.roll(cube_view, -1, 2) + jnp.roll(cube_view, 1, 3) + jnp.roll(cube_view, -1, 3)
    neighbours = padded[:, :-2] + padded[:, 2:] + beside.reshape(moment_count, thickness, plane_cells)
    return porous[None] * (forcing + neighbours) / (rates + 6.0)[:, None, None]


def periodic_pad(field):
    return jnp.concatenate([field[:, -1:], field, field[:, :1]], axis=1)


def reference(distribution, moments_old, pore_mask, synthetic_rate):
    porous = pore_mask.astype(jnp.float32)
    speeds, moment_rows, spread_rows = velocity_tables(0, VX, VX, VY, VZ)
    velocities, planes, plane_cells = distribution.shape
    source = jnp.dot(spread_rows, moments_old.reshape(NMOM, -1), precision=lax.Precision.HIGHEST,
                     preferred_element_type=jnp.float32).reshape(distribution.shape)
    current = distribution
    for sweep_number in range(TSWEEPS):
        current = upwind_sweep(periodic_pad(current), source, porous, speeds, NY, NZ)
    moments_half = jnp.dot(moment_rows, current.reshape(velocities, -1), precision=lax.Precision.HIGHEST,
                           preferred_element_type=jnp.float32).reshape(NMOM, planes, plane_cells)
    change = moments_half - moments_old
    correction = porous[None] * change / (synthetic_rate + 6.0)[:, None, None]
    for sweep_number in range(SWEEPS - 1):
        correction = relax_step(periodic_pad(correction), change, porous, synthetic_rate, NY, NZ)
    moments_new = moments_half + correction
    lifted = jnp.dot(spread_rows, correction.reshape(NMOM, -1), precision=lax.Precision.HIGHEST,
                     preferred_element_type=jnp.float32).reshape(distribution.shape)
    distribution_new = current + porous[None] * lifted
    return distribution_new, moments_new
```

```python
import math

import jax
import jax.numpy as jnp
from jax import lax
from jax.experimental import pallas as pl
from jax.experimental.pallas import tpu as pltpu
from jax.sharding import PartitionSpec as P

F = jnp.float32
SHAPE = (8, 128)
VOL = 216.0 / 2304 / math.pi**1.5
K1, K4, K5 = 2.0, 0.6667, 0.8


def magnitude(kk):
    return 2.75 - 0.5 * kk


def iotas():
    return lax.broadcasted_iota(jnp.int32, SHAPE, 0), lax.broadcasted_iota(jnp.int32, SHAPE, 1)


def first_speed(i_ref):
    return jnp.full(SHAPE, -3.0 + (i_ref[0].astype(F) + 0.5) * 0.375, F)


def field_polynomial(a, m):
    a2 = a * a
    u, w = a2 - 1.5, a2 - 2.5
    return (
        m[0] + K1 * (a * m[1]) + K4 * (u * m[4]) + K5 * (a * w * m[5]),
        K1 * m[2] + K5 * (w * m[6]) + K1 * (a * m[8]),
        K1 * m[3] + K5 * (w * m[7]),
        K4 * m[4] + K5 * (a * m[5]),
        K5 * m[6],
        K5 * m[7],
        K1 * m[9],
    )


def at_second(al, b):
    b2 = b * b
    return (
        al[0] + b * al[1] + b2 * al[3] + (b2 * b) * al[4],
        al[2] + b2 * al[5] + b * al[6],
        al[3] + b * al[4],
        al[5],
    )


def from_z(h, lane, positive):
    inside = lane & 15
    if positive:
        return jnp.where(inside == 0, pltpu.roll(h, 113, 1), pltpu.roll(h, 1, 1))
    return jnp.where(inside == 15, pltpu.roll(h, 15, 1), pltpu.roll(h, 127, 1))


def from_y(h, lane, positive, swap):
    r = pltpu.roll(h, 16 if positive else 112, 1)
    return jnp.where(lane < 16 if positive else lane >= 112, swap(r), r)


def swap_halves(r):
    return pltpu.roll(r, 4, 0)


def swap_pairs(r):
    even = (lax.broadcasted_iota(jnp.int32, SHAPE, 0) & 1) == 0
    return jnp.where(even, pltpu.roll(r, 7, 0), pltpu.roll(r, 1, 0))


def add_raw(sums, b, acc):
    s0, sb, sc, s2, sb2, sc2, sbc = sums
    p, q, r, t = acc
    b2 = b * b
    return (
        s0 + p,
        sb + b * p,
        sc + q,
        s2 + b2 * p + r,
        sb2 + b * (b2 * p + r),
        sc2 + b2 * q + t,
        sbc + b * q,
    )


def pack_kernel(i_ref, x_ref, m_ref, p_ref, o_ref):
    def take(near, far):
        o_ref[0:288, :] = x_ref[pl.ds(near, 288, stride=4), :]
        o_ref[288:576, :] = x_ref[pl.ds(far, 288, stride=4), :]
        o_ref[576:596, :] = m_ref[pl.ds(near, 20, stride=4), :]
        o_ref[596:598, :] = p_ref[pl.ds(near, 2, stride=4), :].astype(F)
        o_ref[598:600, :] = jnp.zeros((2, 128), F)

    pl.when(i_ref[0] >= 8)(lambda: take(3, 2))
    pl.when(i_ref[0] < 8)(lambda: take(0, 1))


def local_kernel(i_ref, x_ref, m_ref, p_ref, h_ref, s_ref):
    a = first_speed(i_ref)
    aa = jnp.abs(a)
    sub, lane = iotas()
    pore = p_ref[...].astype(F)
    al = field_polynomial(a, [m_ref[m] for m in range(10)])
    zero = jnp.zeros(SHAPE, F)

    def sweeps(shift, edge):
        inner = jnp.where((sub & 3) == edge, 0.0, 1.0)

        def step(jj, sums):
            bm = 2.75 - 0.5 * jj.astype(F)
            ex = jnp.exp(-(a * a) - bm * bm)
            accs = [[zero] * 4, [zero] * 4]
            polys = [at_second(al, -bm), at_second(al, bm)]
            rows = [jj * 12, (11 - jj) * 12]
            for kk in range(6):
                cm = magnitude(kk)
                c2 = cm * cm
                pr = pore * (1.0 / (aa + (1.0 + cm + bm)))
                pg = pr * (ex * math.exp(-c2))
                px, py, pz = aa * pr * inner, bm * pr, cm * pr
                for side in range(2):
                    p0, p1, p2, p3 = polys[side]
                    even, odd = p0 + c2 * p2, cm * (p1 + c2 * p3)
                    out = []
                    for up in range(2):
                        v = rows[side] + (11 - kk if up else kk)
                        g = pg * (even + odd if up else even - odd)
                        h = x_ref[v]
                        for _ in range(2):
                            h = (
                                g
                                + px * pltpu.roll(h, shift, 0)
                                + py * from_y(h, lane, side == 1, swap_halves)
                                + pz * from_z(h, lane, up == 1)
                            )
                        h_ref[v] = h
                        out.append(h)
                    s, d = out[1] + out[0], cm * (out[1] - out[0])
                    p, q, r, t = accs[side]
                    accs[side] = [p + s, q + d, r + c2 * s, t + c2 * d]
            sums = add_raw(sums, -bm, accs[0])
            return add_raw(sums, bm, accs[1])

        sums = lax.fori_loop(0, 6, step, (zero,) * 7)
        for n in range(7):
            s_ref[n] = sums[n]

    pl.when(i_ref[0] >= 8)(lambda: sweeps(1, 0))
    pl.when(i_ref[0] < 8)(lambda: sweeps(7, 3))


def halo_kernel(i_ref, g_ref, p_ref, s_ref, o_ref, d_ref):
    a = first_speed(i_ref)
    aa = jnp.abs(a)
    sub, lane = iotas()
    even_row = (sub & 1) == 0
    zero = jnp.zeros(SHAPE, F)
    forward = i_ref[0] >= 8

    def row(ref, r):
        return jnp.broadcast_to(ref[r : r + 1, :].astype(F), SHAPE)

    def pair(ref, r, s):
        return jnp.where(even_row, row(ref, r), row(ref, s))

    def own(plus, minus):
        return jnp.where(forward, pair(p_ref, plus, plus + 4), pair(p_ref, minus, minus + 4))

    pore_out, pore_0, pore_1 = pair(g_ref, 596, 597), own(0, 3), own(1, 2)
    al = field_polynomial(a, [pair(g_ref, 576 + 2 * m, 577 + 2 * m) for m in range(10)])
    cs = [-2.75 + 0.5 * (4 * t + (sub >> 1)).astype(F) for t in range(3)]
    ecs = [jnp.exp(-c * c) for c in cs]

    def back(h, t):
        if t == 0:
            return from_z(h, lane, False)
        if t == 2:
            return from_z(h, lane, True)
        return jnp.where(sub < 4, from_z(h, lane, False), from_z(h, lane, True))

    def step(jj, carry):
        bm = 2.75 - 0.5 * jj.astype(F)
        ex = jnp.exp(-(a * a) - bm * bm)
        accs = [[[zero] * 4, [zero] * 4], [[zero] * 4, [zero] * 4]]
        polys = [at_second(al, -bm), at_second(al, bm)]
        rows = [jj * 24, (11 - jj) * 24]
        for t in range(3):
            c = cs[t]
            ca = jnp.abs(c)
            r = 1.0 / (aa + ca + (1.0 + bm))
            wa, wb, wc = aa * r, bm * r, ca * r
            rg = r * ex * ecs[t]
            for side in range(2):
                p0, p1, p2, p3 = polys[side]
                g = rg * (p0 + c * (p1 + c * (p2 + c * p3)))
                base = pl.multiple_of(rows[side] + 8 * t, 8)
                near, far = g_ref[pl.ds(base, 8), :], g_ref[pl.ds(288 + base, 8), :]
                outer = pore_out * (
                    g + wa * far + wb * from_y(near, lane, side == 1, swap_pairs) + wc * back(near, t)
                )
                first = pore_0 * wa * near
                e0 = pore_0 * (
                    wa * outer + wb * from_y(first, lane, side == 1, swap_pairs) + wc * back(first, t)
                )
                e1 = pore_1 * wa * first
                d_ref[pl.ds(base, 8), :] = e0
                d_ref[pl.ds(288 + base, 8), :] = e1
                for n, e in enumerate((e0, e1)):
                    p, q, u, w = accs[n][side]
                    ce = c * e
                    cce = c * ce
                    accs[n][side] = [p + e, q + ce, u + cce, w + c * cce]
        return tuple(
            add_raw(add_raw(carry[n], -bm, accs[n][0]), bm, accs[n][1]) for n in range(2)
        )

    near_sums, far_sums = lax.fori_loop(0, 6, step, ((zero,) * 7, (zero,) * 7))
    place = sub & 3
    at_near = place == jnp.where(forward, 0, 3)
    at_far = place == jnp.where(forward, 1, 2)
    straight = (sub < 4) == even_row

    def spread(x):
        x = x + pltpu.roll(x, 2, 0)
        x = x + pltpu.roll(x, 4, 0)
        return jnp.where(straight, x, pltpu.roll(x, 1, 0))

    s = [
        s_ref[n] + jnp.where(at_near, spread(near_sums[n]), jnp.where(at_far, spread(far_sums[n]), 0.0))
        for n in range(7)
    ]
    s0, sb, sc, s2, sb2, sc2, sbc = s
    a2 = a * a
    t4, t5 = (a2 - 1.5) * s0 + s2, (a2 - 2.5) * s0 + s2
    moments = (s0, a * s0, sb, sc, t4, a * t5, (a2 - 2.5) * sb + sb2, (a2 - 2.5) * sc + sc2, a * sb, sbc)
    for m in range(10):
        value = moments[m] * VOL
        for n in range(o_ref.shape[0]):
            o_ref[n, m] = value


def final_kernel(i_ref, r_ref, h_ref, d_ref, p_ref, c_ref, left_ref, right_ref, mh_ref, o_ref, mo_ref, k_ref):
    a = first_speed(i_ref)
    sub, lane = iotas()
    pores = [left_ref[10], p_ref[...].astype(F), right_ref[10]]
    low, high = (sub & 3) == 0, (sub & 3) == 3

    def around(h):
        up = pltpu.roll(h, 16, 1)
        down = pltpu.roll(h, 112, 1)
        return (
            jnp.where(lane < 16, swap_halves(up), up)
            + jnp.where(lane >= 112, swap_halves(down), down)
            + from_z(h, lane, True)
            + from_z(h, lane, False)
        )

    for m in range(10):
        inv = 1.0 / (jnp.full(SHAPE, r_ref[m], F) + 6.0)
        q = [p * inv for p in pores]
        change = [left_ref[m], c_ref[m], right_ref[m]]
        cor = [q[n] * change[n] for n in range(3)]
        for it in range(4):
            new = list(cor)
            for n in range(3):
                if it == 3 and n != 1:
                    continue
                below = pltpu.roll(cor[n], 1, 0)
                above = pltpu.roll(cor[n], 7, 0)
                if n > 0:
                    below = jnp.where(low, pltpu.roll(cor[n - 1], 5, 0), below)
                if n < 2:
                    above = jnp.where(high, pltpu.roll(cor[n + 1], 3, 0), above)
                new[n] = q[n] * (change[n] + (below + above + around(cor[n])))
            cor = new
        k_ref[m] = cor[1]
        mo_ref[m] = mh_ref[m] + cor[1]

    al = field_polynomial(a, [k_ref[m] for m in range(10)])
    pore = pores[1]

    def step(jj, carry):
        bm = 2.75 - 0.5 * jj.astype(F)
        ex = pore * jnp.exp(-(a * a) - bm * bm)
        for side in range(2):
            p0, p1, p2, p3 = at_second(al, bm if side else -bm)
            base = (11 - jj if side else jj) * 12
            for kk in range(6):
                cm = magnitude(kk)
                c2 = cm * cm
                w = ex * math.exp(-c2)
                even, odd = w * (p0 + c2 * p2), w * (cm * (p1 + c2 * p3))
                for up in range(2):
                    v = base + (11 - kk if up else kk)
                    o_ref[pl.ds(v * 8, 8), :] = h_ref[v] + (even + odd if up else even - odd)
        return carry

    lax.fori_loop(0, 6, step, 0)

    def put(near, far):
        o_ref[pl.ds(near, 288, stride=4), :] = o_ref[pl.ds(near, 288, stride=4), :] + d_ref[0:288, :]
        o_ref[pl.ds(far, 288, stride=4), :] = o_ref[pl.ds(far, 288, stride=4), :] + d_ref[288:576, :]

    pl.when(i_ref[0] >= 8)(lambda: put(0, 1))
    pl.when(i_ref[0] < 8)(lambda: put(3, 2))


def call(kernel, outs, smem, vmem, cost, scratch=()):
    vm = pl.BlockSpec(memory_space=pltpu.VMEM)
    sm = pl.BlockSpec(memory_space=pltpu.SMEM)
    shapes = [jax.ShapeDtypeStruct(s, F) for s in outs]
    return pl.pallas_call(
        kernel,
        out_shape=shapes if len(shapes) > 1 else shapes[0],
        in_specs=[sm] * len(smem) + [vm] * len(vmem),
        out_specs=[vm] * len(shapes) if len(shapes) > 1 else vm,
        scratch_shapes=list(scratch),
        cost_estimate=pl.CostEstimate(flops=cost, bytes_accessed=4 * cost, transcendentals=0),
    )(*smem, *vmem)


def to_registers(x):
    n = x.shape[0]
    return x.reshape(n, 4, 2, 128).transpose(0, 2, 1, 3).reshape(n, 8, 128)


def from_registers(x):
    n = x.shape[0]
    return x.reshape(n, 2, 4, 128).transpose(0, 2, 1, 3).reshape(n, 4, 256)


def groups_of(key):
    found = {}
    for v in range(16):
        found.setdefault(key(v), []).append(v)
    return list(found.values())


FAR = groups_of(lambda v: (v // 8, v % 2))
NEAR = groups_of(lambda v: (v % 8) // 2)


def upwind_pairs(space):
    return [
        (v * space + s, v * space + (s + (1 if v >= 8 else -1)) % space) for v in range(16) for s in range(space)
    ]


def body(distribution, moments_old, pore_mask, synthetic_rate):
    space = lax.axis_size("space")
    i = lax.axis_index("vel").astype(jnp.int32).reshape(1)
    x = to_registers(distribution)
    old = to_registers(moments_old)
    pore = to_registers(pore_mask[None])[0]
    packed = call(
        pack_kernel, [(600, 128)], [i], [x.reshape(1152, 128), old.reshape(80, 128), pore], 1 << 16
    )
    halo = lax.ppermute(packed, ("vel", "space"), upwind_pairs(space))
    half, sums = call(local_kernel, [(144, 8, 128), (7, 8, 128)], [i], [x, old, pore], 1 << 23)
    copies, extra = call(halo_kernel, [(4, 10, 8, 128), (576, 128)], [i], [halo, pore, sums], 1 << 18)
    got = lax.all_to_all(
        copies.reshape(4, 80, 128), "vel", 0, 0, axis_index_groups=FAR, tiled=True
    )
    total = jnp.sum(got, axis=0)
    got = lax.all_to_all(
        jnp.broadcast_to(total, (4, 80, 128)), "vel", 0, 0, axis_index_groups=NEAR, tiled=True
    )
    moments_half = jnp.sum(got, axis=0)
    change = moments_half - old.reshape(80, 128)
    message = jnp.concatenate([change, pore.astype(F)], axis=0)
    count = [(s, (s + 1) % space) for s in range(space)]
    left = lax.ppermute(message, "space", count)
    right = lax.ppermute(message, "space", [(t, s) for s, t in count])
    out, moments_new = call(
        final_kernel,
        [(1152, 128), (10, 8, 128)],
        [i, synthetic_rate],
        [
            half,
            extra,
            pore,
            change.reshape(10, 8, 128),
            left.reshape(11, 8, 128),
            right.reshape(11, 8, 128),
            moments_half.reshape(10, 8, 128),
        ],
        1 << 20,
        [pltpu.VMEM((10, 8, 128), F)],
    )
    return from_registers(out.reshape(144, 8, 128)), from_registers(moments_new)


def solution(mesh):
    placed = (P("vel", "space", None), P(None, "space", None), P("space", None), P())
    return jax.shard_map(
        body,
        mesh=mesh,
        in_specs=placed,
        out_specs=(P("vel", "space", None), P(None, "space", None)),
        check_vma=False,
    )
```

```python
import math

import jax
import jax.numpy as jnp
from jax import lax
from jax.experimental import pallas as pl
from jax.experimental.pallas import tpu as pltpu
from jax.sharding import PartitionSpec as P

F = jnp.float32
SHAPE = (8, 128)
VOL = 216.0 / 2304 / math.pi**1.5
K1, K4, K5 = 2.0, 0.6667, 0.8


def magnitude(kk):
    return 2.75 - 0.5 * kk


def iotas():
    return lax.broadcasted_iota(jnp.int32, SHAPE, 0), lax.broadcasted_iota(jnp.int32, SHAPE, 1)


def first_speed(i_ref):
    return jnp.full(SHAPE, -3.0 + (i_ref[0].astype(F) + 0.5) * 0.375, F)


def field_polynomial(a, m):
    a2 = a * a
    u, w = a2 - 1.5, a2 - 2.5
    return (
        m[0] + K1 * (a * m[1]) + K4 * (u * m[4]) + K5 * (a * w * m[5]),
        K1 * m[2] + K5 * (w * m[6]) + K1 * (a * m[8]),
        K1 * m[3] + K5 * (w * m[7]),
        K4 * m[4] + K5 * (a * m[5]),
        K5 * m[6],
        K5 * m[7],
        K1 * m[9],
    )


def at_second(al, b):
    b2 = b * b
    return (
        al[0] + b * al[1] + b2 * al[3] + (b2 * b) * al[4],
        al[2] + b2 * al[5] + b * al[6],
        al[3] + b * al[4],
        al[5],
    )


def from_z(h, lane, positive):
    inside = lane & 15
    if positive:
        return jnp.where(inside == 0, pltpu.roll(h, 113, 1), pltpu.roll(h, 1, 1))
    return jnp.where(inside == 15, pltpu.roll(h, 15, 1), pltpu.roll(h, 127, 1))


def from_y(h, lane, positive, swap):
    r = pltpu.roll(h, 16 if positive else 112, 1)
    return jnp.where(lane < 16 if positive else lane >= 112, swap(r), r)


def swap_halves(r):
    return pltpu.roll(r, 4, 0)


def swap_pairs(r):
    even = (lax.broadcasted_iota(jnp.int32, SHAPE, 0) & 1) == 0
    return jnp.where(even, pltpu.roll(r, 7, 0), pltpu.roll(r, 1, 0))


def add_raw(sums, b, acc):
    s0, sb, sc, s2, sb2, sc2, sbc = sums
    p, q, r, t = acc
    b2 = b * b
    return (
        s0 + p,
        sb + b * p,
        sc + q,
        s2 + b2 * p + r,
        sb2 + b * (b2 * p + r),
        sc2 + b2 * q + t,
        sbc + b * q,
    )


def pack_kernel(i_ref, x_ref, m_ref, p_ref, o_ref):
    def take(near, far):
        o_ref[0:288, :] = x_ref[pl.ds(near, 288, stride=4), :]
        o_ref[288:576, :] = x_ref[pl.ds(far, 288, stride=4), :]
        o_ref[576:596, :] = m_ref[pl.ds(near, 20, stride=4), :]
        o_ref[596:598, :] = p_ref[pl.ds(near, 2, stride=4), :].astype(F)
        o_ref[598:600, :] = jnp.zeros((2, 128), F)

    pl.when(i_ref[0] >= 8)(lambda: take(3, 2))
    pl.when(i_ref[0] < 8)(lambda: take(0, 1))


def local_kernel(i_ref, x_ref, m_ref, p_ref, h_ref, s_ref):
    a = first_speed(i_ref)
    aa = jnp.abs(a)
    sub, lane = iotas()
    pore = p_ref[...].astype(F)
    al = field_polynomial(a, [m_ref[m] for m in range(10)])
    zero = jnp.zeros(SHAPE, F)

    def sweeps(shift, edge):
        inner = jnp.where((sub & 3) == edge, 0.0, 1.0)

        def step(jj, sums):
            bm = 2.75 - 0.5 * jj.astype(F)
            ex = jnp.exp(-(a * a) - bm * bm)
            accs = [[zero] * 4, [zero] * 4]
            polys = [at_second(al, -bm), at_second(al, bm)]
            rows = [jj * 12, (11 - jj) * 12]
            for kk in range(6):
                cm = magnitude(kk)
                c2 = cm * cm
                pr = pore * (1.0 / (aa + (1.0 + cm + bm)))
                pg = pr * (ex * math.exp(-c2))
                px, py, pz = aa * pr * inner, bm * pr, cm * pr
                for side in range(2):
                    p0, p1, p2, p3 = polys[side]
                    even, odd = p0 + c2 * p2, cm * (p1 + c2 * p3)
                    out = []
                    for up in range(2):
                        v = rows[side] + (11 - kk if up else kk)
                        g = pg * (even + odd if up else even - odd)
                        h = x_ref[v]
                        for _ in range(2):
                            h = (
                                g
                                + px * pltpu.roll(h, shift, 0)
                                + py * from_y(h, lane, side == 1, swap_halves)
                                + pz * from_z(h, lane, up == 1)
                            )
                        h_ref[v] = h
                        out.append(h)
                    s, d = out[1] + out[0], cm * (out[1] - out[0])
                    p, q, r, t = accs[side]
                    accs[side] = [p + s, q + d, r + c2 * s, t + c2 * d]
            sums = add_raw(sums, -bm, accs[0])
            return add_raw(sums, bm, accs[1])

        sums = lax.fori_loop(0, 6, step, (zero,) * 7)
        for n in range(7):
            s_ref[n] = sums[n]

    pl.when(i_ref[0] >= 8)(lambda: sweeps(1, 0))
    pl.when(i_ref[0] < 8)(lambda: sweeps(7, 3))


def halo_kernel(i_ref, g_ref, p_ref, s_ref, o_ref, d_ref):
    a = first_speed(i_ref)
    aa = jnp.abs(a)
    sub, lane = iotas()
    even_row = (sub & 1) == 0
    zero = jnp.zeros(SHAPE, F)
    forward = i_ref[0] >= 8

    def row(ref, r):
        return jnp.broadcast_to(ref[r : r + 1, :].astype(F), SHAPE)

    def pair(ref, r, s):
        return jnp.where(even_row, row(ref, r), row(ref, s))

    def own(plus, minus):
        return jnp.where(forward, pair(p_ref, plus, plus + 4), pair(p_ref, minus, minus + 4))

    pore_out, pore_0, pore_1 = pair(g_ref, 596, 597), own(0, 3), own(1, 2)
    al = field_polynomial(a, [pair(g_ref, 576 + 2 * m, 577 + 2 * m) for m in range(10)])
    cs = [-2.75 + 0.5 * (4 * t + (sub >> 1)).astype(F) for t in range(3)]
    ecs = [jnp.exp(-c * c) for c in cs]

    def back(h, t):
        if t == 0:
            return from_z(h, lane, False)
        if t == 2:
            return from_z(h, lane, True)
        return jnp.where(sub < 4, from_z(h, lane, False), from_z(h, lane, True))

    def step(jj, carry):
        bm = 2.75 - 0.5 * jj.astype(F)
        ex = jnp.exp(-(a * a) - bm * bm)
        accs = [[[zero] * 4, [zero] * 4], [[zero] * 4, [zero] * 4]]
        polys = [at_second(al, -bm), at_second(al, bm)]
        rows = [jj * 24, (11 - jj) * 24]
        for t in range(3):
            c = cs[t]
            ca = jnp.abs(c)
            r = 1.0 / (aa + ca + (1.0 + bm))
            wa, wb, wc = aa * r, bm * r, ca * r
            rg = r * ex * ecs[t]
            for side in range(2):
                p0, p1, p2, p3 = polys[side]
                g = rg * (p0 + c * (p1 + c * (p2 + c * p3)))
                base = pl.multiple_of(rows[side] + 8 * t, 8)
                near, far = g_ref[pl.ds(base, 8), :], g_ref[pl.ds(288 + base, 8), :]
                outer = pore_out * (
                    g + wa * far + wb * from_y(near, lane, side == 1, swap_pairs) + wc * back(near, t)
                )
                first = pore_0 * wa * near
                e0 = pore_0 * (
                    wa * outer + wb * from_y(first, lane, side == 1, swap_pairs) + wc * back(first, t)
                )
                e1 = pore_1 * wa * first
                d_ref[pl.ds(base, 8), :] = e0
                d_ref[pl.ds(288 + base, 8), :] = e1
                for n, e in enumerate((e0, e1)):
                    p, q, u, w = accs[n][side]
                    ce = c * e
                    cce = c * ce
                    accs[n][side] = [p + e, q + ce, u + cce, w + c * cce]
        return tuple(
            add_raw(add_raw(carry[n], -bm, accs[n][0]), bm, accs[n][1]) for n in range(2)
        )

    near_sums, far_sums = lax.fori_loop(0, 6, step, ((zero,) * 7, (zero,) * 7))
    place = sub & 3
    at_near = place == jnp.where(forward, 0, 3)
    at_far = place == jnp.where(forward, 1, 2)
    straight = (sub < 4) == even_row

    def spread(x):
        x = x + pltpu.roll(x, 2, 0)
        x = x + pltpu.roll(x, 4, 0)
        return jnp.where(straight, x, pltpu.roll(x, 1, 0))

    s = [
        s_ref[n] + jnp.where(at_near, spread(near_sums[n]), jnp.where(at_far, spread(far_sums[n]), 0.0))
        for n in range(7)
    ]
    s0, sb, sc, s2, sb2, sc2, sbc = s
    a2 = a * a
    t4, t5 = (a2 - 1.5) * s0 + s2, (a2 - 2.5) * s0 + s2
    moments = (s0, a * s0, sb, sc, t4, a * t5, (a2 - 2.5) * sb + sb2, (a2 - 2.5) * sc + sc2, a * sb, sbc)
    for m in range(10):
        value = moments[m] * VOL
        for n in range(o_ref.shape[0]):
            o_ref[n, m] = value


def final_kernel(i_ref, r_ref, h_ref, d_ref, p_ref, c_ref, left_ref, right_ref, mh_ref, o_ref, mo_ref, k_ref):
    a = first_speed(i_ref)
    sub, lane = iotas()
    pores = [left_ref[10], p_ref[...].astype(F), right_ref[10]]
    low, high = (sub & 3) == 0, (sub & 3) == 3

    def around(h):
        up = pltpu.roll(h, 16, 1)
        down = pltpu.roll(h, 112, 1)
        return (
            jnp.where(lane < 16, swap_halves(up), up)
            + jnp.where(lane >= 112, swap_halves(down), down)
            + from_z(h, lane, True)
            + from_z(h, lane, False)
        )

    for m in range(10):
        inv = 1.0 / (jnp.full(SHAPE, r_ref[m], F) + 6.0)
        q = [p * inv for p in pores]
        change = [left_ref[m], c_ref[m], right_ref[m]]
        cor = [q[n] * change[n] for n in range(3)]
        for it in range(4):
            new = list(cor)
            for n in range(3):
                if it == 3 and n != 1:
                    continue
                below = pltpu.roll(cor[n], 1, 0)
                above = pltpu.roll(cor[n], 7, 0)
                if n > 0:
                    below = jnp.where(low, pltpu.roll(cor[n - 1], 5, 0), below)
                if n < 2:
                    above = jnp.where(high, pltpu.roll(cor[n + 1], 3, 0), above)
                new[n] = q[n] * (change[n] + (below + above + around(cor[n])))
            cor = new
        k_ref[m] = cor[1]
        mo_ref[m] = mh_ref[m] + cor[1]

    al = field_polynomial(a, [k_ref[m] for m in range(10)])
    pore = pores[1]

    def step(jj, carry):
        bm = 2.75 - 0.5 * jj.astype(F)
        ex = pore * jnp.exp(-(a * a) - bm * bm)
        for side in range(2):
            p0, p1, p2, p3 = at_second(al, bm if side else -bm)
            base = (11 - jj if side else jj) * 12
            for kk in range(6):
                cm = magnitude(kk)
                c2 = cm * cm
                w = ex * math.exp(-c2)
                even, odd = w * (p0 + c2 * p2), w * (cm * (p1 + c2 * p3))
                for up in range(2):
                    v = base + (11 - kk if up else kk)
                    o_ref[pl.ds(v * 8, 8), :] = h_ref[v] + (even + odd if up else even - odd)
        return carry

    lax.fori_loop(0, 6, step, 0)

    def put(near, far):
        o_ref[pl.ds(near, 288, stride=4), :] = o_ref[pl.ds(near, 288, stride=4), :] + d_ref[0:288, :]
        o_ref[pl.ds(far, 288, stride=4), :] = o_ref[pl.ds(far, 288, stride=4), :] + d_ref[288:576, :]

    pl.when(i_ref[0] >= 8)(lambda: put(0, 1))
    pl.when(i_ref[0] < 8)(lambda: put(3, 2))


def call(kernel, outs, smem, vmem, cost, scratch=()):
    vm = pl.BlockSpec(memory_space=pltpu.VMEM)
    sm = pl.BlockSpec(memory_space=pltpu.SMEM)
    shapes = [jax.ShapeDtypeStruct(s, F) for s in outs]
    return pl.pallas_call(
        kernel,
        out_shape=shapes if len(shapes) > 1 else shapes[0],
        in_specs=[sm] * len(smem) + [vm] * len(vmem),
        out_specs=[vm] * len(shapes) if len(shapes) > 1 else vm,
        scratch_shapes=list(scratch),
        compiler_params=pltpu.CompilerParams(vmem_limit_bytes=4 << 20),
        cost_estimate=pl.CostEstimate(flops=cost, bytes_accessed=4 * cost, transcendentals=0),
    )(*smem, *vmem)


def to_registers(x):
    n = x.shape[0]
    return x.reshape(n, 4, 2, 128).transpose(0, 2, 1, 3).reshape(n, 8, 128)


def from_registers(x):
    n = x.shape[0]
    return x.reshape(n, 2, 4, 128).transpose(0, 2, 1, 3).reshape(n, 4, 256)


def groups_of(key):
    found = {}
    for v in range(16):
        found.setdefault(key(v), []).append(v)
    return list(found.values())


FAR = groups_of(lambda v: (v // 8, v % 2))
NEAR = groups_of(lambda v: (v % 8) // 2)


def upwind_pairs(space):
    return [
        (v * space + s, v * space + (s + (1 if v >= 8 else -1)) % space) for v in range(16) for s in range(space)
    ]


def body(distribution, moments_old, pore_mask, synthetic_rate):
    space = lax.axis_size("space")
    i = lax.axis_index("vel").astype(jnp.int32).reshape(1)
    x = to_registers(distribution)
    old = to_registers(moments_old)
    pore = to_registers(pore_mask[None])[0]
    packed = call(
        pack_kernel, [(600, 128)], [i], [x.reshape(1152, 128), old.reshape(80, 128), pore], 1 << 16
    )
    halo = lax.ppermute(packed, ("vel", "space"), upwind_pairs(space))
    half, sums = call(local_kernel, [(144, 8, 128), (7, 8, 128)], [i], [x, old, pore], 1 << 23)
    copies, extra = call(halo_kernel, [(4, 10, 8, 128), (576, 128)], [i], [halo, pore, sums], 1 << 18)
    got = lax.all_to_all(
        copies.reshape(4, 80, 128), "vel", 0, 0, axis_index_groups=FAR, tiled=True
    )
    total = jnp.sum(got, axis=0)
    got = lax.all_to_all(
        jnp.broadcast_to(total, (4, 80, 128)), "vel", 0, 0, axis_index_groups=NEAR, tiled=True
    )
    moments_half = jnp.sum(got, axis=0)
    change = moments_half - old.reshape(80, 128)
    message = jnp.concatenate([change, pore.astype(F)], axis=0)
    count = [(s, (s + 1) % space) for s in range(space)]
    left = lax.ppermute(message, "space", count)
    right = lax.ppermute(message, "space", [(t, s) for s, t in count])
    out, moments_new = call(
        final_kernel,
        [(1152, 128), (10, 8, 128)],
        [i, synthetic_rate],
        [
            half,
            extra,
            pore,
            change.reshape(10, 8, 128),
            left.reshape(11, 8, 128),
            right.reshape(11, 8, 128),
            moments_half.reshape(10, 8, 128),
        ],
        1 << 20,
        [pltpu.VMEM((10, 8, 128), F)],
    )
    return from_registers(out.reshape(144, 8, 128)), from_registers(moments_new)


def solution(mesh):
    placed = (P("vel", "space", None), P(None, "space", None), P("space", None), P())
    return jax.shard_map(
        body,
        mesh=mesh,
        in_specs=placed,
        out_specs=(P("vel", "space", None), P(None, "space", None)),
        check_vma=False,
    )
```

```python
import math

import jax
import jax.numpy as jnp
from jax import lax
from jax.experimental import pallas as pl
from jax.experimental.pallas import tpu as pltpu
from jax.sharding import PartitionSpec as P


F = jnp.float32
SHAPE = (8, 128)
VOL = 216.0 / 2304 / math.pi**1.5
K1, K4, K5 = 2.0, 0.6667, 0.8


def magnitude(kk):
    return 2.75 - 0.5 * kk


def iotas():
    return lax.broadcasted_iota(jnp.int32, SHAPE, 0), lax.broadcasted_iota(jnp.int32, SHAPE, 1)


def first_speed(i_ref):
    return jnp.full(SHAPE, -3.0 + (i_ref[0].astype(F) + 0.5) * 0.375, F)


def field_polynomial(a, m):
    a2 = a * a
    u, w = a2 - 1.5, a2 - 2.5
    return (
        m[0] + K1 * (a * m[1]) + K4 * (u * m[4]) + K5 * (a * w * m[5]),
        K1 * m[2] + K5 * (w * m[6]) + K1 * (a * m[8]),
        K1 * m[3] + K5 * (w * m[7]),
        K4 * m[4] + K5 * (a * m[5]),
        K5 * m[6],
        K5 * m[7],
        K1 * m[9],
    )


def at_second(al, b):
    b2 = b * b
    return (
        al[0] + b * al[1] + b2 * al[3] + (b2 * b) * al[4],
        al[2] + b2 * al[5] + b * al[6],
        al[3] + b * al[4],
        al[5],
    )


def from_z(h, lane, positive):
    inside = lane & 15
    if positive:
        return jnp.where(inside == 0, pltpu.roll(h, 113, 1), pltpu.roll(h, 1, 1))
    return jnp.where(inside == 15, pltpu.roll(h, 15, 1), pltpu.roll(h, 127, 1))


def from_y(h, lane, positive, swap):
    r = pltpu.roll(h, 16 if positive else 112, 1)
    return jnp.where(lane < 16 if positive else lane >= 112, swap(r), r)


def swap_halves(r):
    return pltpu.roll(r, 4, 0)


def swap_pairs(r):
    even = (lax.broadcasted_iota(jnp.int32, SHAPE, 0) & 1) == 0
    return jnp.where(even, pltpu.roll(r, 7, 0), pltpu.roll(r, 1, 0))


def add_raw(sums, b, acc):
    s0, sb, sc, s2, sb2, sc2, sbc = sums
    p, q, r, t = acc
    b2 = b * b
    return (
        s0 + p,
        sb + b * p,
        sc + q,
        s2 + b2 * p + r,
        sb2 + b * (b2 * p + r),
        sc2 + b2 * q + t,
        sbc + b * q,
    )


def pack_kernel(i_ref, x_hbm, m_hbm, p_hbm, g_ref, o_ref, x_ref, m_ref, p_ref, sem):
    copies = [
        pltpu.make_async_copy(src, dst, sem.at[n])
        for n, (src, dst) in enumerate(((x_hbm, x_ref), (m_hbm, m_ref), (p_hbm, p_ref)))
    ]
    for copy in copies:
        copy.start()
    a = first_speed(i_ref)
    aa = jnp.abs(a)
    sub, lane = iotas()
    even_row = (sub & 1) == 0
    zero = jnp.zeros(SHAPE, F)
    cs = [-2.75 + 0.5 * (4 * t + (sub >> 1)).astype(F) for t in range(3)]
    ecs = [jnp.exp(-c * c) for c in cs]
    for copy in copies:
        copy.wait()

    def back(h, t):
        if t == 0:
            return from_z(h, lane, False)
        if t == 2:
            return from_z(h, lane, True)
        return jnp.where(sub < 4, from_z(h, lane, False), from_z(h, lane, True))

    def build(near, far):
        o_ref[0:288, :] = x_ref[pl.ds(near, 288, stride=4), :]
        o_ref[288:576, :] = x_ref[pl.ds(far, 288, stride=4), :]
        o_ref[576:596, :] = m_ref[pl.ds(near, 20, stride=4), :]
        o_ref[596:598, :] = p_ref[pl.ds(near, 2, stride=4), :].astype(F)
        o_ref[598:600, :] = jnp.zeros((2, 128), F)

        def pair(r):
            return jnp.where(
                even_row,
                jnp.broadcast_to(o_ref[r : r + 1, :], SHAPE),
                jnp.broadcast_to(o_ref[r + 1 : r + 2, :], SHAPE),
            )

        pore = pair(596)
        al = field_polynomial(a, [pair(576 + 2 * m) for m in range(10)])

        def step(jj, carry):
            whole, down, up, minus, plus, double = carry
            bm = 2.75 - 0.5 * jj.astype(F)
            ex = jnp.exp(-(a * a) - bm * bm)
            polys = [at_second(al, -bm), at_second(al, bm)]
            outs = [[zero] * 4, [zero] * 4]
            powers = [[[zero] * 5] * 3, [[zero] * 5] * 3]
            for t in range(3):
                c = cs[t]
                ca = jnp.abs(c)
                r = 1.0 / (aa + ca + (1.0 + bm))
                wa, wb, wc = aa * r, bm * r, ca * r
                rg = r * ex * ecs[t]
                for side in range(2):
                    p0, p1, p2, p3 = polys[side]
                    g = rg * (p0 + c * (p1 + c * (p2 + c * p3)))
                    base = pl.multiple_of(((11 - jj) if side else jj) * 24 + 8 * t, 8)
                    f1, f2 = o_ref[pl.ds(base, 8), :], o_ref[pl.ds(288 + base, 8), :]
                    h = (wa * pore) * (
                        g + wa * f2 + wb * from_y(f1, lane, side == 1, swap_pairs) + wc * back(f1, t)
                    )
                    k = wa * r * f1
                    ks, hs = [k], [h]
                    for _ in range(4):
                        ks.append(c * ks[-1])
                    for _ in range(3):
                        hs.append(c * hs[-1])
                    powers[side] = powers[side][:t] + [ks] + powers[side][t + 1 :]
                    outs[side] = [p + q for p, q in zip(outs[side], hs)]
            sides = [down, up]
            for side in range(2):
                b = bm if side else -bm
                low, mid, high = powers[side]
                total = [low[n] + mid[n] + high[n] for n in range(4)]
                sides[side] = add_raw(sides[side], b, [bm * x for x in total])
                double = add_raw(double, b, total)
                minus = add_raw(minus, b, [low[n] + jnp.where(sub < 4, mid[n], 0.0) for n in range(1, 5)])
                plus = add_raw(plus, b, [high[n] + jnp.where(sub < 4, 0.0, mid[n]) for n in range(1, 5)])
                whole = add_raw(whole, b, outs[side])
            return whole, sides[0], sides[1], minus, plus, double

        groups = lax.fori_loop(0, 6, step, ((zero,) * 7,) * 6)
        scale = (1.0, 1.0, 1.0, -1.0, 1.0, aa)
        for n in range(6):
            for m in range(7):
                x = groups[n][m]
                x = x + pltpu.roll(x, 2, 0)
                x = (x + pltpu.roll(x, 4, 0)) * scale[n]
                g_ref[16 * n + 2 * m : 16 * n + 2 * m + 2, :] = x[0:2, :]
            g_ref[16 * n + 14 : 16 * n + 16, :] = jnp.zeros((2, 128), F)

    pl.when(i_ref[0] >= 8)(lambda: build(3, 2))
    pl.when(i_ref[0] < 8)(lambda: build(0, 1))


def local_kernel(i_ref, r_ref, x_ref, m_ref, p_ref, h_ref, s_ref, q_ref):
    for m in range(10):
        q_ref[m] = 1.0 / (jnp.full(SHAPE, r_ref[m], F) + 6.0)
    a = first_speed(i_ref)
    aa = jnp.abs(a)
    sub, lane = iotas()
    pore = p_ref[...].astype(F)
    al = field_polynomial(a, [m_ref[m] for m in range(10)])
    zero = jnp.zeros(SHAPE, F)

    def sweeps(shift, edge):
        inner = jnp.where((sub & 3) == edge, 0.0, 1.0)

        def step(jj, sums):
            bm = 2.75 - 0.5 * jj.astype(F)
            ex = jnp.exp(-(a * a) - bm * bm)
            accs = [[zero] * 4, [zero] * 4]
            polys = [at_second(al, -bm), at_second(al, bm)]
            rows = [jj * 12, (11 - jj) * 12]
            for kk in range(6):
                cm = magnitude(kk)
                c2 = cm * cm
                pr = pore * (1.0 / (aa + (1.0 + cm + bm)))
                pg = pr * (ex * math.exp(-c2))
                px, py, pz = aa * pr * inner, bm * pr, cm * pr
                for side in range(2):
                    p0, p1, p2, p3 = polys[side]
                    even, odd = p0 + c2 * p2, cm * (p1 + c2 * p3)
                    out = []
                    for up in range(2):
                        v = rows[side] + (11 - kk if up else kk)
                        g = pg * (even + odd if up else even - odd)
                        h = x_ref[v]
                        for _ in range(2):
                            h = (
                                g
                                + px * pltpu.roll(h, shift, 0)
                                + py * from_y(h, lane, side == 1, swap_halves)
                                + pz * from_z(h, lane, up == 1)
                            )
                        h_ref[v] = h
                        out.append(h)
                    s, d = out[1] + out[0], cm * (out[1] - out[0])
                    p, q, r, t = accs[side]
                    accs[side] = [p + s, q + d, r + c2 * s, t + c2 * d]
            sums = add_raw(sums, -bm, accs[0])
            return add_raw(sums, bm, accs[1])

        sums = lax.fori_loop(0, 6, step, (zero,) * 7)
        for n in range(7):
            s_ref[n] = sums[n]

    pl.when(i_ref[0] >= 8)(lambda: sweeps(1, 0))
    pl.when(i_ref[0] < 8)(lambda: sweeps(7, 3))


def merge_kernel(i_ref, g_ref, p_ref, s_ref, o_ref, e_ref):
    a = first_speed(i_ref)
    sub, lane = iotas()
    even_row = (sub & 1) == 0
    forward = i_ref[0] >= 8

    def row(ref, r):
        return jnp.broadcast_to(ref[r : r + 1, :].astype(F), SHAPE)

    def own(plus, minus):
        return jnp.where(
            even_row,
            jnp.where(forward, row(p_ref, plus), row(p_ref, minus)),
            jnp.where(forward, row(p_ref, plus + 4), row(p_ref, minus + 4)),
        )

    pore_0, pore_1 = own(0, 3), own(1, 2)
    for n in range(2):
        whole, down, up, minus, plus, double = [g_ref[16 * k + 8 * n : 16 * k + 8 * n + 8, :] for k in range(6)]
        e_ref[8 * n : 8 * n + 8, :] = pore_0 * (
            whole
            + from_y(pore_0 * down, lane, False, swap_pairs)
            + from_y(pore_0 * up, lane, True, swap_pairs)
            + from_z(pore_0 * minus, lane, False)
            + from_z(pore_0 * plus, lane, True)
        )
        e_ref[16 + 8 * n : 24 + 8 * n, :] = pore_0 * pore_1 * double
    place = sub & 3
    at_near = place == jnp.where(forward, 0, 3)
    at_far = place == jnp.where(forward, 1, 2)

    def spread(r):
        return jnp.where(sub < 4, row(e_ref, r), row(e_ref, r + 1))

    s0, sb, sc, s2, sb2, sc2, sbc = [
        s_ref[n] + jnp.where(at_near, spread(2 * n), jnp.where(at_far, spread(16 + 2 * n), 0.0))
        for n in range(7)
    ]
    a2 = a * a
    t4, t5 = (a2 - 1.5) * s0 + s2, (a2 - 2.5) * s0 + s2
    moments = (s0, a * s0, sb, sc, t4, a * t5, (a2 - 2.5) * sb + sb2, (a2 - 2.5) * sc + sc2, a * sb, sbc)
    for m in range(10):
        value = moments[m] * VOL
        for n in range(o_ref.shape[0]):
            o_ref[n, 8 * m : 8 * m + 8, :] = value


def total_kernel(g_ref, o_ref):
    total = (g_ref[0] + g_ref[1]) + (g_ref[2] + g_ref[3])
    for n in range(o_ref.shape[0]):
        o_ref[n] = total


def change_kernel(g_ref, m_ref, p_ref, o_ref, h_ref):
    total = (g_ref[0] + g_ref[1]) + (g_ref[2] + g_ref[3])
    h_ref[...] = total
    o_ref[0:80, :] = total - m_ref[...]
    o_ref[80:88, :] = p_ref[...].astype(F)


def halo_kernel(i_ref, g_ref, p_ref, h_ref, o_ref):
    a = first_speed(i_ref)
    aa = jnp.abs(a)
    sub, lane = iotas()
    even_row = (sub & 1) == 0

    def row(ref, r):
        return jnp.broadcast_to(ref[r : r + 1, :].astype(F), SHAPE)

    def pair(ref, r, s):
        return jnp.where(even_row, row(ref, r), row(ref, s))

    cs = [-2.75 + 0.5 * (4 * t + (sub >> 1)).astype(F) for t in range(3)]
    ecs = [jnp.exp(-c * c) for c in cs]
    pore_out = pair(g_ref, 596, 597)
    al = field_polynomial(a, [pair(g_ref, 576 + 2 * m, 577 + 2 * m) for m in range(10)])
    o_ref[...] = h_ref[...]

    def back(h, t):
        if t == 0:
            return from_z(h, lane, False)
        if t == 2:
            return from_z(h, lane, True)
        return jnp.where(sub < 4, from_z(h, lane, False), from_z(h, lane, True))

    def fix(at_0, at_1):
        pore_0, pore_1 = pair(p_ref, at_0, at_0 + 4), pair(p_ref, at_1, at_1 + 4)

        def step(jj, carry):
            bm = 2.75 - 0.5 * jj.astype(F)
            ex = jnp.exp(-(a * a) - bm * bm)
            polys = [at_second(al, -bm), at_second(al, bm)]
            for t in range(3):
                c = cs[t]
                ca = jnp.abs(c)
                r = 1.0 / (aa + ca + (1.0 + bm))
                wa, wb, wc = aa * r, bm * r, ca * r
                rg = r * ex * ecs[t]
                for side in range(2):
                    p0, p1, p2, p3 = polys[side]
                    g = rg * (p0 + c * (p1 + c * (p2 + c * p3)))
                    base = pl.multiple_of(((11 - jj) if side else jj) * 24 + 8 * t, 8)
                    near, far = g_ref[pl.ds(base, 8), :], g_ref[pl.ds(288 + base, 8), :]
                    outer = pore_out * (
                        g + wa * far + wb * from_y(near, lane, side == 1, swap_pairs) + wc * back(near, t)
                    )
                    first = pore_0 * wa * near
                    e0 = pore_0 * (
                        wa * outer + wb * from_y(first, lane, side == 1, swap_pairs) + wc * back(first, t)
                    )
                    e1 = pore_1 * wa * first
                    rows_0 = pl.ds(base * 4 + at_0, 8, stride=4)
                    rows_1 = pl.ds(base * 4 + at_1, 8, stride=4)
                    o_ref[rows_0, :] = o_ref[rows_0, :] + e0
                    o_ref[rows_1, :] = o_ref[rows_1, :] + e1
            return carry

        lax.fori_loop(0, 6, step, 0)

    pl.when(i_ref[0] >= 8)(lambda: fix(0, 1))
    pl.when(i_ref[0] < 8)(lambda: fix(3, 2))


def final_kernel(i_ref, q_ref, h_ref, c_ref, left_ref, right_ref, mh_ref, o_hbm, mo_ref, k_ref, o_ref, sem):
    a = first_speed(i_ref)
    sub, lane = iotas()
    pores = [left_ref[10], c_ref[10], right_ref[10]]
    low, high = (sub & 3) == 0, (sub & 3) == 3
    wrap_up, wrap_down = lane < 16, lane >= 112

    def around(h):
        up, down = pltpu.roll(h, 16, 1), pltpu.roll(h, 112, 1)
        same = jnp.where(wrap_up, 0.0, up) + jnp.where(wrap_down, 0.0, down)
        other = jnp.where(wrap_up, up, jnp.where(wrap_down, down, 0.0))
        return same + swap_halves(other) + from_z(h, lane, True) + from_z(h, lane, False)

    for m in range(10):
        inv = q_ref[m]
        q = [p * inv for p in pores]
        change = [left_ref[m], c_ref[m], right_ref[m]]
        cor = [q[n] * change[n] for n in range(3)]
        for it in range(4):
            new = list(cor)
            for n in range(3):
                if it == 3 and n != 1:
                    continue
                below = pltpu.roll(cor[n], 1, 0)
                above = pltpu.roll(cor[n], 7, 0)
                if n > 0:
                    below = jnp.where(low, pltpu.roll(cor[n - 1], 5, 0), below)
                if n < 2:
                    above = jnp.where(high, pltpu.roll(cor[n + 1], 3, 0), above)
                new[n] = q[n] * (change[n] + (below + above + around(cor[n])))
            cor = new
        k_ref[m] = cor[1]
        mo_ref[m] = mh_ref[m] + cor[1]

    al = field_polynomial(a, [k_ref[m] for m in range(10)])
    pore = pores[1]

    def chunk(n, j):
        rows = pl.ds(j * 12, 12)
        return pltpu.make_async_copy(o_ref.at[rows], o_hbm.at[rows], sem.at[n])

    def step(jj, carry):
        bm = 2.75 - 0.5 * jj.astype(F)
        ex = pore * jnp.exp(-(a * a) - bm * bm)
        for side in range(2):
            p0, p1, p2, p3 = at_second(al, bm if side else -bm)
            j = 11 - jj if side else jj
            for kk in range(6):
                cm = magnitude(kk)
                c2 = cm * cm
                w = ex * math.exp(-c2)
                even, odd = w * (p0 + c2 * p2), w * (cm * (p1 + c2 * p3))
                for up in range(2):
                    v = j * 12 + (11 - kk if up else kk)
                    o_ref[v] = h_ref[v] + (even + odd if up else even - odd)
            chunk(6 * side + jj, j).start()
        return carry

    lax.fori_loop(0, 6, step, 0)
    for jj in range(6):
        chunk(jj, jj).wait()
        chunk(6 + jj, 11 - jj).wait()


VM = pl.BlockSpec(memory_space=pltpu.VMEM)
SM = pl.BlockSpec(memory_space=pltpu.SMEM)
HBM = pl.BlockSpec(memory_space=pltpu.HBM)


def call(kernel, outs, args, cost, scratch=(), ins=None, out_specs=None, grant=4 << 20):
    shapes = [jax.ShapeDtypeStruct(s, F) for s in outs]
    out_specs = out_specs or [VM] * len(shapes)
    single = len(shapes) == 1
    return pl.pallas_call(
        kernel,
        out_shape=shapes[0] if single else shapes,
        in_specs=ins,
        out_specs=out_specs[0] if single else out_specs,
        scratch_shapes=list(scratch),
        compiler_params=pltpu.CompilerParams(vmem_limit_bytes=grant),
        cost_estimate=pl.CostEstimate(flops=cost, bytes_accessed=4 * cost, transcendentals=0),
    )(*args)


def to_registers(x):
    n = x.shape[0]
    return x.reshape(n, 4, 2, 128).transpose(0, 2, 1, 3).reshape(n, 8, 128)


def from_registers(x):
    n = x.shape[0]
    return x.reshape(n, 2, 4, 128).transpose(0, 2, 1, 3).reshape(n, 4, 256)


def groups_of(key):
    found = {}
    for v in range(16):
        found.setdefault(key(v), []).append(v)
    return list(found.values())


FAR = groups_of(lambda v: (v // 8, v % 2))
NEAR = groups_of(lambda v: (v % 8) // 2)


def upwind_pairs(space):
    return [
        (v * space + s, v * space + (s + (1 if v >= 8 else -1)) % space) for v in range(16) for s in range(space)
    ]


def body(distribution, moments_old, pore_mask, synthetic_rate):
    space = lax.axis_size("space")
    i = lax.axis_index("vel").astype(jnp.int32).reshape(1)
    x = to_registers(distribution)
    old = to_registers(moments_old)
    pore = to_registers(pore_mask[None])[0]
    packed, planes = call(
        pack_kernel,
        [(96, 128), (600, 128)],
        [i, x.reshape(1152, 128), old.reshape(80, 128), pore],
        1 << 20,
        [
            pltpu.VMEM((1152, 128), F),
            pltpu.VMEM((80, 128), F),
            pltpu.VMEM((8, 128), jnp.int32),
            pltpu.SemaphoreType.DMA((3,)),
        ],
        [SM, HBM, HBM, HBM],
        grant=60 << 20,
    )
    pairs = upwind_pairs(space)
    sums_in = lax.ppermute(packed, ("vel", "space"), pairs)
    planes_in = lax.ppermute(planes, ("vel", "space"), pairs)
    half, sums, inverse = call(
        local_kernel,
        [(144, 8, 128), (7, 8, 128), (10, 8, 128)],
        [i, synthetic_rate, x, old, pore],
        1 << 21,
        ins=[SM, SM, VM, VM, VM],
    )
    copies = call(
        merge_kernel,
        [(4, 80, 128)],
        [i, sums_in, pore, sums],
        1 << 16,
        [pltpu.VMEM((32, 128), F)],
        ins=[SM, VM, VM, VM],
    )
    got = lax.all_to_all(copies, "vel", 0, 0, axis_index_groups=FAR, tiled=True)
    copies = call(total_kernel, [(4, 80, 128)], [got], 1 << 16, ins=[VM])
    got = lax.all_to_all(copies, "vel", 0, 0, axis_index_groups=NEAR, tiled=True)
    message, moments_half = call(
        change_kernel, [(88, 128), (80, 128)], [got, old.reshape(80, 128), pore], 1 << 16, ins=[VM] * 3
    )
    ring = [(s, (s + 1) % space) for s in range(space)]
    left = lax.ppermute(message, "space", ring)
    right = lax.ppermute(message, "space", [(t, s) for s, t in ring])
    whole = call(
        halo_kernel,
        [(1152, 128)],
        [i, planes_in, pore, half.reshape(1152, 128)],
        1 << 20,
        ins=[SM, VM, VM, VM],
    )
    out, moments_new = call(
        final_kernel,
        [(144, 8, 128), (10, 8, 128)],
        [
            i,
            inverse,
            whole.reshape(144, 8, 128),
            message.reshape(11, 8, 128),
            left.reshape(11, 8, 128),
            right.reshape(11, 8, 128),
            moments_half.reshape(10, 8, 128),
        ],
        1 << 20,
        [pltpu.VMEM((10, 8, 128), F), pltpu.VMEM((144, 8, 128), F), pltpu.SemaphoreType.DMA((12,))],
        [SM] + [VM] * 6,
        [HBM, VM],
    )
    return from_registers(out), from_registers(moments_new)


def solution(mesh):
    placed = (P("vel", "space", None), P(None, "space", None), P("space", None), P())
    return jax.shard_map(
        body,
        mesh=mesh,
        in_specs=placed,
        out_specs=(P("vel", "space", None), P(None, "space", None)),
        check_vma=False,
    )
```

```python
import math

import jax
import jax.numpy as jnp
from jax import lax
from jax.experimental import pallas as pl
from jax.experimental.pallas import tpu as pltpu
from jax.sharding import PartitionSpec as P


F = jnp.float32
SHAPE = (8, 128)
VOL = 216.0 / 2304 / math.pi**1.5
K1, K4, K5 = 2.0, 0.6667, 0.8


def magnitude(kk):
    return 2.75 - 0.5 * kk


def iotas():
    return lax.broadcasted_iota(jnp.int32, SHAPE, 0), lax.broadcasted_iota(jnp.int32, SHAPE, 1)


def first_speed(i_ref):
    return jnp.full(SHAPE, -3.0 + (i_ref[0].astype(F) + 0.5) * 0.375, F)


def field_polynomial(a, m):
    a2 = a * a
    u, w = a2 - 1.5, a2 - 2.5
    return (
        m[0] + K1 * (a * m[1]) + K4 * (u * m[4]) + K5 * (a * w * m[5]),
        K1 * m[2] + K5 * (w * m[6]) + K1 * (a * m[8]),
        K1 * m[3] + K5 * (w * m[7]),
        K4 * m[4] + K5 * (a * m[5]),
        K5 * m[6],
        K5 * m[7],
        K1 * m[9],
    )


def at_second(al, b):
    b2 = b * b
    return (
        al[0] + b * al[1] + b2 * al[3] + (b2 * b) * al[4],
        al[2] + b2 * al[5] + b * al[6],
        al[3] + b * al[4],
        al[5],
    )


def from_z(h, lane, positive):
    inside = lane & 15
    if positive:
        return jnp.where(inside == 0, pltpu.roll(h, 113, 1), pltpu.roll(h, 1, 1))
    return jnp.where(inside == 15, pltpu.roll(h, 15, 1), pltpu.roll(h, 127, 1))


def from_y(h, lane, positive, swap):
    r = pltpu.roll(h, 16 if positive else 112, 1)
    return jnp.where(lane < 16 if positive else lane >= 112, swap(r), r)


def swap_halves(r):
    return pltpu.roll(r, 4, 0)


def swap_pairs(r):
    even = (lax.broadcasted_iota(jnp.int32, SHAPE, 0) & 1) == 0
    return jnp.where(even, pltpu.roll(r, 7, 0), pltpu.roll(r, 1, 0))


def add_raw(sums, b, acc):
    s0, sb, sc, s2, sb2, sc2, sbc = sums
    p, q, r, t = acc
    b2 = b * b
    return (
        s0 + p,
        sb + b * p,
        sc + q,
        s2 + b2 * p + r,
        sb2 + b * (b2 * p + r),
        sc2 + b2 * q + t,
        sbc + b * q,
    )


def sums_kernel(i_ref, n_ref, x_hbm, m_hbm, p_hbm, g_ref, h_hbm, s_hbm, x_ref, m_ref, p_ref, h_ref, s_ref, sem):
    copies = [
        pltpu.make_async_copy(src, dst, sem.at[n])
        for n, (src, dst) in enumerate(((x_hbm, x_ref), (m_hbm, m_ref), (p_hbm, p_ref)))
    ]
    for copy in copies:
        copy.start()
    a = first_speed(i_ref)
    aa = jnp.abs(a)
    sub, lane = iotas()
    even_row = (sub & 1) == 0
    zero = jnp.zeros(SHAPE, F)
    cs = [-2.75 + 0.5 * (4 * t + (sub >> 1)).astype(F) for t in range(3)]
    ecs = [jnp.exp(-c * c) for c in cs]
    for copy in copies:
        copy.wait()

    def back(h, t):
        if t == 0:
            return from_z(h, lane, False)
        if t == 2:
            return from_z(h, lane, True)
        return jnp.where(sub < 4, from_z(h, lane, False), from_z(h, lane, True))

    def build(near, far):
        def pair(ref, r):
            return jnp.where(
                even_row,
                jnp.broadcast_to(ref[r : r + 1, :].astype(F), SHAPE),
                jnp.broadcast_to(ref[r + 4 : r + 5, :].astype(F), SHAPE),
            )

        pore = pair(p_ref, near)
        al = field_polynomial(a, [pair(m_ref, 8 * m + near) for m in range(10)])

        def step(jj, carry):
            whole, down, up, minus, plus, double = carry
            bm = 2.75 - 0.5 * jj.astype(F)
            ex = jnp.exp(-(a * a) - bm * bm)
            polys = [at_second(al, -bm), at_second(al, bm)]
            outs = [[zero] * 4, [zero] * 4]
            powers = [[[zero] * 5] * 3, [[zero] * 5] * 3]
            for t in range(3):
                c = cs[t]
                ca = jnp.abs(c)
                r = 1.0 / (aa + ca + (1.0 + bm))
                wa, wb, wc = aa * r, bm * r, ca * r
                rg = r * ex * ecs[t]
                for side in range(2):
                    p0, p1, p2, p3 = polys[side]
                    g = rg * (p0 + c * (p1 + c * (p2 + c * p3)))
                    base = pl.multiple_of(((11 - jj) if side else jj) * 24 + 8 * t, 8)
                    f1, f2 = x_ref[pl.ds(4 * base + near, 8, stride=4), :], x_ref[pl.ds(4 * base + far, 8, stride=4), :]
                    h = (wa * pore) * (
                        g + wa * f2 + wb * from_y(f1, lane, side == 1, swap_pairs) + wc * back(f1, t)
                    )
                    k = wa * r * f1
                    ks, hs = [k], [h]
                    for _ in range(4):
                        ks.append(c * ks[-1])
                    for _ in range(3):
                        hs.append(c * hs[-1])
                    powers[side] = powers[side][:t] + [ks] + powers[side][t + 1 :]
                    outs[side] = [p + q for p, q in zip(outs[side], hs)]
            sides = [down, up]
            for side in range(2):
                b = bm if side else -bm
                low, mid, high = powers[side]
                total = [low[n] + mid[n] + high[n] for n in range(4)]
                sides[side] = add_raw(sides[side], b, [bm * x for x in total])
                double = add_raw(double, b, total)
                minus = add_raw(minus, b, [low[n] + jnp.where(sub < 4, mid[n], 0.0) for n in range(1, 5)])
                plus = add_raw(plus, b, [high[n] + jnp.where(sub < 4, 0.0, mid[n]) for n in range(1, 5)])
                whole = add_raw(whole, b, outs[side])
            return whole, sides[0], sides[1], minus, plus, double

        groups = lax.fori_loop(0, 6, step, ((zero,) * 7,) * 6)
        scale = (1.0, 1.0, 1.0, -1.0, 1.0, aa)
        for n in range(6):
            for m in range(7):
                x = groups[n][m]
                x = x + pltpu.roll(x, 2, 0)
                x = (x + pltpu.roll(x, 4, 0)) * scale[n]
                g_ref[16 * n + 2 * m : 16 * n + 2 * m + 2, :] = x[0:2, :]
            g_ref[16 * n + 14 : 16 * n + 16, :] = jnp.zeros((2, 128), F)

    pl.when(i_ref[0] >= 8)(lambda: build(3, 2))
    pl.when(i_ref[0] < 8)(lambda: build(0, 1))

    @pl.when(early(n_ref))
    def _():
        local_sweeps(i_ref, x_ref, m_ref, p_ref, h_ref, s_ref)
        copies = [
            pltpu.make_async_copy(src, dst, sem.at[n]) for n, (src, dst) in enumerate(((h_ref, h_hbm), (s_ref, s_hbm)))
        ]
        for copy in copies:
            copy.start()
        for copy in copies:
            copy.wait()


def planes_kernel(i_ref, x_ref, m_ref, p_ref, o_ref):
    def take(near, far):
        o_ref[0:288, :] = x_ref[pl.ds(near, 288, stride=4), :]
        o_ref[288:576, :] = x_ref[pl.ds(far, 288, stride=4), :]
        o_ref[576:596, :] = m_ref[pl.ds(near, 20, stride=4), :]
        o_ref[596:598, :] = p_ref[pl.ds(near, 2, stride=4), :].astype(F)
        o_ref[598:600, :] = jnp.zeros((2, 128), F)

    pl.when(i_ref[0] >= 8)(lambda: take(3, 2))
    pl.when(i_ref[0] < 8)(lambda: take(0, 1))


def late_kernel(i_ref, n_ref, x_ref, m_ref, p_ref, h_hbm, s_hbm, h_ref, s_ref, sem):
    @pl.when(early(n_ref))
    def _():
        copies = [
            pltpu.make_async_copy(src, dst, sem.at[n]) for n, (src, dst) in enumerate(((h_hbm, h_ref), (s_hbm, s_ref)))
        ]
        for copy in copies:
            copy.start()
        for copy in copies:
            copy.wait()

    pl.when(jnp.logical_not(early(n_ref)))(lambda: local_sweeps(i_ref, x_ref, m_ref, p_ref, h_ref, s_ref))


def early(n_ref):
    return lax.rem(n_ref[0], 16) < 4


def local_sweeps(i_ref, x_ref, m_ref, p_ref, h_ref, s_ref):
    a = first_speed(i_ref)
    aa = jnp.abs(a)
    sub, lane = iotas()
    pore = p_ref[...].astype(F)
    al = field_polynomial(a, [m_ref[8 * m : 8 * m + 8, :] for m in range(10)])
    zero = jnp.zeros(SHAPE, F)

    def sweeps(shift, edge):
        inner = jnp.where((sub & 3) == edge, 0.0, 1.0)

        def step(jj, sums):
            bm = 2.75 - 0.5 * jj.astype(F)
            ex = jnp.exp(-(a * a) - bm * bm)
            accs = [[zero] * 4, [zero] * 4]
            polys = [at_second(al, -bm), at_second(al, bm)]
            rows = [jj * 12, (11 - jj) * 12]
            for kk in range(6):
                cm = magnitude(kk)
                c2 = cm * cm
                pr = pore * (1.0 / (aa + (1.0 + cm + bm)))
                pg = pr * (ex * math.exp(-c2))
                px, py, pz = aa * pr * inner, bm * pr, cm * pr
                for side in range(2):
                    p0, p1, p2, p3 = polys[side]
                    even, odd = p0 + c2 * p2, cm * (p1 + c2 * p3)
                    out = []
                    for up in range(2):
                        v = rows[side] + (11 - kk if up else kk)
                        g = pg * (even + odd if up else even - odd)
                        h = x_ref[pl.ds(pl.multiple_of(8 * v, 8), 8), :]
                        for _ in range(2):
                            h = (
                                g
                                + px * pltpu.roll(h, shift, 0)
                                + py * from_y(h, lane, side == 1, swap_halves)
                                + pz * from_z(h, lane, up == 1)
                            )
                        h_ref[v] = h
                        out.append(h)
                    s, d = out[1] + out[0], cm * (out[1] - out[0])
                    p, q, r, t = accs[side]
                    accs[side] = [p + s, q + d, r + c2 * s, t + c2 * d]
            sums = add_raw(sums, -bm, accs[0])
            return add_raw(sums, bm, accs[1])

        sums = lax.fori_loop(0, 6, step, (zero,) * 7)
        for n in range(7):
            s_ref[n] = sums[n]

    pl.when(i_ref[0] >= 8)(lambda: sweeps(1, 0))
    pl.when(i_ref[0] < 8)(lambda: sweeps(7, 3))


def merge_kernel(i_ref, g_ref, p_ref, s_ref, o_ref, e_ref):
    a = first_speed(i_ref)
    sub, lane = iotas()
    even_row = (sub & 1) == 0
    forward = i_ref[0] >= 8

    def row(ref, r):
        return jnp.broadcast_to(ref[r : r + 1, :].astype(F), SHAPE)

    def own(plus, minus):
        return jnp.where(
            even_row,
            jnp.where(forward, row(p_ref, plus), row(p_ref, minus)),
            jnp.where(forward, row(p_ref, plus + 4), row(p_ref, minus + 4)),
        )

    pore_0, pore_1 = own(0, 3), own(1, 2)
    for n in range(2):
        whole, down, up, minus, plus, double = [g_ref[16 * k + 8 * n : 16 * k + 8 * n + 8, :] for k in range(6)]
        e_ref[8 * n : 8 * n + 8, :] = pore_0 * (
            whole
            + from_y(pore_0 * down, lane, False, swap_pairs)
            + from_y(pore_0 * up, lane, True, swap_pairs)
            + from_z(pore_0 * minus, lane, False)
            + from_z(pore_0 * plus, lane, True)
        )
        e_ref[16 + 8 * n : 24 + 8 * n, :] = pore_0 * pore_1 * double
    place = sub & 3
    at_near = place == jnp.where(forward, 0, 3)
    at_far = place == jnp.where(forward, 1, 2)

    def spread(r):
        return jnp.where(sub < 4, row(e_ref, r), row(e_ref, r + 1))

    s0, sb, sc, s2, sb2, sc2, sbc = [
        s_ref[n] + jnp.where(at_near, spread(2 * n), jnp.where(at_far, spread(16 + 2 * n), 0.0))
        for n in range(7)
    ]
    a2 = a * a
    t4, t5 = (a2 - 1.5) * s0 + s2, (a2 - 2.5) * s0 + s2
    moments = (s0, a * s0, sb, sc, t4, a * t5, (a2 - 2.5) * sb + sb2, (a2 - 2.5) * sc + sc2, a * sb, sbc)
    for m in range(10):
        value = moments[m] * VOL
        for n in range(o_ref.shape[0]):
            o_ref[n, 8 * m : 8 * m + 8, :] = value


def total_kernel(g_ref, o_ref):
    total = (g_ref[0] + g_ref[1]) + (g_ref[2] + g_ref[3])
    for n in range(o_ref.shape[0]):
        o_ref[n] = total


def change_kernel(g_ref, m_ref, p_ref, o_ref, h_ref):
    total = (g_ref[0] + g_ref[1]) + (g_ref[2] + g_ref[3])
    h_ref[...] = total
    o_ref[0:80, :] = total - m_ref[...]
    o_ref[80:88, :] = p_ref[...].astype(F)


def halo_kernel(i_ref, r_ref, g_ref, p_ref, h_ref, o_ref, q_ref):
    for m in range(10):
        q_ref[m] = 1.0 / (jnp.full(SHAPE, r_ref[m], F) + 6.0)
    a = first_speed(i_ref)
    aa = jnp.abs(a)
    sub, lane = iotas()
    even_row = (sub & 1) == 0

    def row(ref, r):
        return jnp.broadcast_to(ref[r : r + 1, :].astype(F), SHAPE)

    def pair(ref, r, s):
        return jnp.where(even_row, row(ref, r), row(ref, s))

    cs = [-2.75 + 0.5 * (4 * t + (sub >> 1)).astype(F) for t in range(3)]
    ecs = [jnp.exp(-c * c) for c in cs]
    pore_out = pair(g_ref, 596, 597)
    al = field_polynomial(a, [pair(g_ref, 576 + 2 * m, 577 + 2 * m) for m in range(10)])
    o_ref[...] = h_ref[...]

    def back(h, t):
        if t == 0:
            return from_z(h, lane, False)
        if t == 2:
            return from_z(h, lane, True)
        return jnp.where(sub < 4, from_z(h, lane, False), from_z(h, lane, True))

    def fix(at_0, at_1):
        pore_0, pore_1 = pair(p_ref, at_0, at_0 + 4), pair(p_ref, at_1, at_1 + 4)

        def step(jj, carry):
            bm = 2.75 - 0.5 * jj.astype(F)
            ex = jnp.exp(-(a * a) - bm * bm)
            polys = [at_second(al, -bm), at_second(al, bm)]
            for t in range(3):
                c = cs[t]
                ca = jnp.abs(c)
                r = 1.0 / (aa + ca + (1.0 + bm))
                wa, wb, wc = aa * r, bm * r, ca * r
                rg = r * ex * ecs[t]
                for side in range(2):
                    p0, p1, p2, p3 = polys[side]
                    g = rg * (p0 + c * (p1 + c * (p2 + c * p3)))
                    base = pl.multiple_of(((11 - jj) if side else jj) * 24 + 8 * t, 8)
                    near, far = g_ref[pl.ds(base, 8), :], g_ref[pl.ds(288 + base, 8), :]
                    outer = pore_out * (
                        g + wa * far + wb * from_y(near, lane, side == 1, swap_pairs) + wc * back(near, t)
                    )
                    first = pore_0 * wa * near
                    e0 = pore_0 * (
                        wa * outer + wb * from_y(first, lane, side == 1, swap_pairs) + wc * back(first, t)
                    )
                    e1 = pore_1 * wa * first
                    rows_0 = pl.ds(base * 4 + at_0, 8, stride=4)
                    rows_1 = pl.ds(base * 4 + at_1, 8, stride=4)
                    o_ref[rows_0, :] = o_ref[rows_0, :] + e0
                    o_ref[rows_1, :] = o_ref[rows_1, :] + e1
            return carry

        lax.fori_loop(0, 6, step, 0)

    pl.when(i_ref[0] >= 8)(lambda: fix(0, 1))
    pl.when(i_ref[0] < 8)(lambda: fix(3, 2))


def final_kernel(i_ref, q_ref, h_ref, c_ref, left_ref, right_ref, mh_ref, o_hbm, mo_ref, k_ref, o_ref, sem):
    a = first_speed(i_ref)
    sub, lane = iotas()
    pores = [left_ref[10], c_ref[10], right_ref[10]]
    low, high = (sub & 3) == 0, (sub & 3) == 3
    wrap_up, wrap_down = lane < 16, lane >= 112

    def around(h):
        up, down = pltpu.roll(h, 16, 1), pltpu.roll(h, 112, 1)
        same = jnp.where(wrap_up, 0.0, up) + jnp.where(wrap_down, 0.0, down)
        other = jnp.where(wrap_up, up, jnp.where(wrap_down, down, 0.0))
        return same + swap_halves(other) + from_z(h, lane, True) + from_z(h, lane, False)

    for m in range(10):
        inv = q_ref[m]
        q = [p * inv for p in pores]
        change = [left_ref[m], c_ref[m], right_ref[m]]
        cor = [q[n] * change[n] for n in range(3)]
        for it in range(4):
            new = list(cor)
            for n in range(3):
                if it == 3 and n != 1:
                    continue
                below = pltpu.roll(cor[n], 1, 0)
                above = pltpu.roll(cor[n], 7, 0)
                if n > 0:
                    below = jnp.where(low, pltpu.roll(cor[n - 1], 5, 0), below)
                if n < 2:
                    above = jnp.where(high, pltpu.roll(cor[n + 1], 3, 0), above)
                new[n] = q[n] * (change[n] + (below + above + around(cor[n])))
            cor = new
        k_ref[m] = cor[1]
        mo_ref[m] = mh_ref[m] + cor[1]

    al = field_polynomial(a, [k_ref[m] for m in range(10)])
    pore = pores[1]

    def chunk(n, j):
        rows = pl.ds(j * 12, 12)
        return pltpu.make_async_copy(o_ref.at[rows], o_hbm.at[rows], sem.at[n])

    def step(jj, carry):
        bm = 2.75 - 0.5 * jj.astype(F)
        ex = pore * jnp.exp(-(a * a) - bm * bm)
        for side in range(2):
            p0, p1, p2, p3 = at_second(al, bm if side else -bm)
            j = 11 - jj if side else jj
            for kk in range(6):
                cm = magnitude(kk)
                c2 = cm * cm
                w = ex * math.exp(-c2)
                even, odd = w * (p0 + c2 * p2), w * (cm * (p1 + c2 * p3))
                for up in range(2):
                    v = j * 12 + (11 - kk if up else kk)
                    o_ref[v] = h_ref[v] + (even + odd if up else even - odd)
            chunk(6 * side + jj, j).start()
        return carry

    lax.fori_loop(0, 6, step, 0)
    for jj in range(6):
        chunk(jj, jj).wait()
        chunk(6 + jj, 11 - jj).wait()


VM = pl.BlockSpec(memory_space=pltpu.VMEM)
SM = pl.BlockSpec(memory_space=pltpu.SMEM)
HBM = pl.BlockSpec(memory_space=pltpu.HBM)


def call(kernel, outs, args, cost, scratch=(), ins=None, out_specs=None, grant=4 << 20):
    shapes = [jax.ShapeDtypeStruct(s, F) for s in outs]
    out_specs = out_specs or [VM] * len(shapes)
    single = len(shapes) == 1
    return pl.pallas_call(
        kernel,
        out_shape=shapes[0] if single else shapes,
        in_specs=ins,
        out_specs=out_specs[0] if single else out_specs,
        scratch_shapes=list(scratch),
        compiler_params=pltpu.CompilerParams(vmem_limit_bytes=grant),
        cost_estimate=pl.CostEstimate(flops=cost, bytes_accessed=4 * cost, transcendentals=0),
    )(*args)


def to_registers(x):
    n = x.shape[0]
    return x.reshape(n, 4, 2, 128).transpose(0, 2, 1, 3).reshape(n, 8, 128)


def from_registers(x):
    n = x.shape[0]
    return x.reshape(n, 2, 4, 128).transpose(0, 2, 1, 3).reshape(n, 4, 256)


def groups_of(key):
    found = {}
    for v in range(16):
        found.setdefault(key(v), []).append(v)
    return list(found.values())


FAR = groups_of(lambda v: (v // 8, v % 2))
NEAR = groups_of(lambda v: (v % 8) // 2)


def upwind_pairs(space):
    return [
        (v * space + s, v * space + (s + (1 if v >= 8 else -1)) % space) for v in range(16) for s in range(space)
    ]


def body(distribution, moments_old, pore_mask, synthetic_rate):
    space = lax.axis_size("space")
    i = lax.axis_index("vel").astype(jnp.int32).reshape(1)
    n = lax.axis_index("space").astype(jnp.int32).reshape(1)
    x = to_registers(distribution)
    old = to_registers(moments_old)
    pore = to_registers(pore_mask[None])[0]
    shapes = [(144, 8, 128), (7, 8, 128)]
    flat = [x.reshape(1152, 128), old.reshape(80, 128), pore]
    packed, half, sums = call(
        sums_kernel,
        [(96, 128)] + shapes,
        [i, n] + flat,
        1 << 20,
        [
            pltpu.VMEM((1152, 128), F),
            pltpu.VMEM((80, 128), F),
            pltpu.VMEM((8, 128), jnp.int32),
            pltpu.VMEM((144, 8, 128), F),
            pltpu.VMEM((7, 8, 128), F),
            pltpu.SemaphoreType.DMA((3,)),
        ],
        [SM, SM, HBM, HBM, HBM],
        [VM, HBM, HBM],
        grant=60 << 20,
    )
    pairs = upwind_pairs(space)
    sums_in = lax.ppermute(packed, ("vel", "space"), pairs)
    planes = call(planes_kernel, [(600, 128)], [i] + flat, 1 << 16, ins=[SM, VM, VM, VM])
    planes_in = lax.ppermute(planes, ("vel", "space"), pairs)
    half, sums = call(
        late_kernel,
        shapes,
        [i, n] + flat + [half, sums],
        1 << 21,
        [pltpu.SemaphoreType.DMA((2,))],
        [SM, SM, VM, VM, VM, HBM, HBM],
    )
    copies = call(
        merge_kernel,
        [(4, 80, 128)],
        [i, sums_in, pore, sums],
        1 << 16,
        [pltpu.VMEM((32, 128), F)],
        ins=[SM, VM, VM, VM],
    )
    got = lax.all_to_all(copies, "vel", 0, 0, axis_index_groups=FAR, tiled=True)
    copies = call(total_kernel, [(4, 80, 128)], [got], 1 << 16, ins=[VM])
    got = lax.all_to_all(copies, "vel", 0, 0, axis_index_groups=NEAR, tiled=True)
    message, moments_half = call(
        change_kernel, [(88, 128), (80, 128)], [got, old.reshape(80, 128), pore], 1 << 16, ins=[VM] * 3
    )
    ring = [(s, (s + 1) % space) for s in range(space)]
    left = lax.ppermute(message, "space", ring)
    right = lax.ppermute(message, "space", [(t, s) for s, t in ring])
    whole, inverse = call(
        halo_kernel,
        [(1152, 128), (10, 8, 128)],
        [i, synthetic_rate, planes_in, pore, half.reshape(1152, 128)],
        1 << 20,
        ins=[SM, SM, VM, VM, VM],
    )
    out, moments_new = call(
        final_kernel,
        [(144, 8, 128), (10, 8, 128)],
        [
            i,
            inverse,
            whole.reshape(144, 8, 128),
            message.reshape(11, 8, 128),
            left.reshape(11, 8, 128),
            right.reshape(11, 8, 128),
            moments_half.reshape(10, 8, 128),
        ],
        1 << 20,
        [pltpu.VMEM((10, 8, 128), F), pltpu.VMEM((144, 8, 128), F), pltpu.SemaphoreType.DMA((12,))],
        [SM] + [VM] * 6,
        [HBM, VM],
    )
    return from_registers(out), from_registers(moments_new)


def solution(mesh):
    placed = (P("vel", "space", None), P(None, "space", None), P("space", None), P())
    return jax.shard_map(
        body,
        mesh=mesh,
        in_specs=placed,
        out_specs=(P("vel", "space", None), P(None, "space", None)),
        check_vma=False,
    )
```

```python
import math

import jax
import jax.numpy as jnp
from jax import lax
from jax.experimental import pallas as pl
from jax.experimental.pallas import tpu as pltpu
from jax.sharding import PartitionSpec as P


F = jnp.float32
SHAPE = (8, 128)
VOL = 216.0 / 2304 / math.pi**1.5
K1, K4, K5 = 2.0, 0.6667, 0.8


def magnitude(kk):
    return 2.75 - 0.5 * kk


def iotas():
    return lax.broadcasted_iota(jnp.int32, SHAPE, 0), lax.broadcasted_iota(jnp.int32, SHAPE, 1)


def first_speed(i_ref):
    return jnp.full(SHAPE, -3.0 + (i_ref[0].astype(F) + 0.5) * 0.375, F)


def field_polynomial(a, m):
    a2 = a * a
    u, w = a2 - 1.5, a2 - 2.5
    return (
        m[0] + K1 * (a * m[1]) + K4 * (u * m[4]) + K5 * (a * w * m[5]),
        K1 * m[2] + K5 * (w * m[6]) + K1 * (a * m[8]),
        K1 * m[3] + K5 * (w * m[7]),
        K4 * m[4] + K5 * (a * m[5]),
        K5 * m[6],
        K5 * m[7],
        K1 * m[9],
    )


def at_second(al, b):
    b2 = b * b
    return (
        al[0] + b * al[1] + b2 * al[3] + (b2 * b) * al[4],
        al[2] + b2 * al[5] + b * al[6],
        al[3] + b * al[4],
        al[5],
    )


def from_z(h, lane, positive):
    inside = lane & 15
    if positive:
        return jnp.where(inside == 0, pltpu.roll(h, 113, 1), pltpu.roll(h, 1, 1))
    return jnp.where(inside == 15, pltpu.roll(h, 15, 1), pltpu.roll(h, 127, 1))


def from_y(h, lane, positive, swap):
    r = pltpu.roll(h, 16 if positive else 112, 1)
    return jnp.where(lane < 16 if positive else lane >= 112, swap(r), r)


def swap_halves(r):
    return pltpu.roll(r, 4, 0)


def swap_pairs(r):
    even = (lax.broadcasted_iota(jnp.int32, SHAPE, 0) & 1) == 0
    return jnp.where(even, pltpu.roll(r, 7, 0), pltpu.roll(r, 1, 0))


def add_raw(sums, b, acc):
    s0, sb, sc, s2, sb2, sc2, sbc = sums
    p, q, r, t = acc
    b2 = b * b
    return (
        s0 + p,
        sb + b * p,
        sc + q,
        s2 + b2 * p + r,
        sb2 + b * (b2 * p + r),
        sc2 + b2 * q + t,
        sbc + b * q,
    )


def sums_kernel(i_ref, n_ref, x_hbm, m_hbm, p_hbm, g_ref, h_hbm, s_hbm, x_ref, m_ref, p_ref, h_ref, s_ref, sem):
    copies = [
        pltpu.make_async_copy(src, dst, sem.at[n])
        for n, (src, dst) in enumerate(((x_hbm, x_ref), (m_hbm, m_ref), (p_hbm, p_ref)))
    ]
    for copy in copies:
        copy.start()
    a = first_speed(i_ref)
    aa = jnp.abs(a)
    sub, lane = iotas()
    even_row = (sub & 1) == 0
    zero = jnp.zeros(SHAPE, F)
    cs = [-2.75 + 0.5 * (4 * t + (sub >> 1)).astype(F) for t in range(3)]
    ecs = [jnp.exp(-c * c) for c in cs]
    for copy in copies:
        copy.wait()

    def back(h, t):
        if t == 0:
            return from_z(h, lane, False)
        if t == 2:
            return from_z(h, lane, True)
        return jnp.where(sub < 4, from_z(h, lane, False), from_z(h, lane, True))

    def build(near, far):
        def pair(ref, r):
            return jnp.where(
                even_row,
                jnp.broadcast_to(ref[r : r + 1, :].astype(F), SHAPE),
                jnp.broadcast_to(ref[r + 4 : r + 5, :].astype(F), SHAPE),
            )

        pore = pair(p_ref, near)
        al = field_polynomial(a, [pair(m_ref, 8 * m + near) for m in range(10)])

        def step(jj, carry):
            whole, down, up, minus, plus, double = carry
            bm = 2.75 - 0.5 * jj.astype(F)
            ex = jnp.exp(-(a * a) - bm * bm)
            polys = [at_second(al, -bm), at_second(al, bm)]
            outs = [[zero] * 4, [zero] * 4]
            powers = [[[zero] * 5] * 3, [[zero] * 5] * 3]
            for t in range(3):
                c = cs[t]
                ca = jnp.abs(c)
                r = 1.0 / (aa + ca + (1.0 + bm))
                wa, wb, wc = aa * r, bm * r, ca * r
                rg = r * ex * ecs[t]
                for side in range(2):
                    p0, p1, p2, p3 = polys[side]
                    g = rg * (p0 + c * (p1 + c * (p2 + c * p3)))
                    base = pl.multiple_of(((11 - jj) if side else jj) * 24 + 8 * t, 8)
                    f1, f2 = x_ref[pl.ds(4 * base + near, 8, stride=4), :], x_ref[pl.ds(4 * base + far, 8, stride=4), :]
                    h = (wa * pore) * (
                        g + wa * f2 + wb * from_y(f1, lane, side == 1, swap_pairs) + wc * back(f1, t)
                    )
                    k = wa * r * f1
                    ks, hs = [k], [h]
                    for _ in range(4):
                        ks.append(c * ks[-1])
                    for _ in range(3):
                        hs.append(c * hs[-1])
                    powers[side] = powers[side][:t] + [ks] + powers[side][t + 1 :]
                    outs[side] = [p + q for p, q in zip(outs[side], hs)]
            sides = [down, up]
            for side in range(2):
                b = bm if side else -bm
                low, mid, high = powers[side]
                total = [low[n] + mid[n] + high[n] for n in range(4)]
                sides[side] = add_raw(sides[side], b, [bm * x for x in total])
                double = add_raw(double, b, total)
                minus = add_raw(minus, b, [low[n] + jnp.where(sub < 4, mid[n], 0.0) for n in range(1, 5)])
                plus = add_raw(plus, b, [high[n] + jnp.where(sub < 4, 0.0, mid[n]) for n in range(1, 5)])
                whole = add_raw(whole, b, outs[side])
            return whole, sides[0], sides[1], minus, plus, double

        groups = lax.fori_loop(0, 6, step, ((zero,) * 7,) * 6)
        scale = (1.0, 1.0, 1.0, -1.0, 1.0, aa)
        for n in range(6):
            for m in range(7):
                x = groups[n][m]
                x = x + pltpu.roll(x, 2, 0)
                x = (x + pltpu.roll(x, 4, 0)) * scale[n]
                g_ref[16 * n + 2 * m : 16 * n + 2 * m + 2, :] = x[0:2, :]
            g_ref[16 * n + 14 : 16 * n + 16, :] = jnp.zeros((2, 128), F)

    pl.when(i_ref[0] >= 8)(lambda: build(3, 2))
    pl.when(i_ref[0] < 8)(lambda: build(0, 1))

    @pl.when(early(n_ref))
    def _():
        local_sweeps(i_ref, x_ref, m_ref, p_ref, h_ref, s_ref)
        copies = [
            pltpu.make_async_copy(src, dst, sem.at[n]) for n, (src, dst) in enumerate(((h_ref, h_hbm), (s_ref, s_hbm)))
        ]
        for copy in copies:
            copy.start()
        for copy in copies:
            copy.wait()


def planes_kernel(i_ref, x_ref, m_ref, p_ref, o_ref):
    def take(near, far):
        o_ref[0:288, :] = x_ref[pl.ds(near, 288, stride=4), :]
        o_ref[288:576, :] = x_ref[pl.ds(far, 288, stride=4), :]
        o_ref[576:596, :] = m_ref[pl.ds(near, 20, stride=4), :]
        o_ref[596:598, :] = p_ref[pl.ds(near, 2, stride=4), :].astype(F)
        o_ref[598:600, :] = jnp.zeros((2, 128), F)

    pl.when(i_ref[0] >= 8)(lambda: take(3, 2))
    pl.when(i_ref[0] < 8)(lambda: take(0, 1))


def late_kernel(i_ref, n_ref, x_ref, m_ref, p_ref, h_hbm, s_hbm, h_ref, s_ref, sem):
    @pl.when(early(n_ref))
    def _():
        copies = [
            pltpu.make_async_copy(src, dst, sem.at[n]) for n, (src, dst) in enumerate(((h_hbm, h_ref), (s_hbm, s_ref)))
        ]
        for copy in copies:
            copy.start()
        for copy in copies:
            copy.wait()

    pl.when(jnp.logical_not(early(n_ref)))(lambda: local_sweeps(i_ref, x_ref, m_ref, p_ref, h_ref, s_ref))


def early(n_ref):
    return lax.rem(n_ref[0], 16) < 4


def local_sweeps(i_ref, x_ref, m_ref, p_ref, h_ref, s_ref):
    a = first_speed(i_ref)
    aa = jnp.abs(a)
    sub, lane = iotas()
    pore = p_ref[...].astype(F)
    al = field_polynomial(a, [m_ref[8 * m : 8 * m + 8, :] for m in range(10)])
    zero = jnp.zeros(SHAPE, F)

    def sweeps(shift, edge):
        inner = jnp.where((sub & 3) == edge, 0.0, 1.0)

        def step(jj, sums):
            bm = 2.75 - 0.5 * jj.astype(F)
            ex = jnp.exp(-(a * a) - bm * bm)
            accs = [[zero] * 4, [zero] * 4]
            polys = [at_second(al, -bm), at_second(al, bm)]
            rows = [jj * 12, (11 - jj) * 12]
            for kk in range(6):
                cm = magnitude(kk)
                c2 = cm * cm
                pr = pore * (1.0 / (aa + (1.0 + cm + bm)))
                pg = pr * (ex * math.exp(-c2))
                px, py, pz = aa * pr * inner, bm * pr, cm * pr
                for side in range(2):
                    p0, p1, p2, p3 = polys[side]
                    even, odd = p0 + c2 * p2, cm * (p1 + c2 * p3)
                    out = []
                    for up in range(2):
                        v = rows[side] + (11 - kk if up else kk)
                        g = pg * (even + odd if up else even - odd)
                        h = x_ref[pl.ds(pl.multiple_of(8 * v, 8), 8), :]
                        for _ in range(2):
                            h = (
                                g
                                + px * pltpu.roll(h, shift, 0)
                                + py * from_y(h, lane, side == 1, swap_halves)
                                + pz * from_z(h, lane, up == 1)
                            )
                        h_ref[v] = h
                        out.append(h)
                    s, d = out[1] + out[0], cm * (out[1] - out[0])
                    p, q, r, t = accs[side]
                    accs[side] = [p + s, q + d, r + c2 * s, t + c2 * d]
            sums = add_raw(sums, -bm, accs[0])
            return add_raw(sums, bm, accs[1])

        sums = lax.fori_loop(0, 6, step, (zero,) * 7)
        for n in range(7):
            s_ref[n] = sums[n]

    pl.when(i_ref[0] >= 8)(lambda: sweeps(1, 0))
    pl.when(i_ref[0] < 8)(lambda: sweeps(7, 3))


def merge_kernel(i_ref, g_ref, p_ref, s_ref, o_ref, e_ref):
    a = first_speed(i_ref)
    sub, lane = iotas()
    even_row = (sub & 1) == 0
    forward = i_ref[0] >= 8

    def row(ref, r):
        return jnp.broadcast_to(ref[r : r + 1, :].astype(F), SHAPE)

    def own(plus, minus):
        return jnp.where(
            even_row,
            jnp.where(forward, row(p_ref, plus), row(p_ref, minus)),
            jnp.where(forward, row(p_ref, plus + 4), row(p_ref, minus + 4)),
        )

    pore_0, pore_1 = own(0, 3), own(1, 2)
    for n in range(2):
        whole, down, up, minus, plus, double = [g_ref[16 * k + 8 * n : 16 * k + 8 * n + 8, :] for k in range(6)]
        e_ref[8 * n : 8 * n + 8, :] = pore_0 * (
            whole
            + from_y(pore_0 * down, lane, False, swap_pairs)
            + from_y(pore_0 * up, lane, True, swap_pairs)
            + from_z(pore_0 * minus, lane, False)
            + from_z(pore_0 * plus, lane, True)
        )
        e_ref[16 + 8 * n : 24 + 8 * n, :] = pore_0 * pore_1 * double
    place = sub & 3
    at_near = place == jnp.where(forward, 0, 3)
    at_far = place == jnp.where(forward, 1, 2)

    def spread(r):
        return jnp.where(sub < 4, row(e_ref, r), row(e_ref, r + 1))

    s0, sb, sc, s2, sb2, sc2, sbc = [
        s_ref[n] + jnp.where(at_near, spread(2 * n), jnp.where(at_far, spread(16 + 2 * n), 0.0))
        for n in range(7)
    ]
    a2 = a * a
    t4, t5 = (a2 - 1.5) * s0 + s2, (a2 - 2.5) * s0 + s2
    moments = (s0, a * s0, sb, sc, t4, a * t5, (a2 - 2.5) * sb + sb2, (a2 - 2.5) * sc + sc2, a * sb, sbc)
    for m in range(10):
        value = moments[m] * VOL
        for n in range(o_ref.shape[0]):
            o_ref[n, 8 * m : 8 * m + 8, :] = value


def total_kernel(g_ref, o_ref):
    total = (g_ref[0] + g_ref[1]) + (g_ref[2] + g_ref[3])
    for n in range(o_ref.shape[0]):
        o_ref[n] = total


def change_kernel(g_ref, m_ref, p_ref, f_ref, o_ref, w_ref, h_ref):
    total = (g_ref[0] + g_ref[1]) + (g_ref[2] + g_ref[3])
    change = total - m_ref[...]
    pore = p_ref[...].astype(F)
    h_ref[...] = total
    for ref in (o_ref, w_ref):
        ref[0:80, :] = change
        ref[80:88, :] = pore
    w_ref[88:688, :] = f_ref[...]


def halo_kernel(i_ref, u_ref, w_ref, p_ref, h_ref, o_ref):
    a = first_speed(i_ref)
    aa = jnp.abs(a)
    sub, lane = iotas()
    even_row = (sub & 1) == 0

    def row(ref, r):
        return jnp.broadcast_to(ref[r : r + 1, :].astype(F), SHAPE)

    def pair(ref, r, s):
        return jnp.where(even_row, row(ref, r), row(ref, s))

    cs = [-2.75 + 0.5 * (4 * t + (sub >> 1)).astype(F) for t in range(3)]
    ecs = [jnp.exp(-c * c) for c in cs]
    o_ref[...] = h_ref[...]

    def back(h, t):
        if t == 0:
            return from_z(h, lane, False)
        if t == 2:
            return from_z(h, lane, True)
        return jnp.where(sub < 4, from_z(h, lane, False), from_z(h, lane, True))

    def fix(g_ref, start, at_0, at_1):
        pore_out = pair(g_ref, start + 596, start + 597)
        al = field_polynomial(a, [pair(g_ref, start + 576 + 2 * m, start + 577 + 2 * m) for m in range(10)])
        pore_0, pore_1 = pair(p_ref, at_0, at_0 + 4), pair(p_ref, at_1, at_1 + 4)

        def step(jj, carry):
            bm = 2.75 - 0.5 * jj.astype(F)
            ex = jnp.exp(-(a * a) - bm * bm)
            polys = [at_second(al, -bm), at_second(al, bm)]
            for t in range(3):
                c = cs[t]
                ca = jnp.abs(c)
                r = 1.0 / (aa + ca + (1.0 + bm))
                wa, wb, wc = aa * r, bm * r, ca * r
                rg = r * ex * ecs[t]
                for side in range(2):
                    p0, p1, p2, p3 = polys[side]
                    g = rg * (p0 + c * (p1 + c * (p2 + c * p3)))
                    base = pl.multiple_of(((11 - jj) if side else jj) * 24 + 8 * t, 8)
                    near, far = g_ref[pl.ds(start + base, 8), :], g_ref[pl.ds(start + 288 + base, 8), :]
                    outer = pore_out * (
                        g + wa * far + wb * from_y(near, lane, side == 1, swap_pairs) + wc * back(near, t)
                    )
                    first = pore_0 * wa * near
                    e0 = pore_0 * (
                        wa * outer + wb * from_y(first, lane, side == 1, swap_pairs) + wc * back(first, t)
                    )
                    e1 = pore_1 * wa * first
                    rows_0 = pl.ds(base * 4 + at_0, 8, stride=4)
                    rows_1 = pl.ds(base * 4 + at_1, 8, stride=4)
                    o_ref[rows_0, :] = o_ref[rows_0, :] + e0
                    o_ref[rows_1, :] = o_ref[rows_1, :] + e1
            return carry

        lax.fori_loop(0, 6, step, 0)

    pl.when(i_ref[0] >= 8)(lambda: fix(u_ref, 0, 0, 1))
    pl.when(i_ref[0] < 8)(lambda: fix(w_ref, 88, 3, 2))


def final_kernel(i_ref, q_ref, h_ref, c_ref, left_ref, right_ref, mh_ref, o_hbm, mo_ref, k_ref, o_ref, sem):
    a = first_speed(i_ref)
    sub, lane = iotas()
    pores = [ref[80:88, :] for ref in (left_ref, c_ref, right_ref)]
    low, high = (sub & 3) == 0, (sub & 3) == 3
    wrap_up, wrap_down = lane < 16, lane >= 112

    def around(h):
        up, down = pltpu.roll(h, 16, 1), pltpu.roll(h, 112, 1)
        same = jnp.where(wrap_up, 0.0, up) + jnp.where(wrap_down, 0.0, down)
        other = jnp.where(wrap_up, up, jnp.where(wrap_down, down, 0.0))
        return same + swap_halves(other) + from_z(h, lane, True) + from_z(h, lane, False)

    for m in range(10):
        inv = jnp.broadcast_to(q_ref[m : m + 1, :], SHAPE)
        q = [p * inv for p in pores]
        change = [ref[8 * m : 8 * m + 8, :] for ref in (left_ref, c_ref, right_ref)]
        cor = [q[n] * change[n] for n in range(3)]
        for it in range(4):
            new = list(cor)
            for n in range(3):
                if it == 3 and n != 1:
                    continue
                below = pltpu.roll(cor[n], 1, 0)
                above = pltpu.roll(cor[n], 7, 0)
                if n > 0:
                    below = jnp.where(low, pltpu.roll(cor[n - 1], 5, 0), below)
                if n < 2:
                    above = jnp.where(high, pltpu.roll(cor[n + 1], 3, 0), above)
                new[n] = q[n] * (change[n] + (below + above + around(cor[n])))
            cor = new
        k_ref[m] = cor[1]
        mo_ref[m] = mh_ref[m] + cor[1]

    al = field_polynomial(a, [k_ref[m] for m in range(10)])
    pore = pores[1]

    def chunk(n, j):
        rows = pl.ds(j * 12, 12)
        return pltpu.make_async_copy(o_ref.at[rows], o_hbm.at[rows], sem.at[n])

    def step(jj, carry):
        bm = 2.75 - 0.5 * jj.astype(F)
        ex = pore * jnp.exp(-(a * a) - bm * bm)
        for side in range(2):
            p0, p1, p2, p3 = at_second(al, bm if side else -bm)
            j = 11 - jj if side else jj
            for kk in range(6):
                cm = magnitude(kk)
                c2 = cm * cm
                w = ex * math.exp(-c2)
                even, odd = w * (p0 + c2 * p2), w * (cm * (p1 + c2 * p3))
                for up in range(2):
                    v = j * 12 + (11 - kk if up else kk)
                    o_ref[v] = h_ref[v] + (even + odd if up else even - odd)
            chunk(6 * side + jj, j).start()
        return carry

    lax.fori_loop(0, 6, step, 0)
    for jj in range(6):
        chunk(jj, jj).wait()
        chunk(6 + jj, 11 - jj).wait()


VM = pl.BlockSpec(memory_space=pltpu.VMEM)
SM = pl.BlockSpec(memory_space=pltpu.SMEM)
HBM = pl.BlockSpec(memory_space=pltpu.HBM)


def call(kernel, outs, args, cost, scratch=(), ins=None, out_specs=None, grant=4 << 20):
    shapes = [jax.ShapeDtypeStruct(s, F) for s in outs]
    out_specs = out_specs or [VM] * len(shapes)
    single = len(shapes) == 1
    return pl.pallas_call(
        kernel,
        out_shape=shapes[0] if single else shapes,
        in_specs=ins,
        out_specs=out_specs[0] if single else out_specs,
        scratch_shapes=list(scratch),
        compiler_params=pltpu.CompilerParams(vmem_limit_bytes=grant),
        cost_estimate=pl.CostEstimate(flops=cost, bytes_accessed=4 * cost, transcendentals=0),
    )(*args)


def to_registers(x):
    n = x.shape[0]
    return x.reshape(n, 4, 2, 128).transpose(0, 2, 1, 3).reshape(n, 8, 128)


def from_registers(x):
    n = x.shape[0]
    return x.reshape(n, 2, 4, 128).transpose(0, 2, 1, 3).reshape(n, 4, 256)


def groups_of(key):
    found = {}
    for v in range(16):
        found.setdefault(key(v), []).append(v)
    return list(found.values())


FAR = groups_of(lambda v: (v // 8, v % 2))
NEAR = groups_of(lambda v: (v % 8) // 2)


def upwind_pairs(space, first=0):
    return [
        (v * space + s, v * space + (s + (1 if v >= 8 else -1)) % space) for v in range(first, 16) for s in range(space)
    ]


def body(distribution, moments_old, pore_mask, synthetic_rate):
    space = lax.axis_size("space")
    i = lax.axis_index("vel").astype(jnp.int32).reshape(1)
    n = lax.axis_index("space").astype(jnp.int32).reshape(1)
    x = to_registers(distribution)
    old = to_registers(moments_old)
    pore = to_registers(pore_mask[None])[0]
    shapes = [(144, 8, 128), (7, 8, 128)]
    flat = [x.reshape(1152, 128), old.reshape(80, 128), pore]
    packed, half, sums = call(
        sums_kernel,
        [(96, 128)] + shapes,
        [i, n] + flat,
        1 << 20,
        [
            pltpu.VMEM((1152, 128), F),
            pltpu.VMEM((80, 128), F),
            pltpu.VMEM((8, 128), jnp.int32),
            pltpu.VMEM((144, 8, 128), F),
            pltpu.VMEM((7, 8, 128), F),
            pltpu.SemaphoreType.DMA((3,)),
        ],
        [SM, SM, HBM, HBM, HBM],
        [VM, HBM, HBM],
        grant=60 << 20,
    )
    pairs = upwind_pairs(space)
    sums_in = lax.ppermute(packed, ("vel", "space"), pairs)
    planes = call(planes_kernel, [(600, 128)], [i] + flat, 1 << 16, ins=[SM, VM, VM, VM])
    planes_in = lax.ppermute(planes, ("vel", "space"), upwind_pairs(space, 8))
    half, sums = call(
        late_kernel,
        shapes,
        [i, n] + flat + [half, sums],
        1 << 21,
        [pltpu.SemaphoreType.DMA((2,))],
        [SM, SM, VM, VM, VM, HBM, HBM],
    )
    copies = call(
        merge_kernel,
        [(4, 80, 128)],
        [i, sums_in, pore, sums],
        1 << 16,
        [pltpu.VMEM((32, 128), F)],
        ins=[SM, VM, VM, VM],
    )
    got = lax.all_to_all(copies, "vel", 0, 0, axis_index_groups=FAR, tiled=True)
    copies = call(total_kernel, [(4, 80, 128)], [got], 1 << 16, ins=[VM])
    got = lax.all_to_all(copies, "vel", 0, 0, axis_index_groups=NEAR, tiled=True)
    message, message_down, moments_half = call(
        change_kernel,
        [(88, 128), (688, 128), (80, 128)],
        [got, old.reshape(80, 128), pore, planes],
        1 << 16,
        ins=[VM] * 4,
    )
    ring = [(s, (s + 1) % space) for s in range(space)]
    left = lax.ppermute(message, "space", ring)
    right = lax.ppermute(message_down, "space", [(t, s) for s, t in ring])
    whole = call(
        halo_kernel,
        [(1152, 128)],
        [i, planes_in, right, pore, half.reshape(1152, 128)],
        1 << 20,
        ins=[SM, VM, VM, VM, VM],
    )
    inverse = jnp.broadcast_to((1.0 / (synthetic_rate + 6.0))[:, None], (10, 128))
    out, moments_new = call(
        final_kernel,
        [(144, 8, 128), (10, 8, 128)],
        [
            i,
            inverse,
            whole.reshape(144, 8, 128),
            message,
            left,
            right,
            moments_half.reshape(10, 8, 128),
        ],
        1 << 20,
        [pltpu.VMEM((10, 8, 128), F), pltpu.VMEM((144, 8, 128), F), pltpu.SemaphoreType.DMA((12,))],
        [SM] + [VM] * 6,
        [HBM, VM],
    )
    return from_registers(out), from_registers(moments_new)


def solution(mesh):
    placed = (P("vel", "space", None), P(None, "space", None), P("space", None), P())
    return jax.shard_map(
        body,
        mesh=mesh,
        in_specs=placed,
        out_specs=(P("vel", "space", None), P(None, "space", None)),
        check_vma=False,
    )
```

```python
import functools
import math

import jax
import jax.numpy as jnp
from jax import lax
from jax.experimental import pallas as pl
from jax.experimental.pallas import tpu as pltpu
from jax.sharding import PartitionSpec as P


F = jnp.float32
SHAPE = (8, 128)
VOL = 216.0 / 2304 / math.pi**1.5
K1, K4, K5 = 2.0, 0.6667, 0.8


def magnitude(kk):
    return 2.75 - 0.5 * kk


def iotas():
    return lax.broadcasted_iota(jnp.int32, SHAPE, 0), lax.broadcasted_iota(jnp.int32, SHAPE, 1)


def first_speed(i_ref):
    return jnp.full(SHAPE, -3.0 + (i_ref[0].astype(F) + 0.5) * 0.375, F)


def field_polynomial(a, m):
    a2 = a * a
    u, w = a2 - 1.5, a2 - 2.5
    return (
        m[0] + K1 * (a * m[1]) + K4 * (u * m[4]) + K5 * (a * w * m[5]),
        K1 * m[2] + K5 * (w * m[6]) + K1 * (a * m[8]),
        K1 * m[3] + K5 * (w * m[7]),
        K4 * m[4] + K5 * (a * m[5]),
        K5 * m[6],
        K5 * m[7],
        K1 * m[9],
    )


def at_second(al, b):
    b2 = b * b
    return (
        al[0] + b * al[1] + b2 * al[3] + (b2 * b) * al[4],
        al[2] + b2 * al[5] + b * al[6],
        al[3] + b * al[4],
        al[5],
    )


def from_z(h, lane, positive):
    inside = lane & 15
    if positive:
        return jnp.where(inside == 0, pltpu.roll(h, 113, 1), pltpu.roll(h, 1, 1))
    return jnp.where(inside == 15, pltpu.roll(h, 15, 1), pltpu.roll(h, 127, 1))


def from_y(h, lane, positive, swap):
    r = pltpu.roll(h, 16 if positive else 112, 1)
    return jnp.where(lane < 16 if positive else lane >= 112, swap(r), r)


def swap_halves(r):
    return pltpu.roll(r, 4, 0)


def swap_pairs(r):
    even = (lax.broadcasted_iota(jnp.int32, SHAPE, 0) & 1) == 0
    return jnp.where(even, pltpu.roll(r, 7, 0), pltpu.roll(r, 1, 0))


def add_raw(sums, b, acc):
    s0, sb, sc, s2, sb2, sc2, sbc = sums
    p, q, r, t = acc
    b2 = b * b
    return (
        s0 + p,
        sb + b * p,
        sc + q,
        s2 + b2 * p + r,
        sb2 + b * (b2 * p + r),
        sc2 + b2 * q + t,
        sbc + b * q,
    )


def sums_kernel(i_ref, n_ref, x_hbm, m_hbm, p_hbm, g_ref, h_hbm, s_hbm, x_ref, m_ref, p_ref, h_ref, s_ref, sem):
    def rows_of(j):
        rows = pl.ds(96 * j, 96)
        return pltpu.make_async_copy(x_hbm.at[rows], x_ref.at[rows], sem.at[2 + j])

    copies = [
        pltpu.make_async_copy(src, dst, sem.at[n]) for n, (src, dst) in enumerate(((m_hbm, m_ref), (p_hbm, p_ref)))
    ]
    for copy in copies:
        copy.start()
    for j in range(6):
        rows_of(j).start()
        rows_of(11 - j).start()
    a = first_speed(i_ref)
    aa = jnp.abs(a)
    sub, lane = iotas()
    even_row = (sub & 1) == 0
    zero = jnp.zeros(SHAPE, F)
    cs = [-2.75 + 0.5 * (4 * t + (sub >> 1)).astype(F) for t in range(3)]
    ecs = [jnp.exp(-c * c) for c in cs]
    for copy in copies:
        copy.wait()

    def back(h, t):
        if t == 0:
            return from_z(h, lane, False)
        if t == 2:
            return from_z(h, lane, True)
        return jnp.where(sub < 4, from_z(h, lane, False), from_z(h, lane, True))

    def build(near, far):
        def pair(ref, r):
            return jnp.where(
                even_row,
                jnp.broadcast_to(ref[r : r + 1, :].astype(F), SHAPE),
                jnp.broadcast_to(ref[r + 4 : r + 5, :].astype(F), SHAPE),
            )

        pore = pair(p_ref, near)
        al = field_polynomial(a, [pair(m_ref, 8 * m + near) for m in range(10)])

        def step(jj, carry):
            whole, down, up, minus, plus, double = carry
            rows_of(jj).wait()
            rows_of(11 - jj).wait()
            bm = 2.75 - 0.5 * jj.astype(F)
            ex = jnp.exp(-(a * a) - bm * bm)
            polys = [at_second(al, -bm), at_second(al, bm)]
            outs = [[zero] * 4, [zero] * 4]
            powers = [[[zero] * 5] * 3, [[zero] * 5] * 3]
            for t in range(3):
                c = cs[t]
                ca = jnp.abs(c)
                r = 1.0 / (aa + ca + (1.0 + bm))
                wa, wb, wc = aa * r, bm * r, ca * r
                rg = r * ex * ecs[t]
                for side in range(2):
                    p0, p1, p2, p3 = polys[side]
                    g = rg * (p0 + c * (p1 + c * (p2 + c * p3)))
                    base = pl.multiple_of(((11 - jj) if side else jj) * 24 + 8 * t, 8)
                    f1, f2 = x_ref[pl.ds(4 * base + near, 8, stride=4), :], x_ref[pl.ds(4 * base + far, 8, stride=4), :]
                    h = (wa * pore) * (
                        g + wa * f2 + wb * from_y(f1, lane, side == 1, swap_pairs) + wc * back(f1, t)
                    )
                    k = wa * r * f1
                    ks, hs = [k], [h]
                    for _ in range(4):
                        ks.append(c * ks[-1])
                    for _ in range(3):
                        hs.append(c * hs[-1])
                    powers[side] = powers[side][:t] + [ks] + powers[side][t + 1 :]
                    outs[side] = [p + q for p, q in zip(outs[side], hs)]
            sides = [down, up]
            for side in range(2):
                b = bm if side else -bm
                low, mid, high = powers[side]
                total = [low[n] + mid[n] + high[n] for n in range(4)]
                sides[side] = add_raw(sides[side], b, [bm * x for x in total])
                double = add_raw(double, b, total)
                minus = add_raw(minus, b, [low[n] + jnp.where(sub < 4, mid[n], 0.0) for n in range(1, 5)])
                plus = add_raw(plus, b, [high[n] + jnp.where(sub < 4, 0.0, mid[n]) for n in range(1, 5)])
                whole = add_raw(whole, b, outs[side])
            return whole, sides[0], sides[1], minus, plus, double

        groups = lax.fori_loop(0, 6, step, ((zero,) * 7,) * 6)
        scale = (1.0, 1.0, 1.0, -1.0, 1.0, aa)
        for n in range(6):
            for m in range(7):
                x = groups[n][m]
                x = x + pltpu.roll(x, 2, 0)
                x = (x + pltpu.roll(x, 4, 0)) * scale[n]
                g_ref[16 * n + 2 * m : 16 * n + 2 * m + 2, :] = x[0:2, :]
            g_ref[16 * n + 14 : 16 * n + 16, :] = jnp.zeros((2, 128), F)

    pl.when(i_ref[0] >= 8)(lambda: build(3, 2))
    pl.when(i_ref[0] < 8)(lambda: build(0, 1))

    @pl.when(early(n_ref))
    def _():
        local_sweeps(i_ref, x_ref, m_ref, p_ref, h_ref, s_ref)
        copies = [
            pltpu.make_async_copy(src, dst, sem.at[n]) for n, (src, dst) in enumerate(((h_ref, h_hbm), (s_ref, s_hbm)))
        ]
        for copy in copies:
            copy.start()
        for copy in copies:
            copy.wait()


def planes_kernel(i_ref, x_ref, m_ref, p_ref, o_ref):
    def take(near, far):
        o_ref[0:288, :] = x_ref[pl.ds(near, 288, stride=4), :]
        o_ref[288:576, :] = x_ref[pl.ds(far, 288, stride=4), :]
        o_ref[576:596, :] = m_ref[pl.ds(near, 20, stride=4), :]
        o_ref[596:598, :] = p_ref[pl.ds(near, 2, stride=4), :].astype(F)
        o_ref[598:600, :] = jnp.zeros((2, 128), F)

    pl.when(i_ref[0] >= 8)(lambda: take(3, 2))
    pl.when(i_ref[0] < 8)(lambda: take(0, 1))


def late_kernel(i_ref, n_ref, x_ref, m_ref, p_ref, h_hbm, s_hbm, h_ref, s_ref, sem):
    @pl.when(early(n_ref))
    def _():
        copies = [
            pltpu.make_async_copy(src, dst, sem.at[n]) for n, (src, dst) in enumerate(((h_hbm, h_ref), (s_hbm, s_ref)))
        ]
        for copy in copies:
            copy.start()
        for copy in copies:
            copy.wait()

    pl.when(jnp.logical_not(early(n_ref)))(lambda: local_sweeps(i_ref, x_ref, m_ref, p_ref, h_ref, s_ref))


def early(n_ref):
    return lax.rem(n_ref[0], 16) < 4


def local_sweeps(i_ref, x_ref, m_ref, p_ref, h_ref, s_ref):
    a = first_speed(i_ref)
    aa = jnp.abs(a)
    sub, lane = iotas()
    pore = p_ref[...].astype(F)
    al = field_polynomial(a, [m_ref[8 * m : 8 * m + 8, :] for m in range(10)])
    zero = jnp.zeros(SHAPE, F)

    def sweeps(shift, edge):
        inner = jnp.where((sub & 3) == edge, 0.0, 1.0)

        def step(jj, sums):
            bm = 2.75 - 0.5 * jj.astype(F)
            ex = jnp.exp(-(a * a) - bm * bm)
            accs = [[zero] * 4, [zero] * 4]
            polys = [at_second(al, -bm), at_second(al, bm)]
            rows = [jj * 12, (11 - jj) * 12]
            for kk in range(6):
                cm = magnitude(kk)
                c2 = cm * cm
                pr = pore * (1.0 / (aa + (1.0 + cm + bm)))
                pg = pr * (ex * math.exp(-c2))
                px, py, pz = aa * pr * inner, bm * pr, cm * pr
                for side in range(2):
                    p0, p1, p2, p3 = polys[side]
                    even, odd = p0 + c2 * p2, cm * (p1 + c2 * p3)
                    out = []
                    for up in range(2):
                        v = rows[side] + (11 - kk if up else kk)
                        g = pg * (even + odd if up else even - odd)
                        h = x_ref[pl.ds(pl.multiple_of(8 * v, 8), 8), :]
                        for _ in range(2):
                            h = (
                                g
                                + px * pltpu.roll(h, shift, 0)
                                + py * from_y(h, lane, side == 1, swap_halves)
                                + pz * from_z(h, lane, up == 1)
                            )
                        h_ref[v] = h
                        out.append(h)
                    s, d = out[1] + out[0], cm * (out[1] - out[0])
                    p, q, r, t = accs[side]
                    accs[side] = [p + s, q + d, r + c2 * s, t + c2 * d]
            sums = add_raw(sums, -bm, accs[0])
            return add_raw(sums, bm, accs[1])

        sums = lax.fori_loop(0, 6, step, (zero,) * 7)
        for n in range(7):
            s_ref[n] = sums[n]

    pl.when(i_ref[0] >= 8)(lambda: sweeps(1, 0))
    pl.when(i_ref[0] < 8)(lambda: sweeps(7, 3))


def merge_kernel(i_ref, g_ref, p_ref, s_ref, o_ref, e_ref):
    a = first_speed(i_ref)
    sub, lane = iotas()
    even_row = (sub & 1) == 0
    forward = i_ref[0] >= 8

    def row(ref, r):
        return jnp.broadcast_to(ref[r : r + 1, :].astype(F), SHAPE)

    def own(plus, minus):
        return jnp.where(
            even_row,
            jnp.where(forward, row(p_ref, plus), row(p_ref, minus)),
            jnp.where(forward, row(p_ref, plus + 4), row(p_ref, minus + 4)),
        )

    pore_0, pore_1 = own(0, 3), own(1, 2)
    for n in range(2):
        whole, down, up, minus, plus, double = [g_ref[16 * k + 8 * n : 16 * k + 8 * n + 8, :] for k in range(6)]
        e_ref[8 * n : 8 * n + 8, :] = pore_0 * (
            whole
            + from_y(pore_0 * down, lane, False, swap_pairs)
            + from_y(pore_0 * up, lane, True, swap_pairs)
            + from_z(pore_0 * minus, lane, False)
            + from_z(pore_0 * plus, lane, True)
        )
        e_ref[16 + 8 * n : 24 + 8 * n, :] = pore_0 * pore_1 * double
    place = sub & 3
    at_near = place == jnp.where(forward, 0, 3)
    at_far = place == jnp.where(forward, 1, 2)

    def spread(r):
        return jnp.where(sub < 4, row(e_ref, r), row(e_ref, r + 1))

    s0, sb, sc, s2, sb2, sc2, sbc = [
        s_ref[n] + jnp.where(at_near, spread(2 * n), jnp.where(at_far, spread(16 + 2 * n), 0.0))
        for n in range(7)
    ]
    a2 = a * a
    t4, t5 = (a2 - 1.5) * s0 + s2, (a2 - 2.5) * s0 + s2
    moments = (s0, a * s0, sb, sc, t4, a * t5, (a2 - 2.5) * sb + sb2, (a2 - 2.5) * sc + sc2, a * sb, sbc)
    for m in range(10):
        value = moments[m] * VOL
        for n in range(o_ref.shape[0]):
            o_ref[n, 8 * m : 8 * m + 8, :] = value


def total_kernel(g_ref, o_ref):
    total = (g_ref[0] + g_ref[1]) + (g_ref[2] + g_ref[3])
    for n in range(o_ref.shape[0]):
        o_ref[n] = total


def change_kernel(g_ref, m_ref, p_ref, o_ref, h_ref):
    total = (g_ref[0] + g_ref[1]) + (g_ref[2] + g_ref[3])
    h_ref[...] = total
    o_ref[0:80, :] = total - m_ref[...]
    o_ref[80:88, :] = p_ref[...].astype(F)


def halo_kernel(wanted, i_ref, n_ref, *refs):
    pl.when(early(n_ref) if wanted else jnp.logical_not(early(n_ref)))(lambda: add_halo(i_ref, *refs))


def add_halo(i_ref, g_ref, p_ref, h_ref, o_ref):
    a = first_speed(i_ref)
    aa = jnp.abs(a)
    sub, lane = iotas()
    even_row = (sub & 1) == 0

    def row(ref, r):
        return jnp.broadcast_to(ref[r : r + 1, :].astype(F), SHAPE)

    def pair(ref, r, s):
        return jnp.where(even_row, row(ref, r), row(ref, s))

    cs = [-2.75 + 0.5 * (4 * t + (sub >> 1)).astype(F) for t in range(3)]
    ecs = [jnp.exp(-c * c) for c in cs]
    pore_out = pair(g_ref, 596, 597)
    al = field_polynomial(a, [pair(g_ref, 576 + 2 * m, 577 + 2 * m) for m in range(10)])
    o_ref[...] = h_ref[...]

    def back(h, t):
        if t == 0:
            return from_z(h, lane, False)
        if t == 2:
            return from_z(h, lane, True)
        return jnp.where(sub < 4, from_z(h, lane, False), from_z(h, lane, True))

    def fix(at_0, at_1):
        pore_0, pore_1 = pair(p_ref, at_0, at_0 + 4), pair(p_ref, at_1, at_1 + 4)

        def step(jj, carry):
            bm = 2.75 - 0.5 * jj.astype(F)
            ex = jnp.exp(-(a * a) - bm * bm)
            polys = [at_second(al, -bm), at_second(al, bm)]
            for t in range(3):
                c = cs[t]
                ca = jnp.abs(c)
                r = 1.0 / (aa + ca + (1.0 + bm))
                wa, wb, wc = aa * r, bm * r, ca * r
                rg = r * ex * ecs[t]
                for side in range(2):
                    p0, p1, p2, p3 = polys[side]
                    g = rg * (p0 + c * (p1 + c * (p2 + c * p3)))
                    base = pl.multiple_of(((11 - jj) if side else jj) * 24 + 8 * t, 8)
                    near, far = g_ref[pl.ds(base, 8), :], g_ref[pl.ds(288 + base, 8), :]
                    outer = pore_out * (
                        g + wa * far + wb * from_y(near, lane, side == 1, swap_pairs) + wc * back(near, t)
                    )
                    first = pore_0 * wa * near
                    e0 = pore_0 * (
                        wa * outer + wb * from_y(first, lane, side == 1, swap_pairs) + wc * back(first, t)
                    )
                    e1 = pore_1 * wa * first
                    rows_0 = pl.ds(base * 4 + at_0, 8, stride=4)
                    rows_1 = pl.ds(base * 4 + at_1, 8, stride=4)
                    o_ref[rows_0, :] = o_ref[rows_0, :] + e0
                    o_ref[rows_1, :] = o_ref[rows_1, :] + e1
            return carry

        lax.fori_loop(0, 6, step, 0)

    pl.when(i_ref[0] >= 8)(lambda: fix(0, 1))
    pl.when(i_ref[0] < 8)(lambda: fix(3, 2))


def final_kernel(i_ref, n_ref, q_ref, e_ref, l_ref, c_ref, left_ref, right_ref, mh_ref, o_hbm, mo_ref, k_ref, o_ref, sem):
    a = first_speed(i_ref)
    sub, lane = iotas()
    pores = [left_ref[10], c_ref[10], right_ref[10]]
    low, high = (sub & 3) == 0, (sub & 3) == 3
    wrap_up, wrap_down = lane < 16, lane >= 112
    z_first, z_last = (lane & 15) == 0, (lane & 15) == 15

    def around(h):
        up, down = pltpu.roll(h, 16, 1), pltpu.roll(h, 112, 1)
        same = jnp.where(wrap_up, 0.0, up) + jnp.where(wrap_down, 0.0, down)
        other = jnp.where(wrap_up, up, jnp.where(wrap_down, down, 0.0))
        forth = pltpu.roll(jnp.where(z_last, down, h), 1, 1)
        back = pltpu.roll(jnp.where(z_first, up, h), 127, 1)
        return same + swap_halves(other) + (forth + back)

    for m in range(10):
        inv = jnp.broadcast_to(q_ref[m : m + 1, :], SHAPE)
        q = [p * inv for p in pores]
        change = [left_ref[m], c_ref[m], right_ref[m]]
        cor = [q[n] * change[n] for n in range(3)]
        for it in range(4):
            new = list(cor)
            for n in range(3):
                if it == 3 and n != 1:
                    continue
                below = pltpu.roll(cor[n], 1, 0)
                above = pltpu.roll(cor[n], 7, 0)
                if n > 0:
                    below = jnp.where(low, pltpu.roll(cor[n - 1], 5, 0), below)
                if n < 2:
                    above = jnp.where(high, pltpu.roll(cor[n + 1], 3, 0), above)
                new[n] = q[n] * (change[n] + (below + above + around(cor[n])))
            cor = new
        k_ref[m] = cor[1]
        mo_ref[m] = mh_ref[m] + cor[1]

    al = field_polynomial(a, [k_ref[m] for m in range(10)])
    pore = pores[1]

    def chunk(n, j):
        rows = pl.ds(j * 12, 12)
        return pltpu.make_async_copy(o_ref.at[rows], o_hbm.at[rows], sem.at[n])

    def lift(h_ref):
        lax.fori_loop(0, 6, functools.partial(step, h_ref), 0)

    def step(h_ref, jj, carry):
        bm = 2.75 - 0.5 * jj.astype(F)
        ex = pore * jnp.exp(-(a * a) - bm * bm)
        for side in range(2):
            p0, p1, p2, p3 = at_second(al, bm if side else -bm)
            j = 11 - jj if side else jj
            for kk in range(6):
                cm = magnitude(kk)
                c2 = cm * cm
                w = ex * math.exp(-c2)
                even, odd = w * (p0 + c2 * p2), w * (cm * (p1 + c2 * p3))
                for up in range(2):
                    v = j * 12 + (11 - kk if up else kk)
                    o_ref[v] = h_ref[v] + (even + odd if up else even - odd)
            chunk(6 * side + jj, j).start()
        return carry

    pl.when(early(n_ref))(lambda: lift(e_ref))
    pl.when(jnp.logical_not(early(n_ref)))(lambda: lift(l_ref))
    for jj in range(6):
        chunk(jj, jj).wait()
        chunk(6 + jj, 11 - jj).wait()


VM = pl.BlockSpec(memory_space=pltpu.VMEM)
SM = pl.BlockSpec(memory_space=pltpu.SMEM)
HBM = pl.BlockSpec(memory_space=pltpu.HBM)


def call(kernel, outs, args, cost, scratch=(), ins=None, out_specs=None, grant=4 << 20):
    shapes = [jax.ShapeDtypeStruct(s, F) for s in outs]
    out_specs = out_specs or [VM] * len(shapes)
    single = len(shapes) == 1
    return pl.pallas_call(
        kernel,
        out_shape=shapes[0] if single else shapes,
        in_specs=ins,
        out_specs=out_specs[0] if single else out_specs,
        scratch_shapes=list(scratch),
        compiler_params=pltpu.CompilerParams(vmem_limit_bytes=grant),
        cost_estimate=pl.CostEstimate(flops=cost, bytes_accessed=4 * cost, transcendentals=0),
    )(*args)


def to_registers(x):
    n = x.shape[0]
    return x.reshape(n, 4, 2, 128).transpose(0, 2, 1, 3).reshape(n, 8, 128)


def from_registers(x):
    n = x.shape[0]
    return x.reshape(n, 2, 4, 128).transpose(0, 2, 1, 3).reshape(n, 4, 256)


def groups_of(key):
    found = {}
    for v in range(16):
        found.setdefault(key(v), []).append(v)
    return list(found.values())


FAR = groups_of(lambda v: (v // 8, v % 2))
NEAR = groups_of(lambda v: (v % 8) // 2)


def upwind_pairs(space):
    return [
        (v * space + s, v * space + (s + (1 if v >= 8 else -1)) % space) for v in range(16) for s in range(space)
    ]


def body(distribution, moments_old, pore_mask, synthetic_rate):
    space = lax.axis_size("space")
    i = lax.axis_index("vel").astype(jnp.int32).reshape(1)
    n = lax.axis_index("space").astype(jnp.int32).reshape(1)
    x = to_registers(distribution)
    old = to_registers(moments_old)
    pore = to_registers(pore_mask[None])[0]
    shapes = [(144, 8, 128), (7, 8, 128)]
    flat = [x.reshape(1152, 128), old.reshape(80, 128), pore]
    packed, half, sums = call(
        sums_kernel,
        [(96, 128)] + shapes,
        [i, n] + flat,
        1 << 20,
        [
            pltpu.VMEM((1152, 128), F),
            pltpu.VMEM((80, 128), F),
            pltpu.VMEM((8, 128), jnp.int32),
            pltpu.VMEM((144, 8, 128), F),
            pltpu.VMEM((7, 8, 128), F),
            pltpu.SemaphoreType.DMA((14,)),
        ],
        [SM, SM, HBM, HBM, HBM],
        [VM, HBM, HBM],
        grant=60 << 20,
    )
    pairs = upwind_pairs(space)
    sums_in = lax.ppermute(packed, ("vel", "space"), pairs)
    planes = call(planes_kernel, [(600, 128)], [i] + flat, 1 << 16, ins=[SM, VM, VM, VM])
    planes_in = lax.ppermute(planes, ("vel", "space"), pairs)
    half, sums = call(
        late_kernel,
        shapes,
        [i, n] + flat + [half, sums],
        1 << 21,
        [pltpu.SemaphoreType.DMA((2,))],
        [SM, SM, VM, VM, VM, HBM, HBM],
    )
    copies = call(
        merge_kernel,
        [(4, 80, 128)],
        [i, sums_in, pore, sums],
        1 << 16,
        [pltpu.VMEM((32, 128), F)],
        ins=[SM, VM, VM, VM],
    )
    got = lax.all_to_all(copies, "vel", 0, 0, axis_index_groups=FAR, tiled=True)
    copies = call(total_kernel, [(4, 80, 128)], [got], 1 << 16, ins=[VM])
    got = lax.all_to_all(copies, "vel", 0, 0, axis_index_groups=NEAR, tiled=True)
    message, moments_half = call(
        change_kernel, [(88, 128), (80, 128)], [got, old.reshape(80, 128), pore], 1 << 16, ins=[VM] * 3
    )
    ring = [(s, (s + 1) % space) for s in range(space)]
    args = [i, n, planes_in, pore, half.reshape(1152, 128)]
    ins = [SM, SM, VM, VM, VM]
    left = lax.ppermute(message, "space", ring)
    whole_early = call(functools.partial(halo_kernel, True), [(1152, 128)], args, 1 << 16, ins=ins)
    right = lax.ppermute(message, "space", [(t, s) for s, t in ring])
    whole_late = call(functools.partial(halo_kernel, False), [(1152, 128)], args, 1 << 20, ins=ins)
    inverse = jnp.broadcast_to((1.0 / (synthetic_rate + 6.0))[:, None], (10, 128))
    out, moments_new = call(
        final_kernel,
        [(144, 8, 128), (10, 8, 128)],
        [
            i,
            n,
            inverse,
            whole_early.reshape(144, 8, 128),
            whole_late.reshape(144, 8, 128),
            message.reshape(11, 8, 128),
            left.reshape(11, 8, 128),
            right.reshape(11, 8, 128),
            moments_half.reshape(10, 8, 128),
        ],
        1 << 20,
        [pltpu.VMEM((10, 8, 128), F), pltpu.VMEM((144, 8, 128), F), pltpu.SemaphoreType.DMA((12,))],
        [SM, SM] + [VM] * 7,
        [HBM, VM],
    )
    return from_registers(out), from_registers(moments_new)


def solution(mesh):
    placed = (P("vel", "space", None), P(None, "space", None), P("space", None), P())
    return jax.shard_map(
        body,
        mesh=mesh,
        in_specs=placed,
        out_specs=(P("vel", "space", None), P(None, "space", None)),
        check_vma=False,
    )
```

```python
import functools
import math

import jax
import jax.numpy as jnp
from jax import lax
from jax.experimental import pallas as pl
from jax.experimental.pallas import tpu as pltpu
from jax.sharding import PartitionSpec as P


F = jnp.float32
SHAPE = (8, 128)
VOL = 216.0 / 2304 / math.pi**1.5
K1, K4, K5 = 2.0, 0.6667, 0.8


def magnitude(kk):
    return 2.75 - 0.5 * kk


def iotas():
    return lax.broadcasted_iota(jnp.int32, SHAPE, 0), lax.broadcasted_iota(jnp.int32, SHAPE, 1)


def first_speed(i_ref):
    return jnp.full(SHAPE, -3.0 + (i_ref[0].astype(F) + 0.5) * 0.375, F)


def field_polynomial(a, m):
    a2 = a * a
    u, w = a2 - 1.5, a2 - 2.5
    return (
        m[0] + K1 * (a * m[1]) + K4 * (u * m[4]) + K5 * (a * w * m[5]),
        K1 * m[2] + K5 * (w * m[6]) + K1 * (a * m[8]),
        K1 * m[3] + K5 * (w * m[7]),
        K4 * m[4] + K5 * (a * m[5]),
        K5 * m[6],
        K5 * m[7],
        K1 * m[9],
    )


def at_second(al, b):
    b2 = b * b
    return (
        al[0] + b * al[1] + b2 * al[3] + (b2 * b) * al[4],
        al[2] + b2 * al[5] + b * al[6],
        al[3] + b * al[4],
        al[5],
    )


def from_z(h, lane, positive):
    inside = lane & 15
    if positive:
        return jnp.where(inside == 0, pltpu.roll(h, 113, 1), pltpu.roll(h, 1, 1))
    return jnp.where(inside == 15, pltpu.roll(h, 15, 1), pltpu.roll(h, 127, 1))


def from_y(h, lane, positive, swap):
    r = pltpu.roll(h, 16 if positive else 112, 1)
    return jnp.where(lane < 16 if positive else lane >= 112, swap(r), r)


def swap_halves(r):
    return pltpu.roll(r, 4, 0)


def swap_pairs(r):
    even = (lax.broadcasted_iota(jnp.int32, SHAPE, 0) & 1) == 0
    return jnp.where(even, pltpu.roll(r, 7, 0), pltpu.roll(r, 1, 0))


def add_raw(sums, b, acc):
    s0, sb, sc, s2, sb2, sc2, sbc = sums
    p, q, r, t = acc
    b2 = b * b
    return (
        s0 + p,
        sb + b * p,
        sc + q,
        s2 + b2 * p + r,
        sb2 + b * (b2 * p + r),
        sc2 + b2 * q + t,
        sbc + b * q,
    )


def sums_kernel(i_ref, n_ref, x_hbm, m_hbm, p_hbm, g_ref, h_hbm, s_hbm, x_ref, m_ref, p_ref, h_ref, s_ref, sem):
    def rows_of(j):
        rows = pl.ds(96 * j, 96)
        return pltpu.make_async_copy(x_hbm.at[rows], x_ref.at[rows], sem.at[2 + j])

    copies = [
        pltpu.make_async_copy(src, dst, sem.at[n]) for n, (src, dst) in enumerate(((m_hbm, m_ref), (p_hbm, p_ref)))
    ]
    for copy in copies:
        copy.start()
    for j in range(6):
        rows_of(j).start()
        rows_of(11 - j).start()
    a = first_speed(i_ref)
    aa = jnp.abs(a)
    sub, lane = iotas()
    even_row = (sub & 1) == 0
    zero = jnp.zeros(SHAPE, F)
    cs = [-2.75 + 0.5 * (4 * t + (sub >> 1)).astype(F) for t in range(3)]
    ecs = [jnp.exp(-c * c) for c in cs]
    for copy in copies:
        copy.wait()

    def back(h, t):
        if t == 0:
            return from_z(h, lane, False)
        if t == 2:
            return from_z(h, lane, True)
        return jnp.where(sub < 4, from_z(h, lane, False), from_z(h, lane, True))

    def build(near, far):
        def pair(ref, r):
            return jnp.where(
                even_row,
                jnp.broadcast_to(ref[r : r + 1, :].astype(F), SHAPE),
                jnp.broadcast_to(ref[r + 4 : r + 5, :].astype(F), SHAPE),
            )

        pore = pair(p_ref, near)
        al = field_polynomial(a, [pair(m_ref, 8 * m + near) for m in range(10)])

        def step(jj, carry):
            whole, down, up, minus, plus, double = carry
            rows_of(jj).wait()
            rows_of(11 - jj).wait()
            bm = 2.75 - 0.5 * jj.astype(F)
            ex = jnp.exp(-(a * a) - bm * bm)
            polys = [at_second(al, -bm), at_second(al, bm)]
            outs = [[zero] * 4, [zero] * 4]
            powers = [[[zero] * 5] * 3, [[zero] * 5] * 3]
            for t in range(3):
                c = cs[t]
                ca = jnp.abs(c)
                r = 1.0 / (aa + ca + (1.0 + bm))
                wa, wb, wc = aa * r, bm * r, ca * r
                rg = r * ex * ecs[t]
                for side in range(2):
                    p0, p1, p2, p3 = polys[side]
                    g = rg * (p0 + c * (p1 + c * (p2 + c * p3)))
                    base = pl.multiple_of(((11 - jj) if side else jj) * 24 + 8 * t, 8)
                    f1, f2 = x_ref[pl.ds(4 * base + near, 8, stride=4), :], x_ref[pl.ds(4 * base + far, 8, stride=4), :]
                    h = (wa * pore) * (
                        g + wa * f2 + wb * from_y(f1, lane, side == 1, swap_pairs) + wc * back(f1, t)
                    )
                    k = wa * r * f1
                    ks, hs = [k], [h]
                    for _ in range(4):
                        ks.append(c * ks[-1])
                    for _ in range(3):
                        hs.append(c * hs[-1])
                    powers[side] = powers[side][:t] + [ks] + powers[side][t + 1 :]
                    outs[side] = [p + q for p, q in zip(outs[side], hs)]
            sides = [down, up]
            for side in range(2):
                b = bm if side else -bm
                low, mid, high = powers[side]
                total = [low[n] + mid[n] + high[n] for n in range(4)]
                sides[side] = add_raw(sides[side], b, [bm * x for x in total])
                double = add_raw(double, b, total)
                minus = add_raw(minus, b, [low[n] + jnp.where(sub < 4, mid[n], 0.0) for n in range(1, 5)])
                plus = add_raw(plus, b, [high[n] + jnp.where(sub < 4, 0.0, mid[n]) for n in range(1, 5)])
                whole = add_raw(whole, b, outs[side])
            return whole, sides[0], sides[1], minus, plus, double

        groups = lax.fori_loop(0, 6, step, ((zero,) * 7,) * 6)
        scale = (1.0, 1.0, 1.0, -1.0, 1.0, aa)
        for n in range(6):
            for m in range(7):
                x = groups[n][m]
                x = x + pltpu.roll(x, 2, 0)
                x = (x + pltpu.roll(x, 4, 0)) * scale[n]
                g_ref[16 * n + 2 * m : 16 * n + 2 * m + 2, :] = x[0:2, :]
            g_ref[16 * n + 14 : 16 * n + 16, :] = jnp.zeros((2, 128), F)

    pl.when(i_ref[0] >= 8)(lambda: build(3, 2))
    pl.when(i_ref[0] < 8)(lambda: build(0, 1))

    @pl.when(early(n_ref))
    def _():
        local_sweeps(i_ref, x_ref, m_ref, p_ref, h_ref, s_ref)
        copies = [
            pltpu.make_async_copy(src, dst, sem.at[n]) for n, (src, dst) in enumerate(((h_ref, h_hbm), (s_ref, s_hbm)))
        ]
        for copy in copies:
            copy.start()
        for copy in copies:
            copy.wait()


def planes_kernel(i_ref, x_ref, m_ref, p_ref, o_ref):
    def take(near, far):
        o_ref[0:288, :] = x_ref[pl.ds(near, 288, stride=4), :]
        o_ref[288:576, :] = x_ref[pl.ds(far, 288, stride=4), :]
        o_ref[576:596, :] = m_ref[pl.ds(near, 20, stride=4), :]
        o_ref[596:598, :] = p_ref[pl.ds(near, 2, stride=4), :].astype(F)
        o_ref[598:600, :] = jnp.zeros((2, 128), F)

    pl.when(i_ref[0] >= 8)(lambda: take(3, 2))
    pl.when(i_ref[0] < 8)(lambda: take(0, 1))


def late_kernel(i_ref, n_ref, x_ref, m_ref, p_ref, h_hbm, s_hbm, h_ref, s_ref, sem):
    @pl.when(early(n_ref))
    def _():
        copies = [
            pltpu.make_async_copy(src, dst, sem.at[n]) for n, (src, dst) in enumerate(((h_hbm, h_ref), (s_hbm, s_ref)))
        ]
        for copy in copies:
            copy.start()
        for copy in copies:
            copy.wait()

    pl.when(jnp.logical_not(early(n_ref)))(lambda: local_sweeps(i_ref, x_ref, m_ref, p_ref, h_ref, s_ref))


def early(n_ref):
    return lax.rem(n_ref[0], 16) < 4


def local_sweeps(i_ref, x_ref, m_ref, p_ref, h_ref, s_ref):
    a = first_speed(i_ref)
    aa = jnp.abs(a)
    sub, lane = iotas()
    pore = p_ref[...].astype(F)
    al = field_polynomial(a, [m_ref[8 * m : 8 * m + 8, :] for m in range(10)])
    zero = jnp.zeros(SHAPE, F)

    def sweeps(shift, edge):
        inner = jnp.where((sub & 3) == edge, 0.0, 1.0)

        def step(jj, sums):
            bm = 2.75 - 0.5 * jj.astype(F)
            ex = jnp.exp(-(a * a) - bm * bm)
            accs = [[zero] * 4, [zero] * 4]
            polys = [at_second(al, -bm), at_second(al, bm)]
            rows = [jj * 12, (11 - jj) * 12]
            for kk in range(6):
                cm = magnitude(kk)
                c2 = cm * cm
                pr = pore * (1.0 / (aa + (1.0 + cm + bm)))
                pg = pr * (ex * math.exp(-c2))
                px, py, pz = aa * pr * inner, bm * pr, cm * pr
                for side in range(2):
                    p0, p1, p2, p3 = polys[side]
                    even, odd = p0 + c2 * p2, cm * (p1 + c2 * p3)
                    out = []
                    for up in range(2):
                        v = rows[side] + (11 - kk if up else kk)
                        g = pg * (even + odd if up else even - odd)
                        h = x_ref[pl.ds(pl.multiple_of(8 * v, 8), 8), :]
                        for _ in range(2):
                            h = (
                                g
                                + px * pltpu.roll(h, shift, 0)
                                + py * from_y(h, lane, side == 1, swap_halves)
                                + pz * from_z(h, lane, up == 1)
                            )
                        h_ref[v] = h
                        out.append(h)
                    s, d = out[1] + out[0], cm * (out[1] - out[0])
                    p, q, r, t = accs[side]
                    accs[side] = [p + s, q + d, r + c2 * s, t + c2 * d]
            sums = add_raw(sums, -bm, accs[0])
            return add_raw(sums, bm, accs[1])

        sums = lax.fori_loop(0, 6, step, (zero,) * 7)
        for n in range(7):
            s_ref[n] = sums[n]

    pl.when(i_ref[0] >= 8)(lambda: sweeps(1, 0))
    pl.when(i_ref[0] < 8)(lambda: sweeps(7, 3))


def merge_kernel(i_ref, g_ref, p_ref, s_ref, o_ref, e_ref):
    a = first_speed(i_ref)
    sub, lane = iotas()
    even_row = (sub & 1) == 0
    forward = i_ref[0] >= 8

    def row(ref, r):
        return jnp.broadcast_to(ref[r : r + 1, :].astype(F), SHAPE)

    def own(plus, minus):
        return jnp.where(
            even_row,
            jnp.where(forward, row(p_ref, plus), row(p_ref, minus)),
            jnp.where(forward, row(p_ref, plus + 4), row(p_ref, minus + 4)),
        )

    pore_0, pore_1 = own(0, 3), own(1, 2)
    for n in range(2):
        whole, down, up, minus, plus, double = [g_ref[16 * k + 8 * n : 16 * k + 8 * n + 8, :] for k in range(6)]
        e_ref[8 * n : 8 * n + 8, :] = pore_0 * (
            whole
            + from_y(pore_0 * down, lane, False, swap_pairs)
            + from_y(pore_0 * up, lane, True, swap_pairs)
            + from_z(pore_0 * minus, lane, False)
            + from_z(pore_0 * plus, lane, True)
        )
        e_ref[16 + 8 * n : 24 + 8 * n, :] = pore_0 * pore_1 * double
    place = sub & 3
    at_near = place == jnp.where(forward, 0, 3)
    at_far = place == jnp.where(forward, 1, 2)

    def spread(r):
        return jnp.where(sub < 4, row(e_ref, r), row(e_ref, r + 1))

    s0, sb, sc, s2, sb2, sc2, sbc = [
        s_ref[n] + jnp.where(at_near, spread(2 * n), jnp.where(at_far, spread(16 + 2 * n), 0.0))
        for n in range(7)
    ]
    a2 = a * a
    t4, t5 = (a2 - 1.5) * s0 + s2, (a2 - 2.5) * s0 + s2
    moments = (s0, a * s0, sb, sc, t4, a * t5, (a2 - 2.5) * sb + sb2, (a2 - 2.5) * sc + sc2, a * sb, sbc)
    for m in range(10):
        value = moments[m] * VOL
        for n in range(o_ref.shape[0]):
            o_ref[n, 8 * m : 8 * m + 8, :] = value


def total_kernel(g_ref, o_ref):
    total = (g_ref[0] + g_ref[1]) + (g_ref[2] + g_ref[3])
    for n in range(o_ref.shape[0]):
        o_ref[n] = total


def change_kernel(g_ref, m_ref, p_ref, o_ref, h_ref):
    total = (g_ref[0] + g_ref[1]) + (g_ref[2] + g_ref[3])
    h_ref[...] = total
    o_ref[0:80, :] = total - m_ref[...]
    o_ref[80:88, :] = p_ref[...].astype(F)


def halo_kernel(wanted, i_ref, n_ref, *refs):
    pl.when(early(n_ref) if wanted else jnp.logical_not(early(n_ref)))(lambda: add_halo(i_ref, *refs))


def add_halo(i_ref, g_ref, p_ref, h_ref, o_ref):
    a = first_speed(i_ref)
    aa = jnp.abs(a)
    sub, lane = iotas()
    even_row = (sub & 1) == 0

    def row(ref, r):
        return jnp.broadcast_to(ref[r : r + 1, :].astype(F), SHAPE)

    def pair(ref, r, s):
        return jnp.where(even_row, row(ref, r), row(ref, s))

    cs = [-2.75 + 0.5 * (4 * t + (sub >> 1)).astype(F) for t in range(3)]
    ecs = [jnp.exp(-c * c) for c in cs]
    pore_out = pair(g_ref, 596, 597)
    al = field_polynomial(a, [pair(g_ref, 576 + 2 * m, 577 + 2 * m) for m in range(10)])
    o_ref[...] = h_ref[...]

    def back(h, t):
        if t == 0:
            return from_z(h, lane, False)
        if t == 2:
            return from_z(h, lane, True)
        return jnp.where(sub < 4, from_z(h, lane, False), from_z(h, lane, True))

    def fix(at_0, at_1):
        pore_0, pore_1 = pair(p_ref, at_0, at_0 + 4), pair(p_ref, at_1, at_1 + 4)

        def step(jj, carry):
            bm = 2.75 - 0.5 * jj.astype(F)
            ex = jnp.exp(-(a * a) - bm * bm)
            polys = [at_second(al, -bm), at_second(al, bm)]
            for t in range(3):
                c = cs[t]
                ca = jnp.abs(c)
                r = 1.0 / (aa + ca + (1.0 + bm))
                wa, wb, wc = aa * r, bm * r, ca * r
                rg = r * ex * ecs[t]
                for side in range(2):
                    p0, p1, p2, p3 = polys[side]
                    g = rg * (p0 + c * (p1 + c * (p2 + c * p3)))
                    base = pl.multiple_of(((11 - jj) if side else jj) * 24 + 8 * t, 8)
                    near, far = g_ref[pl.ds(base, 8), :], g_ref[pl.ds(288 + base, 8), :]
                    outer = pore_out * (
                        g + wa * far + wb * from_y(near, lane, side == 1, swap_pairs) + wc * back(near, t)
                    )
                    first = pore_0 * wa * near
                    e0 = pore_0 * (
                        wa * outer + wb * from_y(first, lane, side == 1, swap_pairs) + wc * back(first, t)
                    )
                    e1 = pore_1 * wa * first
                    rows_0 = pl.ds(base * 4 + at_0, 8, stride=4)
                    rows_1 = pl.ds(base * 4 + at_1, 8, stride=4)
                    o_ref[rows_0, :] = o_ref[rows_0, :] + e0
                    o_ref[rows_1, :] = o_ref[rows_1, :] + e1
            return carry

        lax.fori_loop(0, 6, step, 0)

    pl.when(i_ref[0] >= 8)(lambda: fix(0, 1))
    pl.when(i_ref[0] < 8)(lambda: fix(3, 2))


def final_kernel(i_ref, n_ref, q_ref, e_ref, l_ref, c_ref, left_ref, right_ref, mh_ref, o_hbm, mo_ref, k_ref, o_ref, sem):
    a = first_speed(i_ref)
    sub, lane = iotas()
    pores = [left_ref[10], c_ref[10], right_ref[10]]
    low, high = (sub & 3) == 0, (sub & 3) == 3
    wrap_up, wrap_down = lane < 16, lane >= 112
    z_first, z_last = (lane & 15) == 0, (lane & 15) == 15

    def around(h):
        up, down = pltpu.roll(h, 16, 1), pltpu.roll(h, 112, 1)
        same = jnp.where(wrap_up, 0.0, up) + jnp.where(wrap_down, 0.0, down)
        other = jnp.where(wrap_up, up, jnp.where(wrap_down, down, 0.0))
        forth = pltpu.roll(jnp.where(z_last, down, h), 1, 1)
        back = pltpu.roll(jnp.where(z_first, up, h), 127, 1)
        return same + swap_halves(other) + (forth + back)

    for m in range(10):
        inv = jnp.broadcast_to(q_ref[m : m + 1, :], SHAPE)
        q = [p * inv for p in pores]
        change = [left_ref[m], c_ref[m], right_ref[m]]
        cor = [q[n] * change[n] for n in range(3)]
        for it in range(4):
            new = list(cor)
            for n in range(3):
                if it == 3 and n != 1:
                    continue
                below = pltpu.roll(cor[n], 1, 0)
                above = pltpu.roll(cor[n], 7, 0)
                if n > 0:
                    below = jnp.where(low, pltpu.roll(cor[n - 1], 5, 0), below)
                if n < 2:
                    above = jnp.where(high, pltpu.roll(cor[n + 1], 3, 0), above)
                new[n] = q[n] * (change[n] + (below + above + around(cor[n])))
            cor = new
        k_ref[m] = cor[1]
        mo_ref[m] = mh_ref[m] + cor[1]

    al = field_polynomial(a, [k_ref[m] for m in range(10)])
    pore = pores[1]

    def chunk(n, j):
        rows = pl.ds(j * 12, 12)
        return pltpu.make_async_copy(o_ref.at[rows], o_hbm.at[rows], sem.at[n])

    def lift(h_ref):
        lax.fori_loop(0, 6, functools.partial(step, h_ref), 0)

    def step(h_ref, jj, carry):
        bm = 2.75 - 0.5 * jj.astype(F)
        ex = pore * jnp.exp(-(a * a) - bm * bm)
        for side in range(2):
            p0, p1, p2, p3 = at_second(al, bm if side else -bm)
            j = 11 - jj if side else jj
            for kk in range(6):
                cm = magnitude(kk)
                c2 = cm * cm
                w = ex * math.exp(-c2)
                even, odd = w * (p0 + c2 * p2), w * (cm * (p1 + c2 * p3))
                for up in range(2):
                    v = j * 12 + (11 - kk if up else kk)
                    o_ref[v] = h_ref[v] + (even + odd if up else even - odd)
            chunk(6 * side + jj, j).start()
        return carry

    pl.when(early(n_ref))(lambda: lift(e_ref))
    pl.when(jnp.logical_not(early(n_ref)))(lambda: lift(l_ref))
    for jj in range(6):
        chunk(jj, jj).wait()
        chunk(6 + jj, 11 - jj).wait()


VM = pl.BlockSpec(memory_space=pltpu.VMEM)
SM = pl.BlockSpec(memory_space=pltpu.SMEM)
HBM = pl.BlockSpec(memory_space=pltpu.HBM)


def call(kernel, outs, args, cost, scratch=(), ins=None, out_specs=None, grant=4 << 20):
    shapes = [jax.ShapeDtypeStruct(s, F) for s in outs]
    out_specs = out_specs or [VM] * len(shapes)
    single = len(shapes) == 1
    return pl.pallas_call(
        kernel,
        out_shape=shapes[0] if single else shapes,
        in_specs=ins,
        out_specs=out_specs[0] if single else out_specs,
        scratch_shapes=list(scratch),
        compiler_params=pltpu.CompilerParams(vmem_limit_bytes=grant),
        cost_estimate=pl.CostEstimate(flops=cost, bytes_accessed=4 * cost, transcendentals=0),
    )(*args)


def to_registers(x):
    n = x.shape[0]
    return x.reshape(n, 4, 2, 128).transpose(0, 2, 1, 3).reshape(n, 8, 128)


def from_registers(x):
    n = x.shape[0]
    return x.reshape(n, 2, 4, 128).transpose(0, 2, 1, 3).reshape(n, 4, 256)


def stage_groups(space, odd):
    found = {}
    for v in range(16):
        for s in range(space):
            far = s % 2 == odd
            key = (v // 8, v % 2) if far else (v % 8 // 2, 2)
            found.setdefault((key, s), []).append(v * space + s)
    return list(found.values())


def upwind_pairs(space):
    return [
        (v * space + s, v * space + (s + (1 if v >= 8 else -1)) % space) for v in range(16) for s in range(space)
    ]


def body(distribution, moments_old, pore_mask, synthetic_rate):
    space = lax.axis_size("space")
    i = lax.axis_index("vel").astype(jnp.int32).reshape(1)
    n = lax.axis_index("space").astype(jnp.int32).reshape(1)
    x = to_registers(distribution)
    old = to_registers(moments_old)
    pore = to_registers(pore_mask[None])[0]
    shapes = [(144, 8, 128), (7, 8, 128)]
    flat = [x.reshape(1152, 128), old.reshape(80, 128), pore]
    packed, half, sums = call(
        sums_kernel,
        [(96, 128)] + shapes,
        [i, n] + flat,
        1 << 20,
        [
            pltpu.VMEM((1152, 128), F),
            pltpu.VMEM((80, 128), F),
            pltpu.VMEM((8, 128), jnp.int32),
            pltpu.VMEM((144, 8, 128), F),
            pltpu.VMEM((7, 8, 128), F),
            pltpu.SemaphoreType.DMA((14,)),
        ],
        [SM, SM, HBM, HBM, HBM],
        [VM, HBM, HBM],
        grant=60 << 20,
    )
    pairs = upwind_pairs(space)
    sums_in = lax.ppermute(packed, ("vel", "space"), pairs)
    planes = call(planes_kernel, [(600, 128)], [i] + flat, 1 << 16, ins=[SM, VM, VM, VM])
    planes_in = lax.ppermute(planes, ("vel", "space"), pairs)
    half, sums = call(
        late_kernel,
        shapes,
        [i, n] + flat + [half, sums],
        1 << 21,
        [pltpu.SemaphoreType.DMA((2,))],
        [SM, SM, VM, VM, VM, HBM, HBM],
    )
    copies = call(
        merge_kernel,
        [(4, 80, 128)],
        [i, sums_in, pore, sums],
        1 << 16,
        [pltpu.VMEM((32, 128), F)],
        ins=[SM, VM, VM, VM],
    )
    got = lax.all_to_all(copies, ("vel", "space"), 0, 0, axis_index_groups=stage_groups(space, 0), tiled=True)
    copies = call(total_kernel, [(4, 80, 128)], [got], 1 << 16, ins=[VM])
    got = lax.all_to_all(copies, ("vel", "space"), 0, 0, axis_index_groups=stage_groups(space, 1), tiled=True)
    message, moments_half = call(
        change_kernel, [(88, 128), (80, 128)], [got, old.reshape(80, 128), pore], 1 << 16, ins=[VM] * 3
    )
    ring = [(s, (s + 1) % space) for s in range(space)]
    args = [i, n, planes_in, pore, half.reshape(1152, 128)]
    ins = [SM, SM, VM, VM, VM]
    left = lax.ppermute(message, "space", ring)
    whole_early = call(functools.partial(halo_kernel, True), [(1152, 128)], args, 1 << 16, ins=ins)
    right = lax.ppermute(message, "space", [(t, s) for s, t in ring])
    whole_late = call(functools.partial(halo_kernel, False), [(1152, 128)], args, 1 << 20, ins=ins)
    inverse = jnp.broadcast_to((1.0 / (synthetic_rate + 6.0))[:, None], (10, 128))
    out, moments_new = call(
        final_kernel,
        [(144, 8, 128), (10, 8, 128)],
        [
            i,
            n,
            inverse,
            whole_early.reshape(144, 8, 128),
            whole_late.reshape(144, 8, 128),
            message.reshape(11, 8, 128),
            left.reshape(11, 8, 128),
            right.reshape(11, 8, 128),
            moments_half.reshape(10, 8, 128),
        ],
        1 << 20,
        [pltpu.VMEM((10, 8, 128), F), pltpu.VMEM((144, 8, 128), F), pltpu.SemaphoreType.DMA((12,))],
        [SM, SM] + [VM] * 7,
        [HBM, VM],
    )
    return from_registers(out), from_registers(moments_new)


def solution(mesh):
    placed = (P("vel", "space", None), P(None, "space", None), P("space", None), P())
    return jax.shard_map(
        body,
        mesh=mesh,
        in_specs=placed,
        out_specs=(P("vel", "space", None), P(None, "space", None)),
        check_vma=False,
    )
```

```python
import functools
import math

import jax
import jax.numpy as jnp
from jax import lax
from jax.experimental import pallas as pl
from jax.experimental.pallas import tpu as pltpu
from jax.sharding import PartitionSpec as P


F = jnp.float32
SHAPE = (8, 128)
VOL = 216.0 / 2304 / math.pi**1.5
K1, K4, K5 = 2.0, 0.6667, 0.8


def magnitude(kk):
    return 2.75 - 0.5 * kk


def iotas():
    return lax.broadcasted_iota(jnp.int32, SHAPE, 0), lax.broadcasted_iota(jnp.int32, SHAPE, 1)


def first_speed(i_ref):
    return jnp.full(SHAPE, -3.0 + (i_ref[0].astype(F) + 0.5) * 0.375, F)


def field_polynomial(a, m):
    a2 = a * a
    u, w = a2 - 1.5, a2 - 2.5
    return (
        m[0] + K1 * (a * m[1]) + K4 * (u * m[4]) + K5 * (a * w * m[5]),
        K1 * m[2] + K5 * (w * m[6]) + K1 * (a * m[8]),
        K1 * m[3] + K5 * (w * m[7]),
        K4 * m[4] + K5 * (a * m[5]),
        K5 * m[6],
        K5 * m[7],
        K1 * m[9],
    )


def at_second(al, b):
    b2 = b * b
    return (
        al[0] + b * al[1] + b2 * al[3] + (b2 * b) * al[4],
        al[2] + b2 * al[5] + b * al[6],
        al[3] + b * al[4],
        al[5],
    )


def from_z(h, lane, positive):
    inside = lane & 15
    if positive:
        return jnp.where(inside == 0, pltpu.roll(h, 113, 1), pltpu.roll(h, 1, 1))
    return jnp.where(inside == 15, pltpu.roll(h, 15, 1), pltpu.roll(h, 127, 1))


def from_y(h, lane, positive, swap):
    r = pltpu.roll(h, 16 if positive else 112, 1)
    return jnp.where(lane < 16 if positive else lane >= 112, swap(r), r)


def swap_halves(r):
    return pltpu.roll(r, 4, 0)


def swap_pairs(r):
    even = (lax.broadcasted_iota(jnp.int32, SHAPE, 0) & 1) == 0
    return jnp.where(even, pltpu.roll(r, 7, 0), pltpu.roll(r, 1, 0))


def add_raw(sums, b, acc):
    s0, sb, sc, s2, sb2, sc2, sbc = sums
    p, q, r, t = acc
    b2 = b * b
    return (
        s0 + p,
        sb + b * p,
        sc + q,
        s2 + b2 * p + r,
        sb2 + b * (b2 * p + r),
        sc2 + b2 * q + t,
        sbc + b * q,
    )


def sums_kernel(i_ref, n_ref, x_hbm, m_hbm, p_hbm, g_ref, h_hbm, s_hbm, x_ref, m_ref, p_ref, h_ref, s_ref, w_ref, sem):
    def rows_of(j):
        rows = pl.ds(96 * j, 96)
        return pltpu.make_async_copy(x_hbm.at[rows], x_ref.at[rows], sem.at[2 + j])

    copies = [
        pltpu.make_async_copy(src, dst, sem.at[n]) for n, (src, dst) in enumerate(((m_hbm, m_ref), (p_hbm, p_ref)))
    ]
    for copy in copies:
        copy.start()
    for j in range(6):
        rows_of(j).start()
        rows_of(11 - j).start()
    a = first_speed(i_ref)
    aa = jnp.abs(a)
    sub, lane = iotas()
    even_row = (sub & 1) == 0
    zero = jnp.zeros(SHAPE, F)
    cs = [-2.75 + 0.5 * (4 * t + (sub >> 1)).astype(F) for t in range(3)]
    ecs = [jnp.exp(-c * c - a * a) for c in cs]
    top, first = sub < 4, (sub & 2) == 0
    for jj in range(6):
        bm = magnitude(jj)
        for t in range(3):
            ca = jnp.abs(cs[t])
            r = 1.0 / (aa + ca + (1.0 + bm))
            for n, x in enumerate((aa * r, bm * r, ca * r, (math.exp(-bm * bm) * ecs[t]) * r, aa * r * r)):
                w_ref[(3 * jj + t) * 5 + n] = x
    for copy in copies:
        copy.wait()

    def back(h, t):
        if t == 0:
            return from_z(h, lane, False)
        if t == 2:
            return from_z(h, lane, True)
        return jnp.where(sub < 4, from_z(h, lane, False), from_z(h, lane, True))

    def build(near, far):
        def pair(ref, r):
            return jnp.where(
                even_row,
                jnp.broadcast_to(ref[r : r + 1, :].astype(F), SHAPE),
                jnp.broadcast_to(ref[r + 4 : r + 5, :].astype(F), SHAPE),
            )

        pore = pair(p_ref, near)
        al = field_polynomial(a, [pair(m_ref, 8 * m + near) for m in range(10)])

        def packed(x):
            y = [
                jnp.where(top, x[n], x[n + 2]) + pltpu.roll(jnp.where(top, x[n + 2], x[n]), 4, 0) for n in range(2)
            ]
            return jnp.where(first, y[0], y[1]) + jnp.where(first, pltpu.roll(y[0], 6, 0), pltpu.roll(y[1], 2, 0))

        def step(jj, carry):
            below, above, minus, plus, whole = carry
            rows_of(jj).wait()
            rows_of(11 - jj).wait()
            bm = 2.75 - 0.5 * jj.astype(F)
            polys = [at_second(al, -bm), at_second(al, bm)]
            outs = [[zero] * 4, [zero] * 4]
            powers = [[], []]
            for t in range(3):
                c = cs[t]
                wa, wb, wc, rg, wr = [w_ref[(3 * jj + t) * 5 + n] for n in range(5)]
                for side in range(2):
                    p0, p1, p2, p3 = polys[side]
                    g = rg * (p0 + c * (p1 + c * (p2 + c * p3)))
                    base = pl.multiple_of(((11 - jj) if side else jj) * 24 + 8 * t, 8)
                    f1, f2 = x_ref[pl.ds(4 * base + near, 8, stride=4), :], x_ref[pl.ds(4 * base + far, 8, stride=4), :]
                    h = (wa * pore) * (
                        g + wa * f2 + wb * from_y(f1, lane, side == 1, swap_pairs) + wc * back(f1, t)
                    )
                    ks, hs = [wr * f1], [h]
                    for _ in range(4):
                        ks.append(c * ks[-1])
                    for _ in range(3):
                        hs.append(c * hs[-1])
                    powers[side].append(ks)
                    outs[side] = [p + q for p, q in zip(outs[side], hs)]
            b2 = bm * bm
            b3, b4 = b2 * bm, b2 * b2
            sides = [below, above]
            parts = []
            for side in range(2):
                low, mid, high = powers[side]
                total = packed([low[n] + mid[n] + high[n] for n in range(4)])
                parts.append(
                    (
                        packed([low[n] + jnp.where(sub < 4, mid[n], 0.0) for n in range(1, 5)]),
                        packed([high[n] + jnp.where(sub < 4, 0.0, mid[n]) for n in range(1, 5)]),
                        packed(outs[side]),
                    )
                )
                sides[side] = [x + y * total for x, y in zip(sides[side], (1.0, bm, b2, b3, b4))]

            def both(acc, n):
                even, odd = parts[1][n] + parts[0][n], parts[1][n] - parts[0][n]
                return [acc[0] + even, acc[1] + bm * odd, acc[2] + b2 * even, acc[3] + b3 * odd]

            return sides[0], sides[1], both(minus, 0), both(plus, 1), both(whole, 2)

        below, above, minus, plus, whole = lax.fori_loop(
            0, 6, step, ([zero] * 5, [zero] * 5, [zero] * 4, [zero] * 4, [zero] * 4)
        )
        signs = (1.0, -1.0, 1.0, -1.0)
        groups = (
            whole,
            [signs[n] * below[n + 1] for n in range(4)],
            above[1:],
            [-x for x in minus],
            plus,
            [aa * (above[n] + signs[n] * below[n]) for n in range(4)],
        )
        for n in range(6):
            t0, t1, t2, t3 = groups[n]
            g_ref[16 * n : 16 * n + 4, :] = t0[0:4, :]
            g_ref[16 * n + 4 : 16 * n + 8, :] = t1[0:4, :]
            g_ref[16 * n + 8 : 16 * n + 12, :] = (t2 + pltpu.roll(t0, 4, 0))[0:4, :]
            g_ref[16 * n + 12 : 16 * n + 14, :] = (t3 + pltpu.roll(t1, 4, 0))[0:2, :]
            g_ref[16 * n + 14 : 16 * n + 16, :] = jnp.zeros((2, 128), F)

    pl.when(i_ref[0] >= 8)(lambda: build(3, 2))
    pl.when(i_ref[0] < 8)(lambda: build(0, 1))

    @pl.when(early(n_ref))
    def _():
        local_sweeps(i_ref, x_ref, m_ref, p_ref, h_ref, s_ref)
        copies = [
            pltpu.make_async_copy(src, dst, sem.at[n]) for n, (src, dst) in enumerate(((h_ref, h_hbm), (s_ref, s_hbm)))
        ]
        for copy in copies:
            copy.start()
        for copy in copies:
            copy.wait()


def planes_kernel(i_ref, x_ref, m_ref, p_ref, o_ref):
    def take(near, far):
        o_ref[0:288, :] = x_ref[pl.ds(near, 288, stride=4), :]
        o_ref[288:576, :] = x_ref[pl.ds(far, 288, stride=4), :]
        o_ref[576:596, :] = m_ref[pl.ds(near, 20, stride=4), :]
        o_ref[596:598, :] = p_ref[pl.ds(near, 2, stride=4), :].astype(F)
        o_ref[598:600, :] = jnp.zeros((2, 128), F)

    pl.when(i_ref[0] >= 8)(lambda: take(3, 2))
    pl.when(i_ref[0] < 8)(lambda: take(0, 1))


def late_kernel(i_ref, n_ref, x_ref, m_ref, p_ref, h_hbm, s_hbm, h_ref, s_ref, sem):
    @pl.when(early(n_ref))
    def _():
        copies = [
            pltpu.make_async_copy(src, dst, sem.at[n]) for n, (src, dst) in enumerate(((h_hbm, h_ref), (s_hbm, s_ref)))
        ]
        for copy in copies:
            copy.start()
        for copy in copies:
            copy.wait()

    pl.when(jnp.logical_not(early(n_ref)))(lambda: local_sweeps(i_ref, x_ref, m_ref, p_ref, h_ref, s_ref))


def early(n_ref):
    return lax.rem(n_ref[0], 16) < 4


def local_sweeps(i_ref, x_ref, m_ref, p_ref, h_ref, s_ref):
    a = first_speed(i_ref)
    aa = jnp.abs(a)
    sub, lane = iotas()
    pore = p_ref[...].astype(F)
    al = field_polynomial(a, [m_ref[8 * m : 8 * m + 8, :] for m in range(10)])
    zero = jnp.zeros(SHAPE, F)

    def sweeps(shift, edge):
        inner = jnp.where((sub & 3) == edge, 0.0, 1.0)

        def step(jj, sums):
            bm = 2.75 - 0.5 * jj.astype(F)
            ex = jnp.exp(-(a * a) - bm * bm)
            accs = [[zero] * 4, [zero] * 4]
            polys = [at_second(al, -bm), at_second(al, bm)]
            rows = [jj * 12, (11 - jj) * 12]
            for kk in range(6):
                cm = magnitude(kk)
                c2 = cm * cm
                pr = pore * (1.0 / (aa + (1.0 + cm + bm)))
                pg = pr * (ex * math.exp(-c2))
                px, py, pz = aa * pr * inner, bm * pr, cm * pr
                for side in range(2):
                    p0, p1, p2, p3 = polys[side]
                    even, odd = p0 + c2 * p2, cm * (p1 + c2 * p3)
                    out = []
                    for up in range(2):
                        v = rows[side] + (11 - kk if up else kk)
                        g = pg * (even + odd if up else even - odd)
                        h = x_ref[pl.ds(pl.multiple_of(8 * v, 8), 8), :]
                        for _ in range(2):
                            h = (
                                g
                                + px * pltpu.roll(h, shift, 0)
                                + py * from_y(h, lane, side == 1, swap_halves)
                                + pz * from_z(h, lane, up == 1)
                            )
                        h_ref[v] = h
                        out.append(h)
                    s, d = out[1] + out[0], cm * (out[1] - out[0])
                    p, q, r, t = accs[side]
                    accs[side] = [p + s, q + d, r + c2 * s, t + c2 * d]
            sums = add_raw(sums, -bm, accs[0])
            return add_raw(sums, bm, accs[1])

        sums = lax.fori_loop(0, 6, step, (zero,) * 7)
        for n in range(7):
            s_ref[n] = sums[n]

    pl.when(i_ref[0] >= 8)(lambda: sweeps(1, 0))
    pl.when(i_ref[0] < 8)(lambda: sweeps(7, 3))


def merge_kernel(i_ref, g_ref, p_ref, s_ref, o_ref, e_ref):
    a = first_speed(i_ref)
    sub, lane = iotas()
    even_row = (sub & 1) == 0
    forward = i_ref[0] >= 8

    def row(ref, r):
        return jnp.broadcast_to(ref[r : r + 1, :].astype(F), SHAPE)

    def own(plus, minus):
        return jnp.where(
            even_row,
            jnp.where(forward, row(p_ref, plus), row(p_ref, minus)),
            jnp.where(forward, row(p_ref, plus + 4), row(p_ref, minus + 4)),
        )

    pore_0, pore_1 = own(0, 3), own(1, 2)
    for n in range(2):
        whole, down, up, minus, plus, double = [g_ref[16 * k + 8 * n : 16 * k + 8 * n + 8, :] for k in range(6)]
        e_ref[8 * n : 8 * n + 8, :] = pore_0 * (
            whole
            + from_y(pore_0 * down, lane, False, swap_pairs)
            + from_y(pore_0 * up, lane, True, swap_pairs)
            + from_z(pore_0 * minus, lane, False)
            + from_z(pore_0 * plus, lane, True)
        )
        e_ref[16 + 8 * n : 24 + 8 * n, :] = pore_0 * pore_1 * double
    place = sub & 3
    at_near = place == jnp.where(forward, 0, 3)
    at_far = place == jnp.where(forward, 1, 2)

    def spread(r):
        return jnp.where(sub < 4, row(e_ref, r), row(e_ref, r + 1))

    s0, sb, sc, s2, sb2, sc2, sbc = [
        s_ref[n] + jnp.where(at_near, spread(r), jnp.where(at_far, spread(16 + r), 0.0))
        for n, r in enumerate((0, 4, 2, 8, 12, 10, 6))
    ]
    a2 = a * a
    t4, t5 = (a2 - 1.5) * s0 + s2, (a2 - 2.5) * s0 + s2
    moments = (s0, a * s0, sb, sc, t4, a * t5, (a2 - 2.5) * sb + sb2, (a2 - 2.5) * sc + sc2, a * sb, sbc)
    for m in range(10):
        value = moments[m] * VOL
        for n in range(o_ref.shape[0]):
            o_ref[n, 8 * m : 8 * m + 8, :] = value


def total_kernel(g_ref, o_ref):
    total = (g_ref[0] + g_ref[1]) + (g_ref[2] + g_ref[3])
    for n in range(o_ref.shape[0]):
        o_ref[n] = total


def change_kernel(g_ref, m_ref, p_ref, o_ref, h_ref):
    total = (g_ref[0] + g_ref[1]) + (g_ref[2] + g_ref[3])
    h_ref[...] = total
    o_ref[0:80, :] = total - m_ref[...]
    o_ref[80:88, :] = p_ref[...].astype(F)


def halo_kernel(wanted, i_ref, n_ref, *refs):
    pl.when(early(n_ref) if wanted else jnp.logical_not(early(n_ref)))(lambda: add_halo(i_ref, *refs))


def add_halo(i_ref, g_ref, p_ref, h_ref, o_ref):
    a = first_speed(i_ref)
    aa = jnp.abs(a)
    sub, lane = iotas()
    even_row = (sub & 1) == 0

    def row(ref, r):
        return jnp.broadcast_to(ref[r : r + 1, :].astype(F), SHAPE)

    def pair(ref, r, s):
        return jnp.where(even_row, row(ref, r), row(ref, s))

    cs = [-2.75 + 0.5 * (4 * t + (sub >> 1)).astype(F) for t in range(3)]
    ecs = [jnp.exp(-c * c) for c in cs]
    pore_out = pair(g_ref, 596, 597)
    al = field_polynomial(a, [pair(g_ref, 576 + 2 * m, 577 + 2 * m) for m in range(10)])
    o_ref[...] = h_ref[...]

    def back(h, t):
        if t == 0:
            return from_z(h, lane, False)
        if t == 2:
            return from_z(h, lane, True)
        return jnp.where(sub < 4, from_z(h, lane, False), from_z(h, lane, True))

    def fix(at_0, at_1):
        pore_0, pore_1 = pair(p_ref, at_0, at_0 + 4), pair(p_ref, at_1, at_1 + 4)

        def step(jj, carry):
            bm = 2.75 - 0.5 * jj.astype(F)
            ex = jnp.exp(-(a * a) - bm * bm)
            polys = [at_second(al, -bm), at_second(al, bm)]
            for t in range(3):
                c = cs[t]
                ca = jnp.abs(c)
                r = 1.0 / (aa + ca + (1.0 + bm))
                wa, wb, wc = aa * r, bm * r, ca * r
                rg = r * ex * ecs[t]
                for side in range(2):
                    p0, p1, p2, p3 = polys[side]
                    g = rg * (p0 + c * (p1 + c * (p2 + c * p3)))
                    base = pl.multiple_of(((11 - jj) if side else jj) * 24 + 8 * t, 8)
                    near, far = g_ref[pl.ds(base, 8), :], g_ref[pl.ds(288 + base, 8), :]
                    outer = pore_out * (
                        g + wa * far + wb * from_y(near, lane, side == 1, swap_pairs) + wc * back(near, t)
                    )
                    first = pore_0 * wa * near
                    e0 = pore_0 * (
                        wa * outer + wb * from_y(first, lane, side == 1, swap_pairs) + wc * back(first, t)
                    )
                    e1 = pore_1 * wa * first
                    rows_0 = pl.ds(base * 4 + at_0, 8, stride=4)
                    rows_1 = pl.ds(base * 4 + at_1, 8, stride=4)
                    o_ref[rows_0, :] = o_ref[rows_0, :] + e0
                    o_ref[rows_1, :] = o_ref[rows_1, :] + e1
            return carry

        lax.fori_loop(0, 6, step, 0)

    pl.when(i_ref[0] >= 8)(lambda: fix(0, 1))
    pl.when(i_ref[0] < 8)(lambda: fix(3, 2))


def final_kernel(i_ref, n_ref, q_ref, e_ref, l_ref, c_ref, left_ref, right_ref, mh_ref, o_hbm, mo_ref, k_ref, o_ref, sem):
    a = first_speed(i_ref)
    sub, lane = iotas()
    pores = [left_ref[10], c_ref[10], right_ref[10]]
    low, high = (sub & 3) == 0, (sub & 3) == 3
    wrap_up, wrap_down = lane < 16, lane >= 112
    z_first, z_last = (lane & 15) == 0, (lane & 15) == 15

    def around(h):
        up, down = pltpu.roll(h, 16, 1), pltpu.roll(h, 112, 1)
        same = jnp.where(wrap_up, 0.0, up) + jnp.where(wrap_down, 0.0, down)
        other = jnp.where(wrap_up, up, jnp.where(wrap_down, down, 0.0))
        forth = pltpu.roll(jnp.where(z_last, down, h), 1, 1)
        back = pltpu.roll(jnp.where(z_first, up, h), 127, 1)
        return same + swap_halves(other) + (forth + back)

    for m in range(10):
        inv = jnp.broadcast_to(q_ref[m : m + 1, :], SHAPE)
        q = [p * inv for p in pores]
        change = [left_ref[m], c_ref[m], right_ref[m]]
        cor = [q[n] * change[n] for n in range(3)]
        for it in range(4):
            new = list(cor)
            for n in range(3):
                if it == 3 and n != 1:
                    continue
                below = pltpu.roll(cor[n], 1, 0)
                above = pltpu.roll(cor[n], 7, 0)
                if n > 0:
                    below = jnp.where(low, pltpu.roll(cor[n - 1], 5, 0), below)
                if n < 2:
                    above = jnp.where(high, pltpu.roll(cor[n + 1], 3, 0), above)
                new[n] = q[n] * (change[n] + (below + above + around(cor[n])))
            cor = new
        k_ref[m] = cor[1]
        mo_ref[m] = mh_ref[m] + cor[1]

    al = field_polynomial(a, [k_ref[m] for m in range(10)])
    pore = pores[1]

    def chunk(n, j):
        rows = pl.ds(j * 12, 12)
        return pltpu.make_async_copy(o_ref.at[rows], o_hbm.at[rows], sem.at[n])

    def lift(h_ref):
        lax.fori_loop(0, 6, functools.partial(step, h_ref), 0)

    def step(h_ref, jj, carry):
        bm = 2.75 - 0.5 * jj.astype(F)
        ex = pore * jnp.exp(-(a * a) - bm * bm)
        for side in range(2):
            p0, p1, p2, p3 = at_second(al, bm if side else -bm)
            j = 11 - jj if side else jj
            for kk in range(6):
                cm = magnitude(kk)
                c2 = cm * cm
                w = ex * math.exp(-c2)
                even, odd = w * (p0 + c2 * p2), w * (cm * (p1 + c2 * p3))
                for up in range(2):
                    v = j * 12 + (11 - kk if up else kk)
                    o_ref[v] = h_ref[v] + (even + odd if up else even - odd)
            chunk(6 * side + jj, j).start()
        return carry

    pl.when(early(n_ref))(lambda: lift(e_ref))
    pl.when(jnp.logical_not(early(n_ref)))(lambda: lift(l_ref))
    for jj in range(6):
        chunk(jj, jj).wait()
        chunk(6 + jj, 11 - jj).wait()


VM = pl.BlockSpec(memory_space=pltpu.VMEM)
SM = pl.BlockSpec(memory_space=pltpu.SMEM)
HBM = pl.BlockSpec(memory_space=pltpu.HBM)


def call(kernel, outs, args, cost, scratch=(), ins=None, out_specs=None, grant=4 << 20):
    shapes = [jax.ShapeDtypeStruct(s, F) for s in outs]
    out_specs = out_specs or [VM] * len(shapes)
    single = len(shapes) == 1
    return pl.pallas_call(
        kernel,
        out_shape=shapes[0] if single else shapes,
        in_specs=ins,
        out_specs=out_specs[0] if single else out_specs,
        scratch_shapes=list(scratch),
        compiler_params=pltpu.CompilerParams(vmem_limit_bytes=grant),
        cost_estimate=pl.CostEstimate(flops=cost, bytes_accessed=4 * cost, transcendentals=0),
    )(*args)


def to_registers(x):
    n = x.shape[0]
    return x.reshape(n, 4, 2, 128).transpose(0, 2, 1, 3).reshape(n, 8, 128)


def from_registers(x):
    n = x.shape[0]
    return x.reshape(n, 2, 4, 128).transpose(0, 2, 1, 3).reshape(n, 4, 256)


def stage_groups(space, odd):
    found = {}
    for v in range(16):
        for s in range(space):
            far = s % 2 == odd
            key = (v // 8, v % 2) if far else (v % 8 // 2, 2)
            found.setdefault((key, s), []).append(v * space + s)
    return list(found.values())


def upwind_pairs(space):
    return [
        (v * space + s, v * space + (s + (1 if v >= 8 else -1)) % space) for v in range(16) for s in range(space)
    ]


def body(distribution, moments_old, pore_mask, synthetic_rate):
    space = lax.axis_size("space")
    i = lax.axis_index("vel").astype(jnp.int32).reshape(1)
    n = lax.axis_index("space").astype(jnp.int32).reshape(1)
    x = to_registers(distribution)
    old = to_registers(moments_old)
    pore = to_registers(pore_mask[None])[0]
    shapes = [(144, 8, 128), (7, 8, 128)]
    flat = [x.reshape(1152, 128), old.reshape(80, 128), pore]
    packed, half, sums = call(
        sums_kernel,
        [(96, 128)] + shapes,
        [i, n] + flat,
        1 << 20,
        [
            pltpu.VMEM((1152, 128), F),
            pltpu.VMEM((80, 128), F),
            pltpu.VMEM((8, 128), jnp.int32),
            pltpu.VMEM((144, 8, 128), F),
            pltpu.VMEM((7, 8, 128), F),
            pltpu.VMEM((90, 8, 128), F),
            pltpu.SemaphoreType.DMA((14,)),
        ],
        [SM, SM, HBM, HBM, HBM],
        [VM, HBM, HBM],
        grant=60 << 20,
    )
    pairs = upwind_pairs(space)
    sums_in = lax.ppermute(packed, ("vel", "space"), pairs)
    planes = call(planes_kernel, [(600, 128)], [i] + flat, 1 << 16, ins=[SM, VM, VM, VM])
    planes_in = lax.ppermute(planes, ("vel", "space"), pairs)
    half, sums = call(
        late_kernel,
        shapes,
        [i, n] + flat + [half, sums],
        1 << 21,
        [pltpu.SemaphoreType.DMA((2,))],
        [SM, SM, VM, VM, VM, HBM, HBM],
    )
    copies = call(
        merge_kernel,
        [(4, 80, 128)],
        [i, sums_in, pore, sums],
        1 << 16,
        [pltpu.VMEM((32, 128), F)],
        ins=[SM, VM, VM, VM],
    )
    got = lax.all_to_all(copies, ("vel", "space"), 0, 0, axis_index_groups=stage_groups(space, 0), tiled=True)
    copies = call(total_kernel, [(4, 80, 128)], [got], 1 << 16, ins=[VM])
    got = lax.all_to_all(copies, ("vel", "space"), 0, 0, axis_index_groups=stage_groups(space, 1), tiled=True)
    message, moments_half = call(
        change_kernel, [(88, 128), (80, 128)], [got, old.reshape(80, 128), pore], 1 << 16, ins=[VM] * 3
    )
    ring = [(s, (s + 1) % space) for s in range(space)]
    args = [i, n, planes_in, pore, half.reshape(1152, 128)]
    ins = [SM, SM, VM, VM, VM]
    left = lax.ppermute(message, "space", ring)
    whole_early = call(functools.partial(halo_kernel, True), [(1152, 128)], args, 1 << 16, ins=ins)
    right = lax.ppermute(message, "space", [(t, s) for s, t in ring])
    whole_late = call(functools.partial(halo_kernel, False), [(1152, 128)], args, 1 << 20, ins=ins)
    inverse = jnp.broadcast_to((1.0 / (synthetic_rate + 6.0))[:, None], (10, 128))
    out, moments_new = call(
        final_kernel,
        [(144, 8, 128), (10, 8, 128)],
        [
            i,
            n,
            inverse,
            whole_early.reshape(144, 8, 128),
            whole_late.reshape(144, 8, 128),
            message.reshape(11, 8, 128),
            left.reshape(11, 8, 128),
            right.reshape(11, 8, 128),
            moments_half.reshape(10, 8, 128),
        ],
        1 << 20,
        [pltpu.VMEM((10, 8, 128), F), pltpu.VMEM((144, 8, 128), F), pltpu.SemaphoreType.DMA((12,))],
        [SM, SM] + [VM] * 7,
        [HBM, VM],
    )
    return from_registers(out), from_registers(moments_new)


def solution(mesh):
    placed = (P("vel", "space", None), P(None, "space", None), P("space", None), P())
    return jax.shard_map(
        body,
        mesh=mesh,
        in_specs=placed,
        out_specs=(P("vel", "space", None), P(None, "space", None)),
        check_vma=False,
    )
```

```python
import functools
import math

import jax
import jax.numpy as jnp
from jax import lax
from jax.experimental import pallas as pl
from jax.experimental.pallas import tpu as pltpu
from jax.sharding import PartitionSpec as P


F = jnp.float32
SHAPE = (8, 128)
VOL = 216.0 / 2304 / math.pi**1.5
K1, K4, K5 = 2.0, 0.6667, 0.8


def magnitude(kk):
    return 2.75 - 0.5 * kk


def iotas():
    return lax.broadcasted_iota(jnp.int32, SHAPE, 0), lax.broadcasted_iota(jnp.int32, SHAPE, 1)


def first_speed(i_ref):
    return jnp.full(SHAPE, -3.0 + (i_ref[0].astype(F) + 0.5) * 0.375, F)


def field_polynomial(a, m):
    a2 = a * a
    u, w = a2 - 1.5, a2 - 2.5
    return (
        m[0] + K1 * (a * m[1]) + K4 * (u * m[4]) + K5 * (a * w * m[5]),
        K1 * m[2] + K5 * (w * m[6]) + K1 * (a * m[8]),
        K1 * m[3] + K5 * (w * m[7]),
        K4 * m[4] + K5 * (a * m[5]),
        K5 * m[6],
        K5 * m[7],
        K1 * m[9],
    )


def at_second(al, b):
    b2 = b * b
    return (
        al[0] + b * al[1] + b2 * al[3] + (b2 * b) * al[4],
        al[2] + b2 * al[5] + b * al[6],
        al[3] + b * al[4],
        al[5],
    )


def from_z(h, lane, positive):
    inside = lane & 15
    if positive:
        return jnp.where(inside == 0, pltpu.roll(h, 113, 1), pltpu.roll(h, 1, 1))
    return jnp.where(inside == 15, pltpu.roll(h, 15, 1), pltpu.roll(h, 127, 1))


def from_y(h, lane, positive, swap):
    r = pltpu.roll(h, 16 if positive else 112, 1)
    return jnp.where(lane < 16 if positive else lane >= 112, swap(r), r)


def swap_halves(r):
    return pltpu.roll(r, 4, 0)


def swap_pairs(r):
    even = (lax.broadcasted_iota(jnp.int32, SHAPE, 0) & 1) == 0
    return jnp.where(even, pltpu.roll(r, 7, 0), pltpu.roll(r, 1, 0))


def add_raw(sums, b, acc):
    s0, sb, sc, s2, sb2, sc2, sbc = sums
    p, q, r, t = acc
    b2 = b * b
    return (
        s0 + p,
        sb + b * p,
        sc + q,
        s2 + b2 * p + r,
        sb2 + b * (b2 * p + r),
        sc2 + b2 * q + t,
        sbc + b * q,
    )


def sums_kernel(i_ref, n_ref, x_hbm, m_hbm, p_hbm, g_ref, h_hbm, s_hbm, x_ref, m_ref, p_ref, h_ref, s_ref, w_ref, sem):
    def rows_of(j):
        rows = pl.ds(96 * j, 96)
        return pltpu.make_async_copy(x_hbm.at[rows], x_ref.at[rows], sem.at[2 + j])

    copies = [
        pltpu.make_async_copy(src, dst, sem.at[n]) for n, (src, dst) in enumerate(((m_hbm, m_ref), (p_hbm, p_ref)))
    ]
    for copy in copies:
        copy.start()
    for j in range(6):
        rows_of(j).start()
        rows_of(11 - j).start()
    a = first_speed(i_ref)
    aa = jnp.abs(a)
    sub, lane = iotas()
    even_row = (sub & 1) == 0
    zero = jnp.zeros(SHAPE, F)
    cs = [-2.75 + 0.5 * (4 * t + (sub >> 1)).astype(F) for t in range(3)]
    ecs = [jnp.exp(-c * c - a * a) for c in cs]
    top, first = sub < 4, (sub & 2) == 0
    for jj in range(6):
        bm = magnitude(jj)
        for t in range(3):
            ca = jnp.abs(cs[t])
            r = 1.0 / (aa + ca + (1.0 + bm))
            for n, x in enumerate((aa * r, bm * r, ca * r, (math.exp(-bm * bm) * ecs[t]) * r, aa * r * r)):
                w_ref[(3 * jj + t) * 5 + n] = x
    for copy in copies:
        copy.wait()

    def back(h, t):
        if t == 0:
            return from_z(h, lane, False)
        if t == 2:
            return from_z(h, lane, True)
        return jnp.where(sub < 4, from_z(h, lane, False), from_z(h, lane, True))

    def build(near, far):
        def pair(ref, r):
            return jnp.where(
                even_row,
                jnp.broadcast_to(ref[r : r + 1, :].astype(F), SHAPE),
                jnp.broadcast_to(ref[r + 4 : r + 5, :].astype(F), SHAPE),
            )

        pore = pair(p_ref, near)
        al = field_polynomial(a, [pair(m_ref, 8 * m + near) for m in range(10)])

        def packed(x):
            y = [
                jnp.where(top, x[n], x[n + 2]) + pltpu.roll(jnp.where(top, x[n + 2], x[n]), 4, 0) for n in range(2)
            ]
            return jnp.where(first, y[0], y[1]) + jnp.where(first, pltpu.roll(y[0], 6, 0), pltpu.roll(y[1], 2, 0))

        def step(jj, carry):
            below, above, minus, plus, whole = carry
            rows_of(jj).wait()
            rows_of(11 - jj).wait()
            bm = 2.75 - 0.5 * jj.astype(F)
            polys = [at_second(al, -bm), at_second(al, bm)]
            outs = [[zero] * 4, [zero] * 4]
            powers = [[], []]
            for t in range(3):
                c = cs[t]
                wa, wb, wc, rg, wr = [w_ref[(3 * jj + t) * 5 + n] for n in range(5)]
                for side in range(2):
                    p0, p1, p2, p3 = polys[side]
                    g = rg * (p0 + c * (p1 + c * (p2 + c * p3)))
                    base = pl.multiple_of(((11 - jj) if side else jj) * 24 + 8 * t, 8)
                    f1, f2 = x_ref[pl.ds(4 * base + near, 8, stride=4), :], x_ref[pl.ds(4 * base + far, 8, stride=4), :]
                    h = (wa * pore) * (
                        g + wa * f2 + wb * from_y(f1, lane, side == 1, swap_pairs) + wc * back(f1, t)
                    )
                    ks, hs = [wr * f1], [h]
                    for _ in range(4):
                        ks.append(c * ks[-1])
                    for _ in range(3):
                        hs.append(c * hs[-1])
                    powers[side].append(ks)
                    outs[side] = [p + q for p, q in zip(outs[side], hs)]
            b2 = bm * bm
            b3, b4 = b2 * bm, b2 * b2
            sides = [below, above]
            parts = []
            for side in range(2):
                low, mid, high = powers[side]
                total = packed([low[n] + mid[n] + high[n] for n in range(4)])
                parts.append(
                    (
                        packed([low[n] + jnp.where(sub < 4, mid[n], 0.0) for n in range(1, 5)]),
                        packed([high[n] + jnp.where(sub < 4, 0.0, mid[n]) for n in range(1, 5)]),
                        packed(outs[side]),
                    )
                )
                sides[side] = [x + y * total for x, y in zip(sides[side], (1.0, bm, b2, b3, b4))]

            def both(acc, n):
                even, odd = parts[1][n] + parts[0][n], parts[1][n] - parts[0][n]
                return [acc[0] + even, acc[1] + bm * odd, acc[2] + b2 * even, acc[3] + b3 * odd]

            return sides[0], sides[1], both(minus, 0), both(plus, 1), both(whole, 2)

        below, above, minus, plus, whole = lax.fori_loop(
            0, 6, step, ([zero] * 5, [zero] * 5, [zero] * 4, [zero] * 4, [zero] * 4)
        )
        signs = (1.0, -1.0, 1.0, -1.0)
        groups = (
            whole,
            [signs[n] * below[n + 1] for n in range(4)],
            above[1:],
            [-x for x in minus],
            plus,
            [aa * (above[n] + signs[n] * below[n]) for n in range(4)],
        )
        for n in range(6):
            t0, t1, t2, t3 = groups[n]
            g_ref[16 * n : 16 * n + 4, :] = t0[0:4, :]
            g_ref[16 * n + 4 : 16 * n + 8, :] = t1[0:4, :]
            g_ref[16 * n + 8 : 16 * n + 12, :] = (t2 + pltpu.roll(t0, 4, 0))[0:4, :]
            g_ref[16 * n + 12 : 16 * n + 14, :] = (t3 + pltpu.roll(t1, 4, 0))[0:2, :]
            g_ref[16 * n + 14 : 16 * n + 16, :] = jnp.zeros((2, 128), F)

    pl.when(i_ref[0] >= 8)(lambda: build(3, 2))
    pl.when(i_ref[0] < 8)(lambda: build(0, 1))

    @pl.when(early(n_ref))
    def _():
        local_sweeps(i_ref, x_ref, m_ref, p_ref, h_ref, s_ref)
        copies = [
            pltpu.make_async_copy(src, dst, sem.at[n]) for n, (src, dst) in enumerate(((h_ref, h_hbm), (s_ref, s_hbm)))
        ]
        for copy in copies:
            copy.start()
        for copy in copies:
            copy.wait()


def planes_kernel(i_ref, x_ref, m_ref, p_ref, o_ref):
    def take(near, far):
        o_ref[0:288, :] = x_ref[pl.ds(near, 288, stride=4), :]
        o_ref[288:576, :] = x_ref[pl.ds(far, 288, stride=4), :]
        o_ref[576:596, :] = m_ref[pl.ds(near, 20, stride=4), :]
        o_ref[596:598, :] = p_ref[pl.ds(near, 2, stride=4), :].astype(F)
        o_ref[598:600, :] = jnp.zeros((2, 128), F)

    pl.when(i_ref[0] >= 8)(lambda: take(3, 2))
    pl.when(i_ref[0] < 8)(lambda: take(0, 1))


def late_kernel(i_ref, n_ref, x_ref, m_ref, p_ref, h_hbm, s_hbm, h_ref, s_ref, sem):
    @pl.when(early(n_ref))
    def _():
        copies = [
            pltpu.make_async_copy(src, dst, sem.at[n]) for n, (src, dst) in enumerate(((h_hbm, h_ref), (s_hbm, s_ref)))
        ]
        for copy in copies:
            copy.start()
        for copy in copies:
            copy.wait()

    pl.when(jnp.logical_not(early(n_ref)))(lambda: local_sweeps(i_ref, x_ref, m_ref, p_ref, h_ref, s_ref))


def early(n_ref):
    return lax.rem(n_ref[0], 16) < 4


def local_sweeps(i_ref, x_ref, m_ref, p_ref, h_ref, s_ref):
    a = first_speed(i_ref)
    aa = jnp.abs(a)
    sub, lane = iotas()
    pore = p_ref[...].astype(F)
    al = field_polynomial(a, [m_ref[8 * m : 8 * m + 8, :] for m in range(10)])
    zero = jnp.zeros(SHAPE, F)

    def sweeps(shift, edge):
        inner = jnp.where((sub & 3) == edge, 0.0, 1.0)

        def step(jj, sums):
            bm = 2.75 - 0.5 * jj.astype(F)
            ex = jnp.exp(-(a * a) - bm * bm)
            accs = [[zero] * 4, [zero] * 4]
            polys = [at_second(al, -bm), at_second(al, bm)]
            rows = [jj * 12, (11 - jj) * 12]
            for kk in range(6):
                cm = magnitude(kk)
                c2 = cm * cm
                pr = pore * (1.0 / (aa + (1.0 + cm + bm)))
                pg = pr * (ex * math.exp(-c2))
                px, py, pz = aa * pr * inner, bm * pr, cm * pr
                for side in range(2):
                    p0, p1, p2, p3 = polys[side]
                    even, odd = p0 + c2 * p2, cm * (p1 + c2 * p3)
                    out = []
                    for up in range(2):
                        v = rows[side] + (11 - kk if up else kk)
                        g = pg * (even + odd if up else even - odd)
                        h = x_ref[pl.ds(pl.multiple_of(8 * v, 8), 8), :]
                        for _ in range(2):
                            h = (
                                g
                                + px * pltpu.roll(h, shift, 0)
                                + py * from_y(h, lane, side == 1, swap_halves)
                                + pz * from_z(h, lane, up == 1)
                            )
                        h_ref[v] = h
                        out.append(h)
                    s, d = out[1] + out[0], cm * (out[1] - out[0])
                    p, q, r, t = accs[side]
                    accs[side] = [p + s, q + d, r + c2 * s, t + c2 * d]
            sums = add_raw(sums, -bm, accs[0])
            return add_raw(sums, bm, accs[1])

        sums = lax.fori_loop(0, 6, step, (zero,) * 7)
        for n in range(7):
            s_ref[n] = sums[n]

    pl.when(i_ref[0] >= 8)(lambda: sweeps(1, 0))
    pl.when(i_ref[0] < 8)(lambda: sweeps(7, 3))


def merge_kernel(i_ref, g_ref, p_ref, s_ref, o_ref, e_ref):
    a = first_speed(i_ref)
    sub, lane = iotas()
    even_row = (sub & 1) == 0
    forward = i_ref[0] >= 8

    def row(ref, r):
        return jnp.broadcast_to(ref[r : r + 1, :].astype(F), SHAPE)

    def own(plus, minus):
        return jnp.where(
            even_row,
            jnp.where(forward, row(p_ref, plus), row(p_ref, minus)),
            jnp.where(forward, row(p_ref, plus + 4), row(p_ref, minus + 4)),
        )

    pore_0, pore_1 = own(0, 3), own(1, 2)
    for n in range(2):
        whole, down, up, minus, plus, double = [g_ref[16 * k + 8 * n : 16 * k + 8 * n + 8, :] for k in range(6)]
        e_ref[8 * n : 8 * n + 8, :] = pore_0 * (
            whole
            + from_y(pore_0 * down, lane, False, swap_pairs)
            + from_y(pore_0 * up, lane, True, swap_pairs)
            + from_z(pore_0 * minus, lane, False)
            + from_z(pore_0 * plus, lane, True)
        )
        e_ref[16 + 8 * n : 24 + 8 * n, :] = pore_0 * pore_1 * double
    place = sub & 3
    at_near = place == jnp.where(forward, 0, 3)
    at_far = place == jnp.where(forward, 1, 2)

    def spread(r):
        return jnp.where(sub < 4, row(e_ref, r), row(e_ref, r + 1))

    s0, sb, sc, s2, sb2, sc2, sbc = [
        s_ref[n] + jnp.where(at_near, spread(r), jnp.where(at_far, spread(16 + r), 0.0))
        for n, r in enumerate((0, 4, 2, 8, 12, 10, 6))
    ]
    a2 = a * a
    t4, t5 = (a2 - 1.5) * s0 + s2, (a2 - 2.5) * s0 + s2
    moments = (s0, a * s0, sb, sc, t4, a * t5, (a2 - 2.5) * sb + sb2, (a2 - 2.5) * sc + sc2, a * sb, sbc)
    for m in range(10):
        value = moments[m] * VOL
        for n in range(o_ref.shape[0]):
            o_ref[n, 8 * m : 8 * m + 8, :] = value


def total_kernel(g_ref, o_ref):
    total = (g_ref[0] + g_ref[1]) + (g_ref[2] + g_ref[3])
    for n in range(o_ref.shape[0]):
        o_ref[n] = total


def change_kernel(g_ref, m_ref, p_ref, o_ref, h_ref):
    total = (g_ref[0] + g_ref[1]) + (g_ref[2] + g_ref[3])
    h_ref[...] = total
    o_ref[0:80, :] = total - m_ref[...]
    o_ref[80:88, :] = p_ref[...].astype(F)


def halo_kernel(wanted, i_ref, n_ref, *refs):
    pl.when(early(n_ref) if wanted else jnp.logical_not(early(n_ref)))(lambda: add_halo(i_ref, *refs))


def add_halo(i_ref, g_ref, p_ref, h_ref, o_ref):
    a = first_speed(i_ref)
    aa = jnp.abs(a)
    sub, lane = iotas()
    even_row = (sub & 1) == 0

    def row(ref, r):
        return jnp.broadcast_to(ref[r : r + 1, :].astype(F), SHAPE)

    def pair(ref, r, s):
        return jnp.where(even_row, row(ref, r), row(ref, s))

    cs = [-2.75 + 0.5 * (4 * t + (sub >> 1)).astype(F) for t in range(3)]
    ecs = [jnp.exp(-c * c) for c in cs]
    pore_out = pair(g_ref, 596, 597)
    al = field_polynomial(a, [pair(g_ref, 576 + 2 * m, 577 + 2 * m) for m in range(10)])
    o_ref[...] = h_ref[...]

    def back(h, t):
        if t == 0:
            return from_z(h, lane, False)
        if t == 2:
            return from_z(h, lane, True)
        return jnp.where(sub < 4, from_z(h, lane, False), from_z(h, lane, True))

    def fix(at_0, at_1):
        pore_0, pore_1 = pair(p_ref, at_0, at_0 + 4), pair(p_ref, at_1, at_1 + 4)

        def step(jj, carry):
            bm = 2.75 - 0.5 * jj.astype(F)
            ex = jnp.exp(-(a * a) - bm * bm)
            polys = [at_second(al, -bm), at_second(al, bm)]
            for t in range(3):
                c = cs[t]
                ca = jnp.abs(c)
                r = 1.0 / (aa + ca + (1.0 + bm))
                wa, wb, wc = aa * r, bm * r, ca * r
                rg = r * ex * ecs[t]
                for side in range(2):
                    p0, p1, p2, p3 = polys[side]
                    g = rg * (p0 + c * (p1 + c * (p2 + c * p3)))
                    base = pl.multiple_of(((11 - jj) if side else jj) * 24 + 8 * t, 8)
                    near, far = g_ref[pl.ds(base, 8), :], g_ref[pl.ds(288 + base, 8), :]
                    outer = pore_out * (
                        g + wa * far + wb * from_y(near, lane, side == 1, swap_pairs) + wc * back(near, t)
                    )
                    first = pore_0 * wa * near
                    e0 = pore_0 * (
                        wa * outer + wb * from_y(first, lane, side == 1, swap_pairs) + wc * back(first, t)
                    )
                    e1 = pore_1 * wa * first
                    rows_0 = pl.ds(base * 4 + at_0, 8, stride=4)
                    rows_1 = pl.ds(base * 4 + at_1, 8, stride=4)
                    o_ref[rows_0, :] = o_ref[rows_0, :] + e0
                    o_ref[rows_1, :] = o_ref[rows_1, :] + e1
            return carry

        lax.fori_loop(0, 6, step, 0)

    pl.when(i_ref[0] >= 8)(lambda: fix(0, 1))
    pl.when(i_ref[0] < 8)(lambda: fix(3, 2))


def final_kernel(i_ref, n_ref, q_ref, e_ref, l_ref, c_ref, left_ref, right_ref, mh_ref, o_hbm, mo_hbm, k_ref, mo_ref, o_ref, sem):
    a = first_speed(i_ref)
    sub, lane = iotas()
    pores = [left_ref[10], c_ref[10], right_ref[10]]
    low, high = (sub & 3) == 0, (sub & 3) == 3
    wrap_up, wrap_down = lane < 16, lane >= 112
    z_first, z_last = (lane & 15) == 0, (lane & 15) == 15

    def around(h):
        up, down = pltpu.roll(h, 16, 1), pltpu.roll(h, 112, 1)
        same = jnp.where(wrap_up, 0.0, up) + jnp.where(wrap_down, 0.0, down)
        other = jnp.where(wrap_up, up, jnp.where(wrap_down, down, 0.0))
        forth = pltpu.roll(jnp.where(z_last, down, h), 1, 1)
        back = pltpu.roll(jnp.where(z_first, up, h), 127, 1)
        return same + swap_halves(other) + (forth + back)

    for m in range(10):
        inv = jnp.broadcast_to(q_ref[m : m + 1, :], SHAPE)
        q = [p * inv for p in pores]
        change = [left_ref[m], c_ref[m], right_ref[m]]
        cor = [q[n] * change[n] for n in range(3)]
        for it in range(4):
            new = list(cor)
            for n in range(3):
                if it == 3 and n != 1:
                    continue
                below = pltpu.roll(cor[n], 1, 0)
                above = pltpu.roll(cor[n], 7, 0)
                if n > 0:
                    below = jnp.where(low, pltpu.roll(cor[n - 1], 5, 0), below)
                if n < 2:
                    above = jnp.where(high, pltpu.roll(cor[n + 1], 3, 0), above)
                new[n] = q[n] * (change[n] + (below + above + around(cor[n])))
            cor = new
        k_ref[m] = cor[1]
        mo_ref[m] = mh_ref[m] + cor[1]

    moments_out = pltpu.make_async_copy(mo_ref, mo_hbm, sem.at[12])
    moments_out.start()
    al = field_polynomial(a, [k_ref[m] for m in range(10)])
    pore = pores[1]

    def chunk(n, j):
        rows = pl.ds(j * 12, 12)
        return pltpu.make_async_copy(o_ref.at[rows], o_hbm.at[rows], sem.at[n])

    def lift(h_ref):
        lax.fori_loop(0, 6, functools.partial(step, h_ref), 0)

    def step(h_ref, jj, carry):
        bm = 2.75 - 0.5 * jj.astype(F)
        ex = pore * jnp.exp(-(a * a) - bm * bm)
        for side in range(2):
            p0, p1, p2, p3 = at_second(al, bm if side else -bm)
            j = 11 - jj if side else jj
            for kk in range(6):
                cm = magnitude(kk)
                c2 = cm * cm
                w = ex * math.exp(-c2)
                even, odd = w * (p0 + c2 * p2), w * (cm * (p1 + c2 * p3))
                for up in range(2):
                    v = j * 12 + (11 - kk if up else kk)
                    o_ref[v] = h_ref[v] + (even + odd if up else even - odd)
            chunk(6 * side + jj, j).start()
        return carry

    pl.when(early(n_ref))(lambda: lift(e_ref))
    pl.when(jnp.logical_not(early(n_ref)))(lambda: lift(l_ref))
    for jj in range(6):
        chunk(jj, jj).wait()
        chunk(6 + jj, 11 - jj).wait()
    moments_out.wait()


VM = pl.BlockSpec(memory_space=pltpu.VMEM)
SM = pl.BlockSpec(memory_space=pltpu.SMEM)
HBM = pl.BlockSpec(memory_space=pltpu.HBM)


def call(kernel, outs, args, cost, scratch=(), ins=None, out_specs=None, grant=4 << 20):
    shapes = [jax.ShapeDtypeStruct(s, F) for s in outs]
    out_specs = out_specs or [VM] * len(shapes)
    single = len(shapes) == 1
    return pl.pallas_call(
        kernel,
        out_shape=shapes[0] if single else shapes,
        in_specs=ins,
        out_specs=out_specs[0] if single else out_specs,
        scratch_shapes=list(scratch),
        compiler_params=pltpu.CompilerParams(vmem_limit_bytes=grant),
        cost_estimate=pl.CostEstimate(flops=cost, bytes_accessed=4 * cost, transcendentals=0),
    )(*args)


def to_registers(x):
    n = x.shape[0]
    return x.reshape(n, 4, 2, 128).transpose(0, 2, 1, 3).reshape(n, 8, 128)


def from_registers(x):
    n = x.shape[0]
    return x.reshape(n, 2, 4, 128).transpose(0, 2, 1, 3).reshape(n, 4, 256)


def stage_groups(space, odd):
    found = {}
    for v in range(16):
        for s in range(space):
            far = s % 2 == odd
            key = (v // 8, v % 2) if far else (v % 8 // 2, 2)
            found.setdefault((key, s), []).append(v * space + s)
    return list(found.values())


def upwind_pairs(space):
    return [
        (v * space + s, v * space + (s + (1 if v >= 8 else -1)) % space) for v in range(16) for s in range(space)
    ]


def body(distribution, moments_old, pore_mask, synthetic_rate):
    space = lax.axis_size("space")
    i = lax.axis_index("vel").astype(jnp.int32).reshape(1)
    n = lax.axis_index("space").astype(jnp.int32).reshape(1)
    x = to_registers(distribution)
    old = to_registers(moments_old)
    pore = to_registers(pore_mask[None])[0]
    shapes = [(144, 8, 128), (7, 8, 128)]
    flat = [x.reshape(1152, 128), old.reshape(80, 128), pore]
    packed, half, sums = call(
        sums_kernel,
        [(96, 128)] + shapes,
        [i, n] + flat,
        1 << 20,
        [
            pltpu.VMEM((1152, 128), F),
            pltpu.VMEM((80, 128), F),
            pltpu.VMEM((8, 128), jnp.int32),
            pltpu.VMEM((144, 8, 128), F),
            pltpu.VMEM((7, 8, 128), F),
            pltpu.VMEM((90, 8, 128), F),
            pltpu.SemaphoreType.DMA((14,)),
        ],
        [SM, SM, HBM, HBM, HBM],
        [VM, HBM, HBM],
        grant=60 << 20,
    )
    pairs = upwind_pairs(space)
    sums_in = lax.ppermute(packed, ("vel", "space"), pairs)
    planes = call(planes_kernel, [(600, 128)], [i] + flat, 1 << 16, ins=[SM, VM, VM, VM])
    planes_in = lax.ppermute(planes, ("vel", "space"), pairs)
    half, sums = call(
        late_kernel,
        shapes,
        [i, n] + flat + [half, sums],
        1 << 21,
        [pltpu.SemaphoreType.DMA((2,))],
        [SM, SM, VM, VM, VM, HBM, HBM],
    )
    copies = call(
        merge_kernel,
        [(4, 80, 128)],
        [i, sums_in, pore, sums],
        1 << 16,
        [pltpu.VMEM((32, 128), F)],
        ins=[SM, VM, VM, VM],
    )
    got = lax.all_to_all(copies, ("vel", "space"), 0, 0, axis_index_groups=stage_groups(space, 0), tiled=True)
    copies = call(total_kernel, [(4, 80, 128)], [got], 1 << 16, ins=[VM])
    got = lax.all_to_all(copies, ("vel", "space"), 0, 0, axis_index_groups=stage_groups(space, 1), tiled=True)
    message, moments_half = call(
        change_kernel, [(88, 128), (80, 128)], [got, old.reshape(80, 128), pore], 1 << 16, ins=[VM] * 3
    )
    ring = [(s, (s + 1) % space) for s in range(space)]
    args = [i, n, planes_in, pore, half.reshape(1152, 128)]
    ins = [SM, SM, VM, VM, VM]
    left = lax.ppermute(message, "space", ring)
    whole_early = call(functools.partial(halo_kernel, True), [(1152, 128)], args, 1 << 16, ins=ins)
    right = lax.ppermute(message, "space", [(t, s) for s, t in ring])
    whole_late = call(functools.partial(halo_kernel, False), [(1152, 128)], args, 1 << 20, ins=ins)
    inverse = jnp.broadcast_to((1.0 / (synthetic_rate + 6.0))[:, None], (10, 128))
    out, moments_new = call(
        final_kernel,
        [(144, 8, 128), (10, 8, 128)],
        [
            i,
            n,
            inverse,
            whole_early.reshape(144, 8, 128),
            whole_late.reshape(144, 8, 128),
            message.reshape(11, 8, 128),
            left.reshape(11, 8, 128),
            right.reshape(11, 8, 128),
            moments_half.reshape(10, 8, 128),
        ],
        1 << 20,
        [
            pltpu.VMEM((10, 8, 128), F),
            pltpu.VMEM((10, 8, 128), F),
            pltpu.VMEM((144, 8, 128), F),
            pltpu.SemaphoreType.DMA((13,)),
        ],
        [SM, SM] + [VM] * 7,
        [HBM, HBM],
    )
    return from_registers(out), from_registers(moments_new)


def solution(mesh):
    placed = (P("vel", "space", None), P(None, "space", None), P("space", None), P())
    return jax.shard_map(
        body,
        mesh=mesh,
        in_specs=placed,
        out_specs=(P("vel", "space", None), P(None, "space", None)),
        check_vma=False,
    )
```
